32 devices in a mesh: seq: 4 (over z), tok: 8 (over y, x, core).
Axes of the slice: x: 2, y: 2, z: 4, core: 2. Of those that a mesh axis runs over, the one named last changes fastest.
Arguments:
- tokens: bfloat16 [4, 1024, 1024], P('seq', 'tok'), may hold values from -6 to 6
- cotangent: bfloat16 [4, 1024, 1024], P('seq', 'tok'), may hold values from -6 to 6
- owners: int32 [5409], replicated, may hold values from 0 to 31, as said below
- master: float32 [8160, 2048], P(('seq', 'tok')), may hold values from -4 to 4
- first_moment: float32 [8160, 2048], P(('seq', 'tok')), may hold values from -28.8 to 28.8
- second_moment: float32 [8160, 2048], P(('seq', 'tok')), may hold values from 0 to 901.12, as said below
Outputs:
- result: bfloat16 [4, 1024, 1024], P('seq', 'tok')
- grad_input: bfloat16 [4, 1024, 1024], P('seq', 'tok')
- reduced_grad: float32 [8160, 2048], P(('seq', 'tok'))
- new_first: float32 [8160, 2048], P(('seq', 'tok'))
- new_second: float32 [8160, 2048], P(('seq', 'tok'))
- new_master: float32 [8160, 2048], P(('seq', 'tok'))
The draws below stay inside these ranges and needn't reach their ends.
Inputs may be any that keep to these rules, and one draw needn't show every extreme that they name: owners[b] is the device, indexed over seq then tok, that owns weight block b; no device owns more than 255 blocks and some device owns exactly 255. Entries of second_moment are positive.
All inputs are finite; a program needn't handle non-finite values.
Results may differ from the reference program's by a relative error of at most 0.012.
Values may be sent and summed in bfloat16 or wider, within the bound.
No kernel may reach another device: no remote copies, remote signals or barrier semaphores. Data moves between devices by JAX's collectives and lax.ppermute only.
A program may use at most 576 MiB of HBM per device.

```python
import math
import jax
import jax.numpy as jnp
from jax import lax

D = 1024
HEADS = 16
FD = 16
DV = 64
FF = 2752
STEP = 10
SEQS = 4
SEQLEN = 1024
TF = 273
BLK = 2048
NBLK = 5409
CAP = 255
SLOTS = 8160


def kind_limits_drawn():
    counts = [1, D * HEADS * FD // BLK, D * HEADS * FD // BLK, D * HEADS * DV // BLK, HEADS * DV * D // BLK, D * FF // BLK, D * FF // BLK, FF * D // BLK]
    limits = []
    running = 0
    for amount in counts:
        running = running + amount
        limits.append(running)
    return limits


def block_kinds_drawn(block_ids):
    limits = jnp.array(kind_limits_drawn(), jnp.int32)
    return jnp.sum((block_ids[:, None] >= limits[None, :]).astype(jnp.int32), axis=1)


def slot_table_drawn(owners, devices, capacity):
    count = owners.shape[0]
    order = jnp.argsort(owners, stable=True).astype(jnp.int32)
    sorted_owner = owners[order]
    match = (owners[:, None] == jnp.arange(devices, dtype=jnp.int32)[None, :]).astype(jnp.int32)
    counts = jnp.sum(match, axis=0)
    starts = jnp.cumsum(counts) - counts
    ranked = jnp.arange(count, dtype=jnp.int32) - starts[sorted_owner]
    placed = (sorted_owner * capacity + ranked).astype(jnp.int32)
    table = jnp.full((devices * capacity,), count, jnp.int32).at[placed].set(order)
    return table


def slot_owners(key):
    key = jax.random.fold_in(key, 11)
    key_heavy, key_slots, key_blocks = jax.random.split(key, 3)
    devices = SLOTS // CAP
    heavy = jax.random.randint(key_heavy, (), 0, devices)
    shuffled = jax.random.permutation(key_slots, SLOTS).astype(jnp.int32)
    slot_device = jnp.arange(SLOTS, dtype=jnp.int32) // CAP
    priority = jnp.where(slot_device == heavy, 0, SLOTS) + shuffled
    chosen = jnp.argsort(priority, stable=True)[:NBLK].astype(jnp.int32)
    placing = jax.random.permutation(key_blocks, NBLK)
    return jnp.zeros((NBLK,), jnp.int32).at[placing].set(chosen // CAP)


def slot_kinds(key):
    owners = slot_owners(key)
    return block_kinds_drawn(slot_table_drawn(owners, SLOTS // CAP, CAP))


def unit_noise(key, salt):
    noise_key = jax.random.fold_in(key, salt)
    return jnp.clip(jax.random.normal(noise_key, (SLOTS, BLK), jnp.float32), -4.0, 4.0)


def out_std():
    return 1.0 / math.sqrt(max(1, D * 16 // SEQLEN))


def grad_scales():
    base = math.sqrt(SEQS * SEQLEN)
    y_rms = math.sqrt(math.log(SEQLEN) / SEQLEN)
    value_factor = out_std() * math.sqrt(D) * y_rms
    factors = [1.0, 0.3, 0.3, value_factor, y_rms, 0.5, 0.5, 0.6, 1.0]
    return jnp.array([base * factor for factor in factors], jnp.float32)


def weight_scales():
    inverse_width = 1.0 / math.sqrt(D)
    return jnp.array([0.1, inverse_width, inverse_width, inverse_width, out_std(), inverse_width, inverse_width, 1.0 / math.sqrt(FF), inverse_width], jnp.float32)


def draw_owners(key, part):
    return slot_owners(key)


def draw_master(key, part):
    kinds = slot_kinds(key)
    scales = jnp.take(weight_scales(), kinds)
    offsets = jnp.where(kinds == 0, 1.0, 0.0)
    return offsets[:, None] + scales[:, None] * unit_noise(key, 23)


def draw_first_moment(key, part):
    kinds = slot_kinds(key)
    scales = jnp.take(grad_scales(), kinds) * (0.1 / 0.9)
    return scales[:, None] * unit_noise(key, 29)


def draw_second_moment(key, part):
    kinds = slot_kinds(key)
    scales = jnp.take(grad_scales(), kinds)
    factor_key = jax.random.fold_in(key, 31)
    factors = jnp.exp(jax.random.uniform(factor_key, (SLOTS, BLK), jnp.float32, 0.0, math.log(4.0)))
    return 0.05 / 0.95 * (scales * scales)[:, None] * factors


def level_of(rng, dims, cuts, smallest, high):
    def one(dim, shards_of):
        steps = jax.random.uniform(jax.random.fold_in(jax.random.fold_in(rng, 6), dim), (shards_of,), jnp.float32, smallest / len(cuts), high / len(cuts))
        return jnp.repeat(jnp.exp(steps), dims[dim] // shards_of).reshape((-1,) + (1,) * (len(dims) - dim - 1))

    factor_of = one(*cuts[0])
    for cut in cuts[1:]:
        factor_of = factor_of * one(*cut)
    return factor_of


def centred(stream_key, dims, spread, bound, shards=(), kind=jnp.bfloat16):
    factor_of = level_of(stream_key, dims, shards, -0.22, 0.18) if shards else 1.0
    values = jax.random.normal(stream_key, dims, jnp.float32) * spread * factor_of
    return jnp.minimum(jnp.maximum(values, -bound), bound).astype(kind)


def setup_inputs(seed: int = 0) -> dict:
    splits = jax.random.split(jax.random.key(seed), 7)
    tokens = centred(splits[0], (SEQS, SEQLEN, D), 1.0, 6.0, ((0, 4), (1, 8)))
    cotangent = centred(splits[1], (SEQS, SEQLEN, D), 1.0, 6.0, ((0, 4), (1, 8)))
    owners = draw_owners(jax.random.fold_in(splits[6], 71), 0)
    master = draw_master(jax.random.fold_in(splits[6], 71), 0)
    first_moment = draw_first_moment(jax.random.fold_in(splits[6], 71), 0)
    second_moment = draw_second_moment(jax.random.fold_in(splits[6], 71), 0)
    return dict(tokens=tokens, cotangent=cotangent, owners=owners, master=master, first_moment=first_moment, second_moment=second_moment)


PRECISE = lax.Precision.HIGHEST
NORM_EPSILON = 1e-05
ADAM_EPSILON = 1e-08
BETA_ONE = 0.9
BETA_TWO = 0.95
DECAY_RATE = 0.1

@jax.custom_vjp
def low(v):
    return lax.optimization_barrier(v.astype(jnp.bfloat16)).astype(jnp.float32)

@jax.custom_vjp
def low_back(v):
    return v

def low_keep(v):
    return (low(v), None)

def low_pass(kept, grad):
    return (grad,)

def back_keep(v):
    return (v, None)

def back_low(kept, grad):
    return (low(grad),)
low.defvjp(low_keep, low_pass)
low_back.defvjp(back_keep, back_low)

def product(left, right):
    return jnp.dot(left, right, precision=PRECISE, preferred_element_type=jnp.float32)

def normed(values):
    return values * lax.rsqrt(lax.optimization_barrier(jnp.mean(values * values, axis=-1, keepdims=True)) + NORM_EPSILON)

def features(values):
    feature_dim = values.shape[-1]
    outer_part = (values[..., :, None] * values[..., None, :]).reshape(values.shape[:-1] + (feature_dim * feature_dim,))
    constant = jnp.ones(values.shape[:-1] + (1,), values.dtype)
    return jnp.concatenate([constant, values / feature_dim ** 0.25, outer_part / math.sqrt(2.0 * feature_dim)], axis=-1)

def block_step(carried, block_items):
    prefix_state, prefix_total = carried
    query, keys, values = block_items
    block_size = query.shape[0]
    inner_dot = jnp.einsum('ihf,jhf->hij', query, keys, precision=PRECISE) / math.sqrt(FD)
    causal = jnp.arange(block_size)[:, None] >= jnp.arange(block_size)[None, :]
    weight = jnp.where(causal[None], 1.0 + inner_dot + 0.5 * inner_dot * inner_dot, 0.0)
    phi_query = features(query)
    phi_keys = features(keys)
    numerator = jnp.einsum('hij,jhw->ihw', weight, values, precision=PRECISE) + jnp.einsum('iht,htw->ihw', phi_query, prefix_state, precision=PRECISE)
    denominator = lax.optimization_barrier(jnp.sum(weight, axis=2)).T + jnp.einsum('iht,ht->ih', phi_query, prefix_total, precision=PRECISE)
    mixed_out = numerator / denominator[..., None]
    next_state = prefix_state + jnp.einsum('jht,jhw->htw', phi_keys, values, precision=PRECISE)
    next_total = prefix_total + lax.optimization_barrier(jnp.sum(phi_keys, axis=0))
    return ((next_state, next_total), mixed_out)

def attention(query, keys, values):
    length = query.shape[0]
    block_size = min(512, length)
    block_count = length // block_size
    query_blocks = query.reshape(block_count, block_size, HEADS, FD)
    keys_blocks = keys.reshape(block_count, block_size, HEADS, FD)
    value_blocks = values.reshape(block_count, block_size, HEADS, DV)
    start_pair = (jnp.zeros((HEADS, TF, DV), query.dtype), jnp.zeros((HEADS, TF), query.dtype))
    final_pair, mixed_out = lax.scan(jax.checkpoint(block_step), start_pair, (query_blocks, keys_blocks, value_blocks))
    return mixed_out.reshape(length, HEADS * DV)

def layer(weights, inputs):
    gains, w_query, w_keys, w_values, w_out, w_gate, w_up, w_down = weights
    hidden_one = low(normed(inputs) * gains[0])
    query = low(low_back(product(hidden_one, w_query)))
    keys = low(low_back(product(hidden_one, w_keys)))
    values = low(low_back(product(hidden_one, w_values)))
    mixed = low(low_back(attention(query, keys, values)))
    middle = inputs + low_back(product(mixed, w_out))
    hidden_two = low(normed(middle) * gains[1])
    gate = low_back(product(hidden_two, w_gate))
    up_proj = low_back(product(hidden_two, w_up))
    hidden = low(jax.nn.silu(gate) * up_proj)
    return middle + product(hidden, w_down)

def slot_table(owners, devices, capacity):
    count = owners.shape[0]
    order = jnp.argsort(owners, stable=True).astype(jnp.int32)
    sorted_owner = owners[order]
    match = (owners[:, None] == jnp.arange(devices, dtype=jnp.int32)[None, :]).astype(jnp.int32)
    counts = lax.optimization_barrier(jnp.sum(match, axis=0))
    starts = jnp.cumsum(counts) - counts
    ranked = jnp.arange(count, dtype=jnp.int32) - starts[sorted_owner]
    placed = (sorted_owner * capacity + ranked).astype(jnp.int32)
    table = jnp.full((devices * capacity,), count, jnp.int32).at[placed].set(order)
    position = jnp.zeros((count,), jnp.int32).at[order].set(placed)
    return (table, position)

def kind_limits():
    counts = [1, D * HEADS * FD // BLK, D * HEADS * FD // BLK, D * HEADS * DV // BLK, HEADS * DV * D // BLK, D * FF // BLK, D * FF // BLK, FF * D // BLK]
    limits = []
    running = 0
    for amount in counts:
        running = running + amount
        limits.append(running)
    return limits

def block_kinds(block_ids):
    limits = jnp.array(kind_limits(), jnp.int32)
    return lax.optimization_barrier(jnp.sum((block_ids[:, None] >= limits[None, :]).astype(jnp.int32), axis=1))

def rates_for(kinds, seq_len):
    out_std = 1.0 / math.sqrt(max(1, D * 16 // seq_len))
    matrix_rate = 3.0 / math.sqrt(D)
    rate_list = [1.0, matrix_rate, matrix_rate, matrix_rate, 3.0 * out_std, matrix_rate, matrix_rate, 3.0 / math.sqrt(FF), 0.0]
    decay_list = [0.0] + [DECAY_RATE] * 7 + [0.0]
    chosen = (kinds[:, None] == jnp.arange(9, dtype=jnp.int32)[None, :]).astype(jnp.float32)
    rate_values = lax.optimization_barrier(jnp.sum(chosen * jnp.array(rate_list, jnp.float32)[None, :], axis=1))
    decay_values = lax.optimization_barrier(jnp.sum(chosen * jnp.array(decay_list, jnp.float32)[None, :], axis=1))
    return (rate_values, decay_values)

def adam_update(grads, moment_one, moment_two, weights, rate_values, decay_values):
    first = BETA_ONE * moment_one + (1.0 - BETA_ONE) * grads
    second = BETA_TWO * moment_two + (1.0 - BETA_TWO) * grads * grads
    first_hat = first / (1.0 - BETA_ONE ** STEP)
    second_hat = second / (1.0 - BETA_TWO ** STEP)
    updated = weights - rate_values[:, None] * (first_hat / (jnp.sqrt(second_hat) + ADAM_EPSILON) + decay_values[:, None] * weights)
    return (first, second, updated)

def unpack(flat):
    matrix_shapes = [(2, D), (D, HEADS * FD), (D, HEADS * FD), (D, HEADS * DV), (HEADS * DV, D), (D, FF), (D, FF), (FF, D)]
    pieces = []
    offset = 0
    for matrix_shape in matrix_shapes:
        length = matrix_shape[0] * matrix_shape[1]
        pieces.append(flat[offset:offset + length].reshape(matrix_shape))
        offset = offset + length
    return tuple(pieces)

def reference(tokens, cotangent, owners, master, first_moment, second_moment):
    table, position = slot_table(owners, SLOTS // CAP, CAP)
    blocks = low(jnp.take(master, position, axis=0))
    weights = unpack(blocks.reshape(-1))

    def per_sequence(running, pair):
        seq_tokens, seq_grad = pair
        result, pullback = jax.vjp(layer, weights, seq_tokens.astype(jnp.float32))
        grad_weights, grad_inputs = pullback(seq_grad.astype(jnp.float32))
        running = jax.tree.map(lambda first, second: first + second, running, grad_weights)
        return (running, (result.astype(jnp.bfloat16), grad_inputs.astype(jnp.bfloat16)))
    zero_grads = jax.tree.map(jnp.zeros_like, weights)
    total_grads, (results, grad_inputs) = lax.scan(per_sequence, zero_grads, (tokens, cotangent))
    grad_flat = jnp.concatenate([piece.reshape(-1) for piece in total_grads]).reshape(NBLK, BLK)
    reduced = jnp.take(grad_flat, table, axis=0, mode='fill', fill_value=0.0)
    rate_values, decay_values = rates_for(block_kinds(table), SEQLEN)
    first, second, updated = adam_update(reduced, first_moment, second_moment, master, rate_values, decay_values)
    return (results, grad_inputs, reduced, first, second, updated)
```

```python
import math

import jax
import jax.numpy as jnp
from jax import lax
from jax.sharding import PartitionSpec as P

D = 1024
HEADS = 16
FD = 16
DV = 64
FF = 2752
STEP = 10
BLK = 2048

NORM_EPSILON = 1e-05
ADAM_EPSILON = 1e-08
BETA_ONE = 0.9
BETA_TWO = 0.95
DECAY_RATE = 0.1
BF = jnp.bfloat16
F32 = jnp.float32


MATRIX_BLOCKS = [
    D * HEADS * FD // BLK,
    D * HEADS * FD // BLK,
    D * HEADS * DV // BLK,
    HEADS * DV * D // BLK,
    D * FF // BLK,
    D * FF // BLK,
    FF * D // BLK,
]
MATRIX_STARTS = [1 + sum(MATRIX_BLOCKS[:k]) for k in range(len(MATRIX_BLOCKS))]
LIMITS = [1] + [MATRIX_STARTS[k] + MATRIX_BLOCKS[k] for k in range(len(MATRIX_BLOCKS))]
GROUPS = [(0, 1, 2, 3), (4, 5, 6)]


def product(left, right):
    return jnp.dot(left, right, preferred_element_type=F32)


def left_product(left, right):
    return lax.dot_general(left, right, (((0,), (0,)), ((), ())), preferred_element_type=F32)


def right_product(left, right):
    return lax.dot_general(left, right, (((1,), (1,)), ((), ())), preferred_element_type=F32)


def normalize(values):
    scale = lax.rsqrt(jnp.mean(values * values, axis=-1, keepdims=True) + NORM_EPSILON)
    return (values * scale, scale)


def norm_back(grad_hat, normed_rows, scale):
    return scale * (
        grad_hat - normed_rows * jnp.mean(grad_hat * normed_rows, axis=-1, keepdims=True)
    )


def swap(values, mask):
    return lax.ppermute(values, "tok", [(i, i ^ mask) for i in range(8)])


def gather_rows(rows, tok):
    if tok != 8:
        return lax.all_gather(rows, "tok", axis=0, tiled=False)
    count, width = rows.shape
    half = width // 2
    a, b = rows[:, :half], rows[:, half:]
    ax, by = swap(a, 2), swap(b, 4)
    a2, b2 = jnp.stack([a, ax]), jnp.stack([b, by])
    ay, bx = swap(a2, 4), swap(b2, 2)
    first = jnp.concatenate([a2, ay])
    second = jnp.stack([b, bx[0], by, bx[1]])
    full = jnp.concatenate([first, second], -1)
    other = swap(full, 1)
    return jnp.stack([full, other], 1).reshape(8, count, width)


def scatter_sum(parts, tok):
    if tok != 8:
        sent = lax.all_to_all(parts.astype(BF), "tok", 0, 0, tiled=True)
        return jnp.sum(sent.astype(F32), axis=0)
    _, count, width = parts.shape
    half = width // 2
    pairs = parts.reshape(4, 2, count, width)
    mine = pairs[:, 0] + swap(pairs[:, 1].astype(BF), 1).astype(F32)
    a, b = mine[..., :half], mine[..., half:]
    got_a = swap(a[2:].astype(BF), 4)
    got_b = swap(jnp.stack([b[1], b[3]]).astype(BF), 2)
    a = a[:2] + got_a.astype(F32)
    b = jnp.stack([b[0], b[2]]) + got_b.astype(F32)
    got_a = swap(a[1].astype(BF), 2)
    got_b = swap(b[1].astype(BF), 4)
    return jnp.concatenate([a[0] + got_a.astype(F32), b[0] + got_b.astype(F32)], -1)


def sharded(per_block, tok, group):
    return jnp.concatenate(
        [
            lax.slice_in_dim(
                per_block, MATRIX_STARTS[k], MATRIX_STARTS[k] + MATRIX_BLOCKS[k]
            ).reshape(tok, -1)
            for k in GROUPS[group]
        ],
        axis=1,
    )


def onehot(index, size):
    return (index[:, None] == jnp.arange(size, dtype=jnp.int32)[None, :]).astype(BF)


def before(size):
    rows = jnp.arange(size, dtype=jnp.int32)
    return (rows[:, None] < rows[None, :]).astype(BF)


def slot_ranks(owners, devices):
    count = owners.shape[0]
    chunks = -(-count // 128)
    padded = jnp.pad(owners, (0, chunks * 128 - count), constant_values=-1).reshape(chunks, 128)
    match = (
        padded[None] == jnp.arange(devices, dtype=jnp.int32)[:, None, None]
    ).astype(BF)
    within = jnp.einsum("ocl,lm->ocm", match, before(128), preferred_element_type=F32)
    totals = jnp.sum(match.astype(F32), axis=2)
    base = product(totals.astype(BF), before(chunks))
    ranks = jnp.sum(match.astype(F32) * (within + base[:, :, None]), axis=0)
    return ranks.reshape(-1)[:count].astype(jnp.int32)


def round_up(value, unit):
    return int(-(-value // unit) * unit)


class Route:
    def __init__(self, owners, slots, group, seq, tok, capacity):
        devices = seq * tok
        count = owners.shape[0]
        self.seq, self.tok, self.capacity, self.group = seq, tok, capacity, group
        self.owner = sharded(owners, tok, group)
        self.slot = sharded(slots, tok, group)
        size = self.owner.shape[1]
        self.size = size
        mean = capacity * size / count
        self.pair_cap = round_up(mean + 4.5 * math.sqrt(mean) + 2, 8)
        share = min(1.0, ((tok - 1) * count / devices + capacity) / count)
        mean = size * share
        self.row_cap = min(round_up(mean + 4.2 * math.sqrt(mean * (1 - share)), 16), round_up(size, 8))
        match = (
            self.owner[None] == jnp.arange(devices, dtype=jnp.int32)[:, None, None]
        ).astype(BF)
        earlier = jnp.einsum("otl,lm->otm", match, before(size), preferred_element_type=F32)
        pair_rank = jnp.sum(match.astype(F32) * earlier, axis=0).astype(jnp.int32)
        owner_seq = self.owner // tok
        earlier_seq = jnp.sum(earlier.reshape(seq, tok, tok, size), axis=1)
        match_seq = owner_seq[None] == jnp.arange(seq, dtype=jnp.int32)[:, None, None]
        row_rank = jnp.sum(jnp.where(match_seq, earlier_seq, 0.0), axis=0).astype(jnp.int32)
        self.fits = (jnp.max(pair_rank) < self.pair_cap) & (jnp.max(row_rank) < self.row_cap)
        me_seq, me_tok = lax.axis_index("seq"), lax.axis_index("tok")
        me = me_seq * tok + me_tok
        shard = jnp.arange(tok, dtype=jnp.int32)[:, None]
        place = jnp.where(pair_rank < self.pair_cap, shard * self.pair_cap + pair_rank, -1)
        own_slot = jnp.where(self.owner == me, self.slot, -1).reshape(-1)
        self.slot_of_shard = own_slot
        hit = own_slot[None, :] == jnp.arange(capacity, dtype=jnp.int32)[:, None]
        target = jnp.sum(jnp.where(hit, place.reshape(-1)[None, :] + 1, 0), axis=1) - 1
        self.send = onehot(target, tok * self.pair_cap)
        my_owner = lax.dynamic_index_in_dim(self.owner, me_tok, 0, keepdims=False)
        my_pair = lax.dynamic_index_in_dim(pair_rank, me_tok, 0, keepdims=False)
        my_row = lax.dynamic_index_in_dim(row_rank, me_tok, 0, keepdims=False)
        arrive = jnp.where(
            my_pair < self.pair_cap, (my_owner % tok) * self.pair_cap + my_pair, -1
        )
        from_pairs = onehot(arrive, tok * self.pair_cap)
        to_rows = onehot(jnp.where(my_owner // tok == me_seq, my_row, -1), self.row_cap)
        self.compact = left_product(to_rows, from_pairs).astype(BF)
        self.place = onehot(
            jnp.where(my_row < self.row_cap, (my_owner // tok) * self.row_cap + my_row, -1),
            seq * self.row_cap,
        )

    def fetch(self, rounded):
        width = rounded.shape[1]
        packed = left_product(self.send, rounded).astype(BF)
        packed = lax.all_to_all(packed, "tok", 0, 0, tiled=True)
        rows = product(self.compact, packed).astype(BF)
        rows = lax.all_gather(rows, "seq", axis=0, tiled=True)
        found = product(self.place, rows).astype(BF)

        def slow(found, rounded):
            index = jnp.maximum(self.slot_of_shard, 0)
            mine = jnp.where(
                (self.slot_of_shard >= 0)[:, None], jnp.take(rounded, index, axis=0), 0
            ).astype(BF)
            total = lax.psum(mine, ("seq", "tok")).reshape(self.tok, self.size, width)
            return lax.dynamic_index_in_dim(total, lax.axis_index("tok"), 0, keepdims=False)

        return lax.cond(self.fits, lambda found, rounded: found, slow, found, rounded)

    def give(self, grads):
        width = grads.shape[1]
        rows = left_product(self.place, grads).astype(BF)
        rows = lax.psum_scatter(rows, "seq", scatter_dimension=0, tiled=True)
        packed = left_product(self.compact, rows).astype(BF)
        packed = lax.all_to_all(packed, "tok", 0, 0, tiled=True)
        found = product(self.send, packed)

        def slow(found, grads):
            total = lax.psum(grads, "seq")
            every = lax.all_gather(total, "tok", axis=0, tiled=True)
            hit = self.slot_of_shard[None, :] == jnp.arange(self.capacity, dtype=jnp.int32)[:, None]
            number = jnp.arange(1, self.tok * self.size + 1, dtype=jnp.int32)
            index = jnp.sum(jnp.where(hit, number[None, :], 0), axis=1) - 1
            taken = jnp.take(every, jnp.maximum(index, 0), axis=0).astype(F32)
            return jnp.where((index >= 0)[:, None], taken, 0.0)

        return lax.cond(self.fits, lambda found, grads: found, slow, found, grads)


def rates_for(kinds, seq_len):
    out_std = 1.0 / math.sqrt(max(1, D * 16 // seq_len))
    matrix_rate = 3.0 / math.sqrt(D)
    rate_list = [
        1.0,
        matrix_rate,
        matrix_rate,
        matrix_rate,
        3.0 * out_std,
        matrix_rate,
        matrix_rate,
        3.0 / math.sqrt(FF),
        0.0,
    ]
    decay_list = [0.0] + [DECAY_RATE] * 7 + [0.0]
    chosen = (kinds[:, None] == jnp.arange(9, dtype=jnp.int32)[None, :]).astype(F32)
    rate_values = jnp.sum(chosen * jnp.array(rate_list, F32)[None, :], axis=1)
    decay_values = jnp.sum(chosen * jnp.array(decay_list, F32)[None, :], axis=1)
    return (rate_values, decay_values)


def adam_update(grads, moment_one, moment_two, weights, rate_values, decay_values):
    first = BETA_ONE * moment_one + (1.0 - BETA_ONE) * grads
    second = BETA_TWO * moment_two + (1.0 - BETA_TWO) * grads * grads
    first_hat = first / (1.0 - BETA_ONE**STEP)
    second_hat = second / (1.0 - BETA_TWO**STEP)
    updated = weights - rate_values[:, None] * (
        first_hat / (jnp.sqrt(second_hat) + ADAM_EPSILON) + decay_values[:, None] * weights
    )
    return (first, second, updated)


def columns_out(rows, split):
    return rows.reshape(rows.shape[0], split, -1).transpose(1, 0, 2)


def on_device(tokens, cotangent, owners, master, first_moment, second_moment):
    seq = lax.axis_size("seq")
    tok = lax.axis_size("tok")
    me_seq, me_tok = lax.axis_index("seq"), lax.axis_index("tok")
    me = me_seq * tok + me_tok
    capacity = master.shape[0]
    row_count = tokens.shape[1]
    seq_len = row_count * tok
    value_split = max(1, tok // HEADS)
    units = max(1, HEADS // tok)
    unit_width = DV // value_split
    slice_rows = D // tok
    ff_slice = FF // tok
    qk_width = units * FD
    v_width = units * unit_width

    x_all = gather_rows(tokens[0], tok)
    c_all = gather_rows(cotangent[0], tok).reshape(seq_len, D)

    slots = slot_ranks(owners, seq * tok)
    routes = [Route(owners, slots, group, seq, tok, capacity) for group in range(2)]
    rounded = master.astype(BF)
    gains = lax.psum(jnp.where(owners[0] == me, rounded[0], 0).astype(BF), ("seq", "tok"))
    gain_one = gains[:D].astype(F32)
    gain_two = gains[D:].astype(F32)

    shard = routes[0].fetch(rounded)
    a, b, c, d = (MATRIX_BLOCKS[k] // tok for k in GROUPS[0])

    def spread(columns):
        wide = columns.reshape(slice_rows, tok // value_split, 1, qk_width)
        return jnp.broadcast_to(
            wide, (slice_rows, tok // value_split, value_split, qk_width)
        ).reshape(slice_rows, tok, qk_width)

    sent = jnp.concatenate(
        [
            spread(shard[:a].reshape(slice_rows, HEADS * FD)),
            spread(shard[a : a + b].reshape(slice_rows, HEADS * FD)),
            shard[a + b : a + b + c].reshape(slice_rows, tok, v_width),
        ],
        axis=-1,
    ).transpose(1, 0, 2)
    w_qkv = lax.all_to_all(sent, "tok", 0, 0, tiled=True).reshape(D, -1)
    w_out = shard[a + b + c :].reshape(v_width, D)

    shard = routes[1].fetch(rounded)
    a = MATRIX_BLOCKS[4] // tok
    sent = jnp.concatenate(
        [
            columns_out(shard[:a].reshape(slice_rows, FF), tok),
            columns_out(shard[a : 2 * a].reshape(slice_rows, FF), tok),
        ],
        axis=-1,
    )
    w_gate_up = lax.all_to_all(sent, "tok", 0, 0, tiled=True).reshape(D, -1)
    w_down = shard[2 * a :].reshape(ff_slice, D)

    normed_all, scale_all = normalize(x_all.reshape(seq_len, D).astype(F32))
    hidden_one = (normed_all * gain_one).astype(BF)
    qkv = product(hidden_one, w_qkv).astype(BF)
    query = qkv[:, :qk_width].reshape(seq_len, units, FD).transpose(1, 0, 2)
    keys = qkv[:, qk_width : 2 * qk_width].reshape(seq_len, units, FD).transpose(1, 0, 2)
    values = qkv[:, 2 * qk_width :].reshape(seq_len, units, unit_width).transpose(1, 0, 2)
    place = jnp.arange(tok, dtype=jnp.int32)
    if tok == 8:
        place = place ^ me_tok
    index = (place[:, None] * row_count + jnp.arange(row_count, dtype=jnp.int32)[None, :]).reshape(-1)
    causal = (index[:, None] >= index[None, :])[None]
    inner = jnp.einsum("uif,ujf->uij", query, keys, preferred_element_type=F32) * (
        1.0 / math.sqrt(FD)
    )
    weight = jnp.where(causal, 1.0 + inner + 0.5 * inner * inner, 0.0)
    total = jnp.sum(weight, axis=2, keepdims=True)
    mixed_f = (
        jnp.einsum("uij,ujw->uiw", weight.astype(BF), values, preferred_element_type=F32) / total
    )
    mixed = mixed_f.astype(BF).transpose(1, 0, 2).reshape(seq_len, v_width)
    out = scatter_sum(product(mixed, w_out).reshape(tok, row_count, D), tok)

    input_rows = tokens[0].astype(F32)
    middle = input_rows + out
    normed_two, scale_two = normalize(middle)
    hidden_two = gather_rows((normed_two * gain_two).astype(BF), tok).reshape(seq_len, D)

    gate_up = product(hidden_two, w_gate_up)
    gate, up_proj = gate_up[:, :ff_slice], gate_up[:, ff_slice:]
    sigmoid = jax.nn.sigmoid(gate)
    activated = gate * sigmoid
    hidden = (activated * up_proj).astype(BF)
    grad_hidden = right_product(c_all, w_down)
    grad_gate = (grad_hidden * up_proj * sigmoid * (1.0 + gate * (1.0 - sigmoid))).astype(BF)
    grad_up = (grad_hidden * activated).astype(BF)
    grad_gate_up = jnp.concatenate([grad_gate, grad_up], axis=1)
    grad_two_terms = right_product(grad_gate_up, w_gate_up)
    grad_hidden_two = scatter_sum(grad_two_terms.reshape(tok, row_count, D), tok)
    result = middle + scatter_sum(product(hidden, w_down).reshape(tok, row_count, D), tok)
    result = result.astype(BF)

    grad_gain_two = jnp.sum(grad_hidden_two * normed_two, axis=0)
    grad_middle = cotangent[0].astype(F32) + norm_back(
        grad_hidden_two * gain_two, normed_two, scale_two
    )
    grad_mixer = gather_rows(grad_middle.astype(BF), tok).reshape(seq_len, D)

    grad_w_down = left_product(hidden, c_all).astype(BF)
    grad_w_gate_up = left_product(hidden_two, grad_gate_up).astype(BF)
    back = lax.all_to_all(
        grad_w_gate_up.reshape(tok, slice_rows, 2 * ff_slice), "tok", 0, 0, tiled=True
    )
    back_gate = back[..., :ff_slice].transpose(1, 0, 2).reshape(-1, BLK)
    back_up = back[..., ff_slice:].transpose(1, 0, 2).reshape(-1, BLK)
    reduced = routes[1].give(
        jnp.concatenate([back_gate, back_up, grad_w_down.reshape(-1, BLK)], axis=0)
    )

    grad_w_out = left_product(mixed, grad_mixer).astype(BF)
    grad_mixed = right_product(grad_mixer, w_out).astype(BF)
    grad_units = grad_mixed.reshape(seq_len, units, unit_width).transpose(1, 0, 2).astype(F32)
    grad_numer = (grad_units / total).astype(BF)
    grad_denom = -jnp.sum(grad_units * mixed_f, axis=-1, keepdims=True) / total
    grad_weight = (
        jnp.einsum("uiw,ujw->uij", grad_numer, values, preferred_element_type=F32) + grad_denom
    )
    grad_inner = (
        jnp.where(causal, grad_weight * (1.0 + inner), 0.0) * (1.0 / math.sqrt(FD))
    ).astype(BF)
    grad_query = jnp.einsum("uij,ujf->iuf", grad_inner, keys, preferred_element_type=F32)
    grad_keys = jnp.einsum("uij,uif->juf", grad_inner, query, preferred_element_type=F32)
    grad_values = jnp.einsum(
        "uij,uiw->juw", weight.astype(BF), grad_numer, preferred_element_type=F32
    )
    grad_qkv = jnp.concatenate(
        [
            grad_query.reshape(seq_len, -1),
            grad_keys.reshape(seq_len, -1),
            grad_values.reshape(seq_len, -1),
        ],
        axis=1,
    ).astype(BF)
    grad_w_qkv = left_product(hidden_one, grad_qkv).astype(BF)
    grad_hidden_one = scatter_sum(
        right_product(grad_qkv, w_qkv).reshape(tok, row_count, D), tok
    )
    back = lax.all_to_all(
        grad_w_qkv.reshape(tok, slice_rows, -1), "tok", 0, 0, tiled=True
    ).transpose(1, 0, 2)

    def gathered(columns):
        if value_split > 1:
            columns = jnp.sum(
                columns.reshape(slice_rows, tok // value_split, value_split, -1).astype(F32), axis=2
            ).astype(BF)
        return columns.reshape(-1, BLK)

    reduced = reduced + routes[0].give(
        jnp.concatenate(
            [
                gathered(back[..., :qk_width]),
                gathered(back[..., qk_width : 2 * qk_width]),
                back[..., 2 * qk_width :].reshape(-1, BLK),
                grad_w_out.reshape(-1, BLK),
            ],
            axis=0,
        )
    )

    normed_one, scale_one = normalize(input_rows)
    grad_gain_one = jnp.sum(grad_hidden_one * normed_one, axis=0)
    grad_input = grad_middle + norm_back(grad_hidden_one * gain_one, normed_one, scale_one)
    grad_gains = lax.psum(jnp.concatenate([grad_gain_one, grad_gain_two]), ("seq", "tok"))
    at_gains = (jnp.arange(capacity, dtype=jnp.int32) == 0) & (owners[0] == me)
    reduced = reduced + jnp.where(at_gains[:, None], grad_gains[None, :], 0.0)

    mine = (owners == me)[None, :]
    numbers = jnp.arange(owners.shape[0], dtype=jnp.int32)[None, :]
    counts = jnp.sum((mine & (numbers < jnp.array(LIMITS, jnp.int32)[:, None])).astype(jnp.int32), axis=1)
    kinds = jnp.sum(
        (jnp.arange(capacity, dtype=jnp.int32)[:, None] >= counts[None, :]).astype(jnp.int32), axis=1
    )
    rate_values, decay_values = rates_for(kinds, seq_len)
    first, second, updated = adam_update(
        reduced, first_moment, second_moment, master, rate_values, decay_values
    )
    return (result[None], grad_input.astype(BF)[None], reduced, first, second, updated)


def solution(mesh):
    in_specs = (
        P("seq", "tok", None),
        P("seq", "tok", None),
        P(),
        P(("seq", "tok"), None),
        P(("seq", "tok"), None),
        P(("seq", "tok"), None),
    )
    out_specs = (
        P("seq", "tok", None),
        P("seq", "tok", None),
        P(("seq", "tok"), None),
        P(("seq", "tok"), None),
        P(("seq", "tok"), None),
        P(("seq", "tok"), None),
    )
    return jax.shard_map(
        on_device, mesh=mesh, in_specs=in_specs, out_specs=out_specs, check_vma=False
    )
```

```python
import math

import jax
import jax.numpy as jnp
from jax import lax
from jax.sharding import PartitionSpec as P

D = 1024
HEADS = 16
FD = 16
DV = 64
FF = 2752
STEP = 10
BLK = 2048

NORM_EPSILON = 1e-05
ADAM_EPSILON = 1e-08
BETA_ONE = 0.9
BETA_TWO = 0.95
DECAY_RATE = 0.1
BF = jnp.bfloat16
F32 = jnp.float32


MATRIX_BLOCKS = [
    D * HEADS * FD // BLK,
    D * HEADS * FD // BLK,
    D * HEADS * DV // BLK,
    HEADS * DV * D // BLK,
    D * FF // BLK,
    D * FF // BLK,
    FF * D // BLK,
]
MATRIX_STARTS = [1 + sum(MATRIX_BLOCKS[:k]) for k in range(len(MATRIX_BLOCKS))]
LIMITS = [1] + [MATRIX_STARTS[k] + MATRIX_BLOCKS[k] for k in range(len(MATRIX_BLOCKS))]
GROUPS = [(0, 1, 2, 3), (4, 5, 6)]


def product(left, right):
    return jnp.dot(left, right, preferred_element_type=F32)


def left_product(left, right):
    return lax.dot_general(left, right, (((0,), (0,)), ((), ())), preferred_element_type=F32)


def right_product(left, right):
    return lax.dot_general(left, right, (((1,), (1,)), ((), ())), preferred_element_type=F32)


def normalize(values):
    scale = lax.rsqrt(jnp.mean(values * values, axis=-1, keepdims=True) + NORM_EPSILON)
    return (values * scale, scale)


def norm_back(grad_hat, normed_rows, scale):
    return scale * (
        grad_hat - normed_rows * jnp.mean(grad_hat * normed_rows, axis=-1, keepdims=True)
    )


def swap(values, mask):
    return lax.ppermute(values, "tok", [(i, i ^ mask) for i in range(8)])


def gather_rows(rows, tok):
    if tok != 8:
        return lax.all_gather(rows, "tok", axis=0, tiled=False)
    count, width = rows.shape
    half = width // 2
    a, b = rows[:, :half], rows[:, half:]
    ax, by = swap(a, 2), swap(b, 4)
    a2, b2 = jnp.stack([a, ax]), jnp.stack([b, by])
    ay, bx = swap(a2, 4), swap(b2, 2)
    first = jnp.concatenate([a2, ay])
    second = jnp.stack([b, bx[0], by, bx[1]])
    full = jnp.concatenate([first, second], -1)
    other = swap(full, 1)
    return jnp.stack([full, other], 1).reshape(8, count, width)


def scatter_sum(parts, tok):
    if tok != 8:
        sent = lax.all_to_all(parts.astype(BF), "tok", 0, 0, tiled=True)
        return jnp.sum(sent.astype(F32), axis=0)
    _, count, width = parts.shape
    half = width // 2
    pairs = parts.reshape(4, 2, count, width)
    mine = pairs[:, 0] + swap(pairs[:, 1].astype(BF), 1).astype(F32)
    a, b = mine[..., :half], mine[..., half:]
    got_a = swap(a[2:].astype(BF), 4)
    got_b = swap(jnp.stack([b[1], b[3]]).astype(BF), 2)
    a = a[:2] + got_a.astype(F32)
    b = jnp.stack([b[0], b[2]]) + got_b.astype(F32)
    got_a = swap(a[1].astype(BF), 2)
    got_b = swap(b[1].astype(BF), 4)
    return jnp.concatenate([a[0] + got_a.astype(F32), b[0] + got_b.astype(F32)], -1)


def ff_share(tok):
    return round_up(FF / tok, 128)


def sharded(per_block, tok, group, fill):
    pieces = []
    if group == 0:
        pieces.append(jnp.broadcast_to(per_block[:1][None], (tok, 1)))
    for k in GROUPS[group]:
        piece = lax.slice_in_dim(per_block, MATRIX_STARTS[k], MATRIX_STARTS[k] + MATRIX_BLOCKS[k])
        if k == 6:
            missing = tok * ff_share(tok) * D // BLK - MATRIX_BLOCKS[k]
            piece = jnp.pad(piece, (0, missing), constant_values=fill)
        pieces.append(piece.reshape(tok, -1))
    return jnp.concatenate(pieces, axis=1)


def line(count, step):
    return [(i, i + step) for i in range(count) if 0 <= i + step < count]


def rotate(values, count):
    return lax.ppermute(values, "seq", [(i, (i + 1) % count) for i in range(count)])


def gather_line(rows, seq):
    up, down = rows, rows
    ups, downs = [], []
    for _ in range(seq - 1):
        up = lax.ppermute(up, "seq", line(seq, 1))
        down = lax.ppermute(down, "seq", line(seq, -1))
        ups.append(up)
        downs.append(down)
    return jnp.concatenate([rows] + [downs[m - 1] + ups[seq - m - 1] for m in range(1, seq)])


def sum_line(pieces, seq):
    pieces = pieces.reshape(seq, -1, pieces.shape[1])
    up = down = None
    for k in range(1, seq):
        own_up, own_down = pieces[seq - k], pieces[k]
        up = own_up if up is None else (own_up.astype(F32) + up.astype(F32)).astype(BF)
        down = own_down if down is None else (own_down.astype(F32) + down.astype(F32)).astype(BF)
        up = lax.ppermute(up, "seq", line(seq, 1))
        down = lax.ppermute(down, "seq", line(seq, -1))
    return pieces[0].astype(F32) + up.astype(F32) + down.astype(F32)


def onehot(index, size):
    return (index[:, None] == jnp.arange(size, dtype=jnp.int32)[None, :]).astype(BF)


def before(size):
    rows = jnp.arange(size, dtype=jnp.int32)
    return (rows[:, None] < rows[None, :]).astype(BF)


def slot_ranks(owners, devices):
    count = owners.shape[0]
    chunks = -(-count // 128)
    padded = jnp.pad(owners, (0, chunks * 128 - count), constant_values=-1).reshape(chunks, 128)
    match = (
        padded[None] == jnp.arange(devices, dtype=jnp.int32)[:, None, None]
    ).astype(BF)
    within = jnp.einsum("ocl,lm->ocm", match, before(128), preferred_element_type=F32)
    totals = jnp.sum(match.astype(F32), axis=2)
    base = product(totals.astype(BF), before(chunks))
    ranks = jnp.sum(match.astype(F32) * (within + base[:, :, None]), axis=0)
    return ranks.reshape(-1)[:count].astype(jnp.int32)


def round_up(value, unit):
    return int(-(-value // unit) * unit)


class Route:
    def __init__(self, owners, slots, group, seq, tok, capacity):
        devices = seq * tok
        count = owners.shape[0]
        self.seq, self.tok, self.capacity, self.group = seq, tok, capacity, group
        owner = sharded(owners, tok, group, -1)
        slot = sharded(slots, tok, group, 0)
        size = owner.shape[1]
        self.size = size
        mean = capacity * size / count
        self.pair_cap = round_up(mean + 4.2 * math.sqrt(mean) + 1, 8)
        share = min(1.0, ((tok - 1) * count / devices + capacity) / count)
        mean = size * share
        self.row_cap = min(round_up(mean + 3.7 * math.sqrt(mean * (1 - share)), 8), round_up(size, 8))
        match = (owner[None] == jnp.arange(devices, dtype=jnp.int32)[:, None, None]).astype(BF)
        earlier = jnp.einsum("otl,lm->otm", match, before(size), preferred_element_type=F32)
        pair_rank = jnp.sum(match.astype(F32) * earlier, axis=0).astype(jnp.int32)
        owner_seq = jnp.where(owner >= 0, owner // tok, -1)
        earlier_seq = jnp.sum(earlier.reshape(seq, tok, tok, size), axis=1)
        match_seq = owner_seq[None] == jnp.arange(seq, dtype=jnp.int32)[:, None, None]
        row_rank = jnp.sum(jnp.where(match_seq, earlier_seq, 0.0), axis=0).astype(jnp.int32)
        self.fits = (jnp.max(pair_rank) < self.pair_cap) & (jnp.max(row_rank) < self.row_cap)
        me_seq, me_tok = lax.axis_index("seq"), lax.axis_index("tok")
        me = me_seq * tok + me_tok
        shard = jnp.arange(tok, dtype=jnp.int32)[:, None]
        place = jnp.where(pair_rank < self.pair_cap, shard * self.pair_cap + pair_rank, -1)
        self.own_slot = jnp.where(owner == me, slot, -1)
        self.has_gains = (owners[0] == me) & (jnp.arange(capacity, dtype=jnp.int32) == 0)
        once = 1 if group == 0 else 0
        own_slot = self.own_slot[:, once:].reshape(-1)
        hit = own_slot[None, :] == jnp.arange(capacity, dtype=jnp.int32)[:, None]
        target = (
            jnp.sum(jnp.where(hit, place[:, once:].reshape(-1)[None, :] + 1, 0), axis=1) - 1
        )
        columns = jnp.arange(tok * self.pair_cap, dtype=jnp.int32)[None, :]
        send = target[:, None] == columns
        if once:
            send = send | (self.has_gains[:, None] & (columns % self.pair_cap == 0))
        self.send = send.astype(BF)
        my_owner = lax.dynamic_index_in_dim(owner, me_tok, 0, keepdims=False)
        my_seq = lax.dynamic_index_in_dim(owner_seq, me_tok, 0, keepdims=False)
        my_pair = lax.dynamic_index_in_dim(pair_rank, me_tok, 0, keepdims=False)
        my_row = lax.dynamic_index_in_dim(row_rank, me_tok, 0, keepdims=False)
        arrive = jnp.where(
            (my_pair < self.pair_cap) & (my_owner >= 0),
            (my_owner % tok) * self.pair_cap + my_pair,
            -1,
        )
        from_pairs = onehot(arrive, tok * self.pair_cap)
        to_rows = onehot(jnp.where(my_seq == me_seq, my_row, -1), self.row_cap)
        self.compact = left_product(to_rows, from_pairs).astype(BF)
        self.place = onehot(
            jnp.where(
                (my_row < self.row_cap) & (my_owner >= 0),
                ((my_seq - me_seq + seq) % seq) * self.row_cap + my_row,
                -1,
            ),
            seq * self.row_cap,
        )

    def fetch(self, rounded):
        width = rounded.shape[1]
        packed = left_product(self.send, rounded).astype(BF)
        packed = lax.all_to_all(packed, "tok", 0, 0, tiled=True)
        rows = product(self.compact, packed).astype(BF)
        found = product(self.place, gather_line(rows, self.seq)).astype(BF)

        def slow(found, rounded):
            own = self.own_slot.reshape(-1)
            mine = jnp.where(
                (own >= 0)[:, None], jnp.take(rounded, jnp.maximum(own, 0), axis=0), 0
            ).astype(BF)
            mine = lax.all_to_all(
                mine.reshape(self.tok, self.size, width), "tok", 0, 0, tiled=True
            )
            mine = jnp.sum(mine, axis=0)
            total = mine
            for _ in range(self.seq - 1):
                mine = rotate(mine, self.seq)
                total = total + mine
            return total

        return lax.cond(self.fits, lambda found, rounded: found, slow, found, rounded)

    def give(self, grads):
        width = grads.shape[1]
        rows = left_product(self.place, grads).astype(BF)
        rows = sum_line(rows, self.seq).astype(BF)
        packed = left_product(self.compact, rows).astype(BF)
        packed = lax.all_to_all(packed, "tok", 0, 0, tiled=True)
        found = product(self.send, packed)

        def slow(found, grads):
            total = grads.astype(F32)
            passing = grads
            for _ in range(self.seq - 1):
                passing = rotate(passing, self.seq)
                total = total + passing.astype(F32)
            every = jnp.broadcast_to(total.astype(BF)[None], (self.tok, self.size, width))
            every = lax.all_to_all(every, "tok", 0, 0, tiled=True)
            once = 1 if self.group == 0 else 0
            own = self.own_slot[:, once:].reshape(-1)
            hit = own[None, :] == jnp.arange(self.capacity, dtype=jnp.int32)[:, None]
            index = jnp.sum(
                jnp.where(hit, jnp.arange(1, own.shape[0] + 1, dtype=jnp.int32)[None, :], 0), axis=1
            )
            taken = jnp.take(
                every[:, once:].reshape(-1, width), jnp.maximum(index - 1, 0), axis=0
            ).astype(F32)
            taken = jnp.where((index > 0)[:, None], taken, 0.0)
            if once:
                gains = jnp.sum(every[:, 0].astype(F32), axis=0)
                taken = jnp.where(self.has_gains[:, None], gains[None, :], taken)
            return taken

        return lax.cond(self.fits, lambda found, grads: found, slow, found, grads)


def rates_for(kinds, seq_len):
    out_std = 1.0 / math.sqrt(max(1, D * 16 // seq_len))
    matrix_rate = 3.0 / math.sqrt(D)
    rate_list = [
        1.0,
        matrix_rate,
        matrix_rate,
        matrix_rate,
        3.0 * out_std,
        matrix_rate,
        matrix_rate,
        3.0 / math.sqrt(FF),
        0.0,
    ]
    decay_list = [0.0] + [DECAY_RATE] * 7 + [0.0]
    chosen = (kinds[:, None] == jnp.arange(9, dtype=jnp.int32)[None, :]).astype(F32)
    rate_values = jnp.sum(chosen * jnp.array(rate_list, F32)[None, :], axis=1)
    decay_values = jnp.sum(chosen * jnp.array(decay_list, F32)[None, :], axis=1)
    return (rate_values, decay_values)


def adam_update(grads, moment_one, moment_two, weights, rate_values, decay_values):
    first = BETA_ONE * moment_one + (1.0 - BETA_ONE) * grads
    second = BETA_TWO * moment_two + (1.0 - BETA_TWO) * grads * grads
    first_hat = first / (1.0 - BETA_ONE**STEP)
    second_hat = second / (1.0 - BETA_TWO**STEP)
    updated = weights - rate_values[:, None] * (
        first_hat / (jnp.sqrt(second_hat) + ADAM_EPSILON) + decay_values[:, None] * weights
    )
    return (first, second, updated)


def columns_out(rows, split):
    return rows.reshape(rows.shape[0], split, -1).transpose(1, 0, 2)


def on_device(tokens, cotangent, owners, master, first_moment, second_moment):
    seq = lax.axis_size("seq")
    tok = lax.axis_size("tok")
    me_seq, me_tok = lax.axis_index("seq"), lax.axis_index("tok")
    me = me_seq * tok + me_tok
    capacity = master.shape[0]
    row_count = tokens.shape[1]
    seq_len = row_count * tok
    value_split = max(1, tok // HEADS)
    units = max(1, HEADS // tok)
    unit_width = DV // value_split
    slice_rows = D // tok
    ff_slice = ff_share(tok)
    qk_width = units * FD
    v_width = units * unit_width

    x_all = gather_rows(tokens[0], tok)
    c_all = gather_rows(cotangent[0], tok).reshape(seq_len, D)

    slots = slot_ranks(owners, seq * tok)
    routes = [Route(owners, slots, group, seq, tok, capacity) for group in range(2)]
    rounded = master.astype(BF)
    shard = routes[0].fetch(rounded)
    gain_one = shard[0, :D].astype(F32)
    gain_two = shard[0, D:].astype(F32)
    shard = shard[1:]
    a, b, c, d = (MATRIX_BLOCKS[k] // tok for k in GROUPS[0])

    def spread(columns):
        wide = columns.reshape(slice_rows, tok // value_split, 1, qk_width)
        return jnp.broadcast_to(
            wide, (slice_rows, tok // value_split, value_split, qk_width)
        ).reshape(slice_rows, tok, qk_width)

    sent = jnp.concatenate(
        [
            spread(shard[:a].reshape(slice_rows, HEADS * FD)),
            spread(shard[a : a + b].reshape(slice_rows, HEADS * FD)),
            shard[a + b : a + b + c].reshape(slice_rows, tok, v_width),
        ],
        axis=-1,
    ).transpose(1, 0, 2)
    w_qkv = lax.all_to_all(sent, "tok", 0, 0, tiled=True).reshape(D, -1)
    w_out = shard[a + b + c :].reshape(v_width, D)

    def padded(blocks):
        return jnp.pad(blocks.reshape(slice_rows, FF), ((0, 0), (0, tok * ff_slice - FF)))

    shard = routes[1].fetch(rounded)
    a = MATRIX_BLOCKS[4] // tok
    sent = jnp.concatenate(
        [
            columns_out(padded(shard[:a]), tok),
            columns_out(padded(shard[a : 2 * a]), tok),
        ],
        axis=-1,
    )
    w_gate_up = lax.all_to_all(sent, "tok", 0, 0, tiled=True).reshape(D, -1)
    w_down = shard[2 * a :].reshape(ff_slice, D)

    normed_all, scale_all = normalize(x_all.reshape(seq_len, D).astype(F32))
    hidden_one = (normed_all * gain_one).astype(BF)
    qkv = product(hidden_one, w_qkv).astype(BF)
    query = qkv[:, :qk_width].reshape(seq_len, units, FD).transpose(1, 0, 2)
    keys = qkv[:, qk_width : 2 * qk_width].reshape(seq_len, units, FD).transpose(1, 0, 2)
    values = qkv[:, 2 * qk_width :].reshape(seq_len, units, unit_width).transpose(1, 0, 2)
    place = jnp.arange(tok, dtype=jnp.int32)
    if tok == 8:
        place = place ^ me_tok
    index = (place[:, None] * row_count + jnp.arange(row_count, dtype=jnp.int32)[None, :]).reshape(-1)
    causal = (index[:, None] >= index[None, :])[None]
    inner = jnp.einsum("uif,ujf->uij", query, keys, preferred_element_type=F32) * (
        1.0 / math.sqrt(FD)
    )
    weight = jnp.where(causal, 1.0 + inner + 0.5 * inner * inner, 0.0)
    total = jnp.sum(weight, axis=2, keepdims=True)
    mixed_f = (
        jnp.einsum("uij,ujw->uiw", weight.astype(BF), values, preferred_element_type=F32) / total
    )
    mixed = mixed_f.astype(BF).transpose(1, 0, 2).reshape(seq_len, v_width)
    out = scatter_sum(product(mixed, w_out).reshape(tok, row_count, D), tok)

    input_rows = tokens[0].astype(F32)
    middle = input_rows + out
    normed_two, scale_two = normalize(middle)
    hidden_two = gather_rows((normed_two * gain_two).astype(BF), tok).reshape(seq_len, D)

    gate_up = product(hidden_two, w_gate_up)
    gate, up_proj = gate_up[:, :ff_slice], gate_up[:, ff_slice:]
    sigmoid = jax.nn.sigmoid(gate)
    activated = gate * sigmoid
    hidden = (activated * up_proj).astype(BF)
    grad_hidden = right_product(c_all, w_down)
    grad_gate = (grad_hidden * up_proj * sigmoid * (1.0 + gate * (1.0 - sigmoid))).astype(BF)
    grad_up = (grad_hidden * activated).astype(BF)
    grad_gate_up = jnp.concatenate([grad_gate, grad_up], axis=1)
    grad_two_terms = right_product(grad_gate_up, w_gate_up)
    grad_hidden_two = scatter_sum(grad_two_terms.reshape(tok, row_count, D), tok)
    result = middle + scatter_sum(product(hidden, w_down).reshape(tok, row_count, D), tok)
    result = result.astype(BF)

    grad_gain_two = jnp.sum(grad_hidden_two * normed_two, axis=0)
    grad_middle = cotangent[0].astype(F32) + norm_back(
        grad_hidden_two * gain_two, normed_two, scale_two
    )
    grad_mixer = gather_rows(grad_middle.astype(BF), tok).reshape(seq_len, D)

    grad_w_down = left_product(hidden, c_all).astype(BF)
    grad_w_gate_up = left_product(hidden_two, grad_gate_up).astype(BF)
    back = lax.all_to_all(
        grad_w_gate_up.reshape(tok, slice_rows, 2 * ff_slice), "tok", 0, 0, tiled=True
    )

    def flat(columns):
        rows = columns.transpose(1, 0, 2).reshape(slice_rows, tok * ff_slice)
        return rows[:, :FF].reshape(-1, BLK)

    back_gate, back_up = flat(back[..., :ff_slice]), flat(back[..., ff_slice:])
    reduced = routes[1].give(
        jnp.concatenate([back_gate, back_up, grad_w_down.reshape(-1, BLK)], axis=0)
    )

    grad_w_out = left_product(mixed, grad_mixer).astype(BF)
    grad_mixed = right_product(grad_mixer, w_out).astype(BF)
    grad_units = grad_mixed.reshape(seq_len, units, unit_width).transpose(1, 0, 2).astype(F32)
    grad_numer = (grad_units / total).astype(BF)
    grad_denom = -jnp.sum(grad_units * mixed_f, axis=-1, keepdims=True) / total
    grad_weight = (
        jnp.einsum("uiw,ujw->uij", grad_numer, values, preferred_element_type=F32) + grad_denom
    )
    grad_inner = (
        jnp.where(causal, grad_weight * (1.0 + inner), 0.0) * (1.0 / math.sqrt(FD))
    ).astype(BF)
    grad_query = jnp.einsum("uij,ujf->iuf", grad_inner, keys, preferred_element_type=F32)
    grad_keys = jnp.einsum("uij,uif->juf", grad_inner, query, preferred_element_type=F32)
    grad_values = jnp.einsum(
        "uij,uiw->juw", weight.astype(BF), grad_numer, preferred_element_type=F32
    )
    grad_qkv = jnp.concatenate(
        [
            grad_query.reshape(seq_len, -1),
            grad_keys.reshape(seq_len, -1),
            grad_values.reshape(seq_len, -1),
        ],
        axis=1,
    ).astype(BF)
    grad_w_qkv = left_product(hidden_one, grad_qkv).astype(BF)
    grad_one_terms = right_product(grad_qkv, w_qkv)
    grad_hidden_one = scatter_sum(grad_one_terms.reshape(tok, row_count, D), tok)
    grad_gains = jnp.concatenate([jnp.sum(grad_one_terms * normed_all, axis=0), grad_gain_two])
    back = lax.all_to_all(
        grad_w_qkv.reshape(tok, slice_rows, -1), "tok", 0, 0, tiled=True
    ).transpose(1, 0, 2)

    def gathered(columns):
        if value_split > 1:
            columns = jnp.sum(
                columns.reshape(slice_rows, tok // value_split, value_split, -1).astype(F32), axis=2
            ).astype(BF)
        return columns.reshape(-1, BLK)

    reduced = reduced + routes[0].give(
        jnp.concatenate(
            [
                grad_gains.astype(BF).reshape(1, BLK),
                gathered(back[..., :qk_width]),
                gathered(back[..., qk_width : 2 * qk_width]),
                back[..., 2 * qk_width :].reshape(-1, BLK),
                grad_w_out.reshape(-1, BLK),
            ],
            axis=0,
        )
    )

    normed_one, scale_one = normalize(input_rows)
    grad_input = grad_middle + norm_back(grad_hidden_one * gain_one, normed_one, scale_one)
    mine = (owners == me)[None, :]
    numbers = jnp.arange(owners.shape[0], dtype=jnp.int32)[None, :]
    counts = jnp.sum((mine & (numbers < jnp.array(LIMITS, jnp.int32)[:, None])).astype(jnp.int32), axis=1)
    kinds = jnp.sum(
        (jnp.arange(capacity, dtype=jnp.int32)[:, None] >= counts[None, :]).astype(jnp.int32), axis=1
    )
    rate_values, decay_values = rates_for(kinds, seq_len)
    first, second, updated = adam_update(
        reduced, first_moment, second_moment, master, rate_values, decay_values
    )
    return (result[None], grad_input.astype(BF)[None], reduced, first, second, updated)


def solution(mesh):
    in_specs = (
        P("seq", "tok", None),
        P("seq", "tok", None),
        P(),
        P(("seq", "tok"), None),
        P(("seq", "tok"), None),
        P(("seq", "tok"), None),
    )
    out_specs = (
        P("seq", "tok", None),
        P("seq", "tok", None),
        P(("seq", "tok"), None),
        P(("seq", "tok"), None),
        P(("seq", "tok"), None),
        P(("seq", "tok"), None),
    )
    return jax.shard_map(
        on_device, mesh=mesh, in_specs=in_specs, out_specs=out_specs, check_vma=False
    )
```

```python
import math

import jax
import jax.numpy as jnp
from jax import lax
from jax.sharding import PartitionSpec as P


D = 1024
HEADS = 16
FD = 16
DV = 64
FF = 2752
STEP = 10
BLK = 2048

NORM_EPSILON = 1e-05
ADAM_EPSILON = 1e-08
BETA_ONE = 0.9
BETA_TWO = 0.95
DECAY_RATE = 0.1
BF = jnp.bfloat16
F32 = jnp.float32


MATRIX_BLOCKS = [
    D * HEADS * FD // BLK,
    D * HEADS * FD // BLK,
    D * HEADS * DV // BLK,
    HEADS * DV * D // BLK,
    D * FF // BLK,
    D * FF // BLK,
    FF * D // BLK,
]
MATRIX_STARTS = [1 + sum(MATRIX_BLOCKS[:k]) for k in range(len(MATRIX_BLOCKS))]
LIMITS = [1] + [MATRIX_STARTS[k] + MATRIX_BLOCKS[k] for k in range(len(MATRIX_BLOCKS))]
GROUPS = [(0, 1, 2, 3), (4, 5, 6)]


def product(left, right):
    return jnp.dot(left, right, preferred_element_type=F32)


def left_product(left, right):
    return lax.dot_general(left, right, (((0,), (0,)), ((), ())), preferred_element_type=F32)


def right_product(left, right):
    return lax.dot_general(left, right, (((1,), (1,)), ((), ())), preferred_element_type=F32)


def normalize(values):
    scale = lax.rsqrt(jnp.mean(values * values, axis=-1, keepdims=True) + NORM_EPSILON)
    return (values * scale, scale)


def norm_back(grad_hat, normed_rows, scale):
    return scale * (
        grad_hat - normed_rows * jnp.mean(grad_hat * normed_rows, axis=-1, keepdims=True)
    )


def swap(values, mask):
    return lax.ppermute(values, "tok", [(i, i ^ mask) for i in range(8)])


def exchange(values):
    return lax.all_to_all(values, "tok", 0, 0, tiled=True)


def gather_rows(rows, tok):
    if tok != 8:
        return lax.all_gather(rows, "tok", axis=0, tiled=False)
    count, width = rows.shape
    half = width // 2
    a, b = rows[:, :half], rows[:, half:]
    ax, by = swap(a, 2), swap(b, 4)
    a2, b2 = jnp.stack([a, ax]), jnp.stack([b, by])
    ay, bx = swap(a2, 4), swap(b2, 2)
    first = jnp.concatenate([a2, ay])
    second = jnp.stack([b, bx[0], by, bx[1]])
    full = jnp.concatenate([first, second], -1)
    other = swap(full, 1)
    return jnp.stack([full, other], 1).reshape(8, count, width)


def scatter_sum(parts, tok):
    if tok != 8:
        sent = exchange(parts.astype(BF))
        return jnp.sum(sent.astype(F32), axis=0)
    _, count, width = parts.shape
    half = width // 2
    pairs = parts.reshape(4, 2, count, width)
    mine = pairs[:, 0] + swap(pairs[:, 1].astype(BF), 1).astype(F32)
    a, b = mine[..., :half], mine[..., half:]
    got_a = swap(a[2:].astype(BF), 4)
    got_b = swap(jnp.stack([b[1], b[3]]).astype(BF), 2)
    a = a[:2] + got_a.astype(F32)
    b = jnp.stack([b[0], b[2]]) + got_b.astype(F32)
    got_a = swap(a[1].astype(BF), 2)
    got_b = swap(b[1].astype(BF), 4)
    return jnp.concatenate([a[0] + got_a.astype(F32), b[0] + got_b.astype(F32)], -1)


def ff_share(tok):
    return round_up(FF / tok, 128)


def sharded(per_block, tok, group, fill):
    pieces = []
    if group == 0:
        pieces.append(jnp.broadcast_to(per_block[:1][None], (tok, 1)))
    for k in GROUPS[group]:
        piece = lax.slice_in_dim(per_block, MATRIX_STARTS[k], MATRIX_STARTS[k] + MATRIX_BLOCKS[k])
        if k == 6:
            missing = tok * ff_share(tok) * D // BLK - MATRIX_BLOCKS[k]
            piece = jnp.pad(piece, (0, missing), constant_values=fill)
        pieces.append(piece.reshape(tok, -1))
    return jnp.concatenate(pieces, axis=1)


def line(count, step):
    return [(i, i + step) for i in range(count) if 0 <= i + step < count]


def rotate(values, count):
    return lax.ppermute(values, "seq", [(i, (i + 1) % count) for i in range(count)])


def shift(values, step, seq):
    return lax.ppermute(values, "seq", line(seq, step))


def gather_line(rows, seq):
    up, down = rows, rows
    ups, downs = [], []
    for _ in range(1, seq):
        up = shift(up, 1, seq)
        down = shift(down, -1, seq)
        ups.append(up)
        downs.append(down)
    return jnp.concatenate([rows] + [downs[m - 1] + ups[seq - m - 1] for m in range(1, seq)])


def sum_line(pieces, seq):
    pieces = pieces.reshape(seq, -1, pieces.shape[1])
    up = down = None
    for k in range(1, seq):
        own_up, own_down = pieces[seq - k], pieces[k]
        up = own_up if up is None else (own_up.astype(F32) + up.astype(F32)).astype(BF)
        down = own_down if down is None else (own_down.astype(F32) + down.astype(F32)).astype(BF)
        up = shift(up, 1, seq)
        down = shift(down, -1, seq)
    return pieces[0].astype(F32) + up.astype(F32) + down.astype(F32)


def onehot(index, size):
    return (index[:, None] == jnp.arange(size, dtype=jnp.int32)[None, :]).astype(BF)


def before(size):
    rows = jnp.arange(size, dtype=jnp.int32)
    return (rows[:, None] < rows[None, :]).astype(BF)


def slot_ranks(owners, devices):
    count = owners.shape[0]
    chunks = -(-count // 128)
    padded = jnp.pad(owners, (0, chunks * 128 - count), constant_values=-1).reshape(chunks, 128)
    match = (
        padded[None] == jnp.arange(devices, dtype=jnp.int32)[:, None, None]
    ).astype(BF)
    within = jnp.einsum("ocl,lm->ocm", match, before(128), preferred_element_type=F32)
    totals = jnp.sum(match.astype(F32), axis=2)
    base = product(totals.astype(BF), before(chunks))
    ranks = jnp.sum(match.astype(F32) * (within + base[:, :, None]), axis=0)
    return ranks.reshape(-1)[:count].astype(jnp.int32)


def round_up(value, unit):
    return int(-(-value // unit) * unit)


class Route:
    def __init__(self, owners, slots, group, seq, tok, capacity):
        devices = seq * tok
        count = owners.shape[0]
        self.seq, self.tok, self.capacity, self.group = seq, tok, capacity, group
        owner = sharded(owners, tok, group, -1)
        slot = sharded(slots, tok, group, 0)
        size = owner.shape[1]
        self.size = size
        mean = capacity * size / count
        self.pair_cap = round_up(mean + 4.2 * math.sqrt(mean) + 1, 8)
        share = min(1.0, ((tok - 1) * count / devices + capacity) / count)
        mean = size * share
        self.row_cap = min(round_up(mean + 3.7 * math.sqrt(mean * (1 - share)), 8), round_up(size, 8))
        match = (owner[None] == jnp.arange(devices, dtype=jnp.int32)[:, None, None]).astype(BF)
        earlier = jnp.einsum("otl,lm->otm", match, before(size), preferred_element_type=F32)
        pair_rank = jnp.sum(match.astype(F32) * earlier, axis=0).astype(jnp.int32)
        owner_seq = jnp.where(owner >= 0, owner // tok, -1)
        earlier_seq = jnp.sum(earlier.reshape(seq, tok, tok, size), axis=1)
        match_seq = owner_seq[None] == jnp.arange(seq, dtype=jnp.int32)[:, None, None]
        row_rank = jnp.sum(jnp.where(match_seq, earlier_seq, 0.0), axis=0).astype(jnp.int32)
        self.fits = (jnp.max(pair_rank) < self.pair_cap) & (jnp.max(row_rank) < self.row_cap)
        me_seq, me_tok = lax.axis_index("seq"), lax.axis_index("tok")
        me = me_seq * tok + me_tok
        shard = jnp.arange(tok, dtype=jnp.int32)[:, None]
        place = jnp.where(pair_rank < self.pair_cap, shard * self.pair_cap + pair_rank, -1)
        self.own_slot = jnp.where(owner == me, slot, -1)
        self.has_gains = (owners[0] == me) & (jnp.arange(capacity, dtype=jnp.int32) == 0)
        once = 1 if group == 0 else 0
        own_slot = self.own_slot[:, once:].reshape(-1)
        hit = own_slot[None, :] == jnp.arange(capacity, dtype=jnp.int32)[:, None]
        target = (
            jnp.sum(jnp.where(hit, place[:, once:].reshape(-1)[None, :] + 1, 0), axis=1) - 1
        )
        columns = jnp.arange(tok * self.pair_cap, dtype=jnp.int32)[None, :]
        send = target[:, None] == columns
        if once:
            send = send | (self.has_gains[:, None] & (columns % self.pair_cap == 0))
        self.send = send.astype(BF)
        my_owner = lax.dynamic_index_in_dim(owner, me_tok, 0, keepdims=False)
        my_seq = lax.dynamic_index_in_dim(owner_seq, me_tok, 0, keepdims=False)
        my_pair = lax.dynamic_index_in_dim(pair_rank, me_tok, 0, keepdims=False)
        my_row = lax.dynamic_index_in_dim(row_rank, me_tok, 0, keepdims=False)
        arrive = jnp.where(
            (my_pair < self.pair_cap) & (my_owner >= 0),
            (my_owner % tok) * self.pair_cap + my_pair,
            -1,
        )
        from_pairs = onehot(arrive, tok * self.pair_cap)
        to_rows = onehot(jnp.where(my_seq == me_seq, my_row, -1), self.row_cap)
        self.compact = left_product(to_rows, from_pairs).astype(BF)
        self.place = onehot(
            jnp.where(
                (my_row < self.row_cap) & (my_owner >= 0),
                ((my_seq - me_seq + seq) % seq) * self.row_cap + my_row,
                -1,
            ),
            seq * self.row_cap,
        )

    def fetch(self, rounded):
        packed = left_product(self.send, rounded).astype(BF)
        packed = exchange(packed)
        rows = product(self.compact, packed).astype(BF)
        rows = gather_line(rows, self.seq)
        return product(self.place, rows).astype(BF)

    def fetch_any(self, rounded):
        width = rounded.shape[1]
        own = self.own_slot.reshape(-1)
        mine = jnp.where(
            (own >= 0)[:, None], jnp.take(rounded, jnp.maximum(own, 0), axis=0), 0
        ).astype(BF)
        mine = lax.all_to_all(mine.reshape(self.tok, self.size, width), "tok", 0, 0, tiled=True)
        mine = jnp.sum(mine, axis=0)
        total = mine
        for _ in range(self.seq - 1):
            mine = rotate(mine, self.seq)
            total = total + mine
        return total

    def give(self, grads):
        rows = left_product(self.place, grads).astype(BF)
        rows = sum_line(rows, self.seq).astype(BF)
        packed = left_product(self.compact, rows).astype(BF)
        packed = exchange(packed)
        return product(self.send, packed)

    def give_any(self, grads):
        width = grads.shape[1]
        total = grads.astype(F32)
        passing = grads
        for _ in range(self.seq - 1):
            passing = rotate(passing, self.seq)
            total = total + passing.astype(F32)
        every = jnp.broadcast_to(total.astype(BF)[None], (self.tok, self.size, width))
        every = lax.all_to_all(every, "tok", 0, 0, tiled=True)
        once = 1 if self.group == 0 else 0
        own = self.own_slot[:, once:].reshape(-1)
        hit = own[None, :] == jnp.arange(self.capacity, dtype=jnp.int32)[:, None]
        index = jnp.sum(
            jnp.where(hit, jnp.arange(1, own.shape[0] + 1, dtype=jnp.int32)[None, :], 0), axis=1
        )
        taken = jnp.take(
            every[:, once:].reshape(-1, width), jnp.maximum(index - 1, 0), axis=0
        ).astype(F32)
        taken = jnp.where((index > 0)[:, None], taken, 0.0)
        if once:
            gains = jnp.sum(every[:, 0].astype(F32), axis=0)
            taken = jnp.where(self.has_gains[:, None], gains[None, :], taken)
        return taken


def rates_for(kinds, seq_len):
    out_std = 1.0 / math.sqrt(max(1, D * 16 // seq_len))
    matrix_rate = 3.0 / math.sqrt(D)
    rate_list = [
        1.0,
        matrix_rate,
        matrix_rate,
        matrix_rate,
        3.0 * out_std,
        matrix_rate,
        matrix_rate,
        3.0 / math.sqrt(FF),
        0.0,
    ]
    decay_list = [0.0] + [DECAY_RATE] * 7 + [0.0]
    chosen = (kinds[:, None] == jnp.arange(9, dtype=jnp.int32)[None, :]).astype(F32)
    rate_values = jnp.sum(chosen * jnp.array(rate_list, F32)[None, :], axis=1)
    decay_values = jnp.sum(chosen * jnp.array(decay_list, F32)[None, :], axis=1)
    return (rate_values, decay_values)


def adam_update(grads, moment_one, moment_two, weights, rate_values, decay_values):
    first = BETA_ONE * moment_one + (1.0 - BETA_ONE) * grads
    second = BETA_TWO * moment_two + (1.0 - BETA_TWO) * grads * grads
    first_hat = first / (1.0 - BETA_ONE**STEP)
    second_hat = second / (1.0 - BETA_TWO**STEP)
    updated = weights - rate_values[:, None] * (
        first_hat / (jnp.sqrt(second_hat) + ADAM_EPSILON) + decay_values[:, None] * weights
    )
    return (first, second, updated)


def columns_out(rows, split):
    return rows.reshape(rows.shape[0], split, -1).transpose(1, 0, 2)


def step(tokens, cotangent, owners, master, first_moment, second_moment):
    seq = lax.axis_size("seq")
    tok = lax.axis_size("tok")
    capacity = master.shape[0]
    me = lax.axis_index("seq") * tok + lax.axis_index("tok")
    slots = slot_ranks(owners, seq * tok)
    routes = [Route(owners, slots, group, seq, tok, capacity) for group in range(2)]
    rounded = master.astype(BF)
    found = layer(tokens, cotangent, rounded, [(r.fetch, r.give) for r in routes])

    def any_owners(tokens, cotangent, rounded, *found):
        return layer(tokens, cotangent, rounded, [(r.fetch_any, r.give_any) for r in routes])

    result, grad_input, reduced = lax.cond(
        routes[0].fits & routes[1].fits,
        lambda tokens, cotangent, rounded, *found: found,
        any_owners,
        tokens,
        cotangent,
        rounded,
        *found,
    )
    mine = (owners == me)[None, :]
    numbers = jnp.arange(owners.shape[0], dtype=jnp.int32)[None, :]
    counts = jnp.sum(
        (mine & (numbers < jnp.array(LIMITS, jnp.int32)[:, None])).astype(jnp.int32), axis=1
    )
    kinds = jnp.sum(
        (jnp.arange(capacity, dtype=jnp.int32)[:, None] >= counts[None, :]).astype(jnp.int32), axis=1
    )
    rate_values, decay_values = rates_for(kinds, tokens.shape[1] * tok)
    first, second, updated = adam_update(
        reduced, first_moment, second_moment, master, rate_values, decay_values
    )
    return (result[None], grad_input[None], reduced, first, second, updated)


def layer(tokens, cotangent, rounded, routes):
    tok = lax.axis_size("tok")
    me_tok = lax.axis_index("tok")
    row_count = tokens.shape[1]
    seq_len = row_count * tok
    value_split = max(1, tok // HEADS)
    units = max(1, HEADS // tok)
    unit_width = DV // value_split
    slice_rows = D // tok
    ff_slice = ff_share(tok)
    qk_width = units * FD
    v_width = units * unit_width

    x_all = gather_rows(tokens[0], tok)
    later, x_all = lax.optimization_barrier((cotangent[0], x_all))
    c_all = gather_rows(later, tok).reshape(seq_len, D)

    shard = routes[0][0](rounded)
    gain_one = shard[0, :D].astype(F32)
    gain_two = shard[0, D:].astype(F32)
    shard = shard[1:]
    a, b, c, _ = (MATRIX_BLOCKS[k] // tok for k in GROUPS[0])

    def spread(columns):
        wide = columns.reshape(slice_rows, tok // value_split, 1, qk_width)
        return jnp.broadcast_to(
            wide, (slice_rows, tok // value_split, value_split, qk_width)
        ).reshape(slice_rows, tok, qk_width)

    sent = jnp.concatenate(
        [
            spread(shard[:a].reshape(slice_rows, HEADS * FD)),
            spread(shard[a : a + b].reshape(slice_rows, HEADS * FD)),
            shard[a + b : a + b + c].reshape(slice_rows, tok, v_width),
        ],
        axis=-1,
    ).transpose(1, 0, 2)
    w_qkv = exchange(sent).reshape(D, -1)
    w_out = shard[a + b + c :].reshape(v_width, D)

    def padded(blocks):
        return jnp.pad(blocks.reshape(slice_rows, FF), ((0, 0), (0, tok * ff_slice - FF)))

    shard = routes[1][0](rounded)
    a = MATRIX_BLOCKS[4] // tok
    sent = jnp.concatenate(
        [
            columns_out(padded(shard[:a]), tok),
            columns_out(padded(shard[a : 2 * a]), tok),
        ],
        axis=-1,
    )
    w_gate_up = exchange(sent).reshape(D, -1)
    w_down = shard[2 * a :].reshape(ff_slice, D)

    normed_all, _ = normalize(x_all.reshape(seq_len, D).astype(F32))
    hidden_one = (normed_all * gain_one).astype(BF)
    qkv = product(hidden_one, w_qkv).astype(BF)
    query = qkv[:, :qk_width].reshape(seq_len, units, FD).transpose(1, 0, 2)
    keys = qkv[:, qk_width : 2 * qk_width].reshape(seq_len, units, FD).transpose(1, 0, 2)
    values = qkv[:, 2 * qk_width :].reshape(seq_len, units, unit_width).transpose(1, 0, 2)
    place = jnp.arange(tok, dtype=jnp.int32)
    if tok == 8:
        place = place ^ me_tok
    index = (place[:, None] * row_count + jnp.arange(row_count, dtype=jnp.int32)[None, :]).reshape(-1)
    causal = (index[:, None] >= index[None, :])[None]
    inner = jnp.einsum("uif,ujf->uij", query, keys, preferred_element_type=F32) * (
        1.0 / math.sqrt(FD)
    )
    weight = jnp.where(causal, 1.0 + inner + 0.5 * inner * inner, 0.0)
    total = jnp.sum(weight, axis=2, keepdims=True)
    mixed_f = (
        jnp.einsum("uij,ujw->uiw", weight.astype(BF), values, preferred_element_type=F32) / total
    )
    mixed = mixed_f.astype(BF).transpose(1, 0, 2).reshape(seq_len, v_width)
    out = scatter_sum(product(mixed, w_out).reshape(tok, row_count, D), tok)

    input_rows = tokens[0].astype(F32)
    middle = input_rows + out
    normed_two, scale_two = normalize(middle)
    hidden_two = gather_rows((normed_two * gain_two).astype(BF), tok).reshape(seq_len, D)

    gate_up = product(hidden_two, w_gate_up)
    gate, up_proj = gate_up[:, :ff_slice], gate_up[:, ff_slice:]
    sigmoid = jax.nn.sigmoid(gate)
    activated = gate * sigmoid
    hidden = (activated * up_proj).astype(BF)
    grad_hidden = right_product(c_all, w_down)
    grad_gate = (grad_hidden * up_proj * sigmoid * (1.0 + gate * (1.0 - sigmoid))).astype(BF)
    grad_up = (grad_hidden * activated).astype(BF)
    grad_gate_up = jnp.concatenate([grad_gate, grad_up], axis=1)
    grad_two_terms = right_product(grad_gate_up, w_gate_up)
    grad_hidden_two = scatter_sum(grad_two_terms.reshape(tok, row_count, D), tok)
    result_terms = product(hidden, w_down)

    grad_gain_two = jnp.sum(grad_hidden_two * normed_two, axis=0)
    grad_middle = cotangent[0].astype(F32) + norm_back(
        grad_hidden_two * gain_two, normed_two, scale_two
    )
    grad_mixer = gather_rows(grad_middle.astype(BF), tok).reshape(seq_len, D)

    grad_w_down = left_product(hidden, c_all).astype(BF)
    grad_w_gate_up = left_product(hidden_two, grad_gate_up).astype(BF)
    back = exchange(grad_w_gate_up.reshape(tok, slice_rows, 2 * ff_slice))

    def flat(columns):
        rows = columns.transpose(1, 0, 2).reshape(slice_rows, tok * ff_slice)
        return rows[:, :FF].reshape(-1, BLK)

    back_gate, back_up = flat(back[..., :ff_slice]), flat(back[..., ff_slice:])
    reduced = routes[1][1](
        jnp.concatenate([back_gate, back_up, grad_w_down.reshape(-1, BLK)], axis=0)
    )

    grad_w_out = left_product(mixed, grad_mixer).astype(BF)
    grad_mixed = right_product(grad_mixer, w_out).astype(BF)
    grad_units = grad_mixed.reshape(seq_len, units, unit_width).transpose(1, 0, 2).astype(F32)
    grad_numer = (grad_units / total).astype(BF)
    grad_denom = -jnp.sum(grad_units * mixed_f, axis=-1, keepdims=True) / total
    grad_weight = (
        jnp.einsum("uiw,ujw->uij", grad_numer, values, preferred_element_type=F32) + grad_denom
    )
    grad_inner = (
        jnp.where(causal, grad_weight * (1.0 + inner), 0.0) * (1.0 / math.sqrt(FD))
    ).astype(BF)
    grad_query = jnp.einsum("uij,ujf->iuf", grad_inner, keys, preferred_element_type=F32)
    grad_keys = jnp.einsum("uij,uif->juf", grad_inner, query, preferred_element_type=F32)
    grad_values = jnp.einsum(
        "uij,uiw->juw", weight.astype(BF), grad_numer, preferred_element_type=F32
    )
    grad_qkv = jnp.concatenate(
        [
            grad_query.reshape(seq_len, -1),
            grad_keys.reshape(seq_len, -1),
            grad_values.reshape(seq_len, -1),
        ],
        axis=1,
    ).astype(BF)
    result_terms, grad_qkv = lax.optimization_barrier((result_terms, grad_qkv))
    result = middle + scatter_sum(result_terms.reshape(tok, row_count, D), tok)
    result = result.astype(BF)
    grad_w_qkv = left_product(hidden_one, grad_qkv).astype(BF)
    grad_one_terms = right_product(grad_qkv, w_qkv)
    grad_hidden_one = scatter_sum(grad_one_terms.reshape(tok, row_count, D), tok)
    grad_gains = jnp.concatenate([jnp.sum(grad_one_terms * normed_all, axis=0), grad_gain_two])
    back = exchange(grad_w_qkv.reshape(tok, slice_rows, -1)).transpose(1, 0, 2)

    def gathered(columns):
        if value_split > 1:
            columns = jnp.sum(
                columns.reshape(slice_rows, tok // value_split, value_split, -1).astype(F32), axis=2
            ).astype(BF)
        return columns.reshape(-1, BLK)

    reduced = reduced + routes[0][1](
        jnp.concatenate(
            [
                grad_gains.astype(BF).reshape(1, BLK),
                gathered(back[..., :qk_width]),
                gathered(back[..., qk_width : 2 * qk_width]),
                back[..., 2 * qk_width :].reshape(-1, BLK),
                grad_w_out.reshape(-1, BLK),
            ],
            axis=0,
        )
    )

    normed_one, scale_one = normalize(input_rows)
    grad_input = grad_middle + norm_back(grad_hidden_one * gain_one, normed_one, scale_one)
    return result, grad_input.astype(BF), reduced


def solution(mesh):
    in_specs = (
        P("seq", "tok", None),
        P("seq", "tok", None),
        P(),
        P(("seq", "tok"), None),
        P(("seq", "tok"), None),
        P(("seq", "tok"), None),
    )
    out_specs = (
        P("seq", "tok", None),
        P("seq", "tok", None),
        P(("seq", "tok"), None),
        P(("seq", "tok"), None),
        P(("seq", "tok"), None),
        P(("seq", "tok"), None),
    )
    return jax.shard_map(step, mesh=mesh, in_specs=in_specs, out_specs=out_specs, check_vma=False)
```

```python
import math

import jax
import jax.numpy as jnp
from jax import lax
from jax.sharding import PartitionSpec as P


D = 1024
HEADS = 16
FD = 16
DV = 64
FF = 2752
STEP = 10
BLK = 2048

NORM_EPSILON = 1e-05
ADAM_EPSILON = 1e-08
BETA_ONE = 0.9
BETA_TWO = 0.95
DECAY_RATE = 0.1
BF = jnp.bfloat16
F32 = jnp.float32


MATRIX_BLOCKS = [
    D * HEADS * FD // BLK,
    D * HEADS * FD // BLK,
    D * HEADS * DV // BLK,
    HEADS * DV * D // BLK,
    D * FF // BLK,
    D * FF // BLK,
    FF * D // BLK,
]
MATRIX_STARTS = [1 + sum(MATRIX_BLOCKS[:k]) for k in range(len(MATRIX_BLOCKS))]
LIMITS = [1] + [MATRIX_STARTS[k] + MATRIX_BLOCKS[k] for k in range(len(MATRIX_BLOCKS))]
GROUPS = [(0, 1, 2, 3), (4, 5, 6)]


def product(left, right):
    return jnp.dot(left, right, preferred_element_type=F32)


def left_product(left, right):
    return lax.dot_general(left, right, (((0,), (0,)), ((), ())), preferred_element_type=F32)


def right_product(left, right):
    return lax.dot_general(left, right, (((1,), (1,)), ((), ())), preferred_element_type=F32)


def normalize(values):
    scale = lax.rsqrt(jnp.mean(values * values, axis=-1, keepdims=True) + NORM_EPSILON)
    return (values * scale, scale)


def norm_back(grad_hat, normed_rows, scale):
    return scale * (
        grad_hat - normed_rows * jnp.mean(grad_hat * normed_rows, axis=-1, keepdims=True)
    )


def swap(values, mask):
    return lax.ppermute(values, "tok", [(i, i ^ mask) for i in range(8)])


def exchange(values):
    return lax.all_to_all(values, "tok", 0, 0, tiled=True)


def gather_rows(rows, tok):
    if tok != 8:
        return lax.all_gather(rows, "tok", axis=1, tiled=False)
    half = rows.shape[2] // 2
    a, b = rows[:, :, :half], rows[:, :, half:]
    ax, by = swap(a, 2), swap(b, 4)
    a2, b2 = jnp.stack([a, ax], 1), jnp.stack([b, by], 1)
    ay, bx = swap(a2, 4), swap(b2, 2)
    first = jnp.concatenate([a2, ay], 1)
    second = jnp.stack([b, bx[:, 0], by, bx[:, 1]], 1)
    full = jnp.concatenate([first, second], -1)
    other = swap(full, 1)
    count = rows.shape[0]
    return jnp.stack([full, other], 2).reshape((count, 8) + rows.shape[1:])


def scatter_sum(parts, tok):
    if tok != 8:
        sent = lax.all_to_all(parts.astype(BF), "tok", 1, 1, tiled=True)
        return jnp.sum(sent.astype(F32), axis=1)
    many, _, count, width = parts.shape
    half = width // 2
    pairs = parts.reshape(many, 4, 2, count, width)
    mine = pairs[:, :, 0] + swap(pairs[:, :, 1].astype(BF), 1).astype(F32)
    a, b = mine[..., :half], mine[..., half:]
    got_a = swap(a[:, 2:].astype(BF), 4)
    got_b = swap(jnp.stack([b[:, 1], b[:, 3]], 1).astype(BF), 2)
    a = a[:, :2] + got_a.astype(F32)
    b = jnp.stack([b[:, 0], b[:, 2]], 1) + got_b.astype(F32)
    got_a = swap(a[:, 1].astype(BF), 2)
    got_b = swap(b[:, 1].astype(BF), 4)
    return jnp.concatenate([a[:, 0] + got_a.astype(F32), b[:, 0] + got_b.astype(F32)], -1)


def ff_share(tok):
    return round_up(FF / tok, 128)


def sharded(per_block, tok, group, fill):
    pieces = []
    if group == 0:
        pieces.append(jnp.broadcast_to(per_block[:1][None], (tok, 1)))
    for k in GROUPS[group]:
        piece = lax.slice_in_dim(per_block, MATRIX_STARTS[k], MATRIX_STARTS[k] + MATRIX_BLOCKS[k])
        if k == 6:
            missing = tok * ff_share(tok) * D // BLK - MATRIX_BLOCKS[k]
            piece = jnp.pad(piece, (0, missing), constant_values=fill)
        pieces.append(piece.reshape(tok, -1))
    return jnp.concatenate(pieces, axis=1)


def rotate(values, count):
    return lax.ppermute(values, "seq", [(i, (i + 1) % count) for i in range(count)])


def onehot(index, size):
    return (index[:, None] == jnp.arange(size, dtype=jnp.int32)[None, :]).astype(BF)


def before(size):
    rows = jnp.arange(size, dtype=jnp.int32)
    return (rows[:, None] < rows[None, :]).astype(BF)


def slot_ranks(owners, devices):
    count = owners.shape[0]
    chunks = -(-count // 128)
    padded = jnp.pad(owners, (0, chunks * 128 - count), constant_values=-1).reshape(chunks, 128)
    match = (
        padded[None] == jnp.arange(devices, dtype=jnp.int32)[:, None, None]
    ).astype(BF)
    within = jnp.einsum("ocl,lm->ocm", match, before(128), preferred_element_type=F32)
    totals = jnp.sum(match.astype(F32), axis=2)
    base = product(totals.astype(BF), before(chunks))
    ranks = jnp.sum(match.astype(F32) * (within + base[:, :, None]), axis=0)
    return ranks.reshape(-1)[:count].astype(jnp.int32)


def round_up(value, unit):
    return int(-(-value // unit) * unit)


class Route:
    def __init__(self, owners, slots, group, seq, tok, capacity):
        devices = seq * tok
        count = owners.shape[0]
        self.seq, self.tok, self.capacity, self.group = seq, tok, capacity, group
        owner = sharded(owners, tok, group, -1)
        slot = sharded(slots, tok, group, 0)
        size = owner.shape[1]
        self.size = size
        mean = capacity * size / count
        self.pair_cap = round_up(mean + 4.2 * math.sqrt(mean) + 1, 8)
        share = min(1.0, ((tok - 1) * count / devices + capacity) / count)
        mean = size * share
        self.row_cap = min(round_up(mean + 3.7 * math.sqrt(mean * (1 - share)), 8), round_up(size, 8))
        match = (owner[None] == jnp.arange(devices, dtype=jnp.int32)[:, None, None]).astype(BF)
        earlier = jnp.einsum("otl,lm->otm", match, before(size), preferred_element_type=F32)
        pair_rank = jnp.sum(match.astype(F32) * earlier, axis=0).astype(jnp.int32)
        owner_seq = jnp.where(owner >= 0, owner // tok, -1)
        earlier_seq = jnp.sum(earlier.reshape(seq, tok, tok, size), axis=1)
        match_seq = owner_seq[None] == jnp.arange(seq, dtype=jnp.int32)[:, None, None]
        row_rank = jnp.sum(jnp.where(match_seq, earlier_seq, 0.0), axis=0).astype(jnp.int32)
        self.fits = (jnp.max(pair_rank) < self.pair_cap) & (jnp.max(row_rank) < self.row_cap)
        me_seq, me_tok = lax.axis_index("seq"), lax.axis_index("tok")
        me = me_seq * tok + me_tok
        shard = jnp.arange(tok, dtype=jnp.int32)[:, None]
        place = jnp.where(pair_rank < self.pair_cap, shard * self.pair_cap + pair_rank, -1)
        self.own_slot = jnp.where(owner == me, slot, -1)
        self.has_gains = (owners[0] == me) & (jnp.arange(capacity, dtype=jnp.int32) == 0)
        once = 1 if group == 0 else 0
        own_slot = self.own_slot[:, once:].reshape(-1)
        hit = own_slot[None, :] == jnp.arange(capacity, dtype=jnp.int32)[:, None]
        target = (
            jnp.sum(jnp.where(hit, place[:, once:].reshape(-1)[None, :] + 1, 0), axis=1) - 1
        )
        columns = jnp.arange(tok * self.pair_cap, dtype=jnp.int32)[None, :]
        send = target[:, None] == columns
        if once:
            send = send | (self.has_gains[:, None] & (columns % self.pair_cap == 0))
        self.send = send.astype(BF)
        my_owner = lax.dynamic_index_in_dim(owner, me_tok, 0, keepdims=False)
        my_seq = lax.dynamic_index_in_dim(owner_seq, me_tok, 0, keepdims=False)
        my_pair = lax.dynamic_index_in_dim(pair_rank, me_tok, 0, keepdims=False)
        my_row = lax.dynamic_index_in_dim(row_rank, me_tok, 0, keepdims=False)
        arrive = jnp.where(
            (my_pair < self.pair_cap) & (my_owner >= 0),
            (my_owner % tok) * self.pair_cap + my_pair,
            -1,
        )
        from_pairs = onehot(arrive, tok * self.pair_cap)
        to_rows = onehot(jnp.where(my_seq == me_seq, my_row, -1), self.row_cap)
        self.compact = left_product(to_rows, from_pairs).astype(BF)
        self.place = onehot(
            jnp.where(
                (my_row < self.row_cap) & (my_owner >= 0),
                my_seq * self.row_cap + my_row,
                -1,
            ),
            seq * self.row_cap,
        )

    def fetch(self, rounded):
        packed = left_product(self.send, rounded).astype(BF)
        packed = exchange(packed)
        rows = product(self.compact, packed).astype(BF)
        rows = lax.all_gather(rows, "seq", axis=0, tiled=True)
        return product(self.place, rows).astype(BF)

    def fetch_any(self, rounded):
        width = rounded.shape[1]
        own = self.own_slot.reshape(-1)
        mine = jnp.where(
            (own >= 0)[:, None], jnp.take(rounded, jnp.maximum(own, 0), axis=0), 0
        ).astype(BF)
        mine = lax.all_to_all(mine.reshape(self.tok, self.size, width), "tok", 0, 0, tiled=True)
        mine = jnp.sum(mine, axis=0)
        total = mine
        for _ in range(self.seq - 1):
            mine = rotate(mine, self.seq)
            total = total + mine
        return total

    def give(self, grads):
        rows = left_product(self.place, grads).astype(BF)
        rows = lax.psum_scatter(rows, "seq", scatter_dimension=0, tiled=True)
        packed = left_product(self.compact, rows).astype(BF)
        packed = exchange(packed)
        return product(self.send, packed)

    def give_any(self, grads):
        width = grads.shape[1]
        total = grads.astype(F32)
        passing = grads
        for _ in range(self.seq - 1):
            passing = rotate(passing, self.seq)
            total = total + passing.astype(F32)
        every = jnp.broadcast_to(total.astype(BF)[None], (self.tok, self.size, width))
        every = lax.all_to_all(every, "tok", 0, 0, tiled=True)
        once = 1 if self.group == 0 else 0
        own = self.own_slot[:, once:].reshape(-1)
        hit = own[None, :] == jnp.arange(self.capacity, dtype=jnp.int32)[:, None]
        index = jnp.sum(
            jnp.where(hit, jnp.arange(1, own.shape[0] + 1, dtype=jnp.int32)[None, :], 0), axis=1
        )
        taken = jnp.take(
            every[:, once:].reshape(-1, width), jnp.maximum(index - 1, 0), axis=0
        ).astype(F32)
        taken = jnp.where((index > 0)[:, None], taken, 0.0)
        if once:
            gains = jnp.sum(every[:, 0].astype(F32), axis=0)
            taken = jnp.where(self.has_gains[:, None], gains[None, :], taken)
        return taken


def rates_for(kinds, seq_len):
    out_std = 1.0 / math.sqrt(max(1, D * 16 // seq_len))
    matrix_rate = 3.0 / math.sqrt(D)
    rate_list = [
        1.0,
        matrix_rate,
        matrix_rate,
        matrix_rate,
        3.0 * out_std,
        matrix_rate,
        matrix_rate,
        3.0 / math.sqrt(FF),
        0.0,
    ]
    decay_list = [0.0] + [DECAY_RATE] * 7 + [0.0]
    chosen = (kinds[:, None] == jnp.arange(9, dtype=jnp.int32)[None, :]).astype(F32)
    rate_values = jnp.sum(chosen * jnp.array(rate_list, F32)[None, :], axis=1)
    decay_values = jnp.sum(chosen * jnp.array(decay_list, F32)[None, :], axis=1)
    return (rate_values, decay_values)


def adam_update(grads, moment_one, moment_two, weights, rate_values, decay_values):
    first = BETA_ONE * moment_one + (1.0 - BETA_ONE) * grads
    second = BETA_TWO * moment_two + (1.0 - BETA_TWO) * grads * grads
    first_hat = first / (1.0 - BETA_ONE**STEP)
    second_hat = second / (1.0 - BETA_TWO**STEP)
    updated = weights - rate_values[:, None] * (
        first_hat / (jnp.sqrt(second_hat) + ADAM_EPSILON) + decay_values[:, None] * weights
    )
    return (first, second, updated)


def columns_out(rows, split):
    return rows.reshape(rows.shape[0], split, -1).transpose(1, 0, 2)


def step(tokens, cotangent, owners, master, first_moment, second_moment):
    seq = lax.axis_size("seq")
    tok = lax.axis_size("tok")
    capacity = master.shape[0]
    me = lax.axis_index("seq") * tok + lax.axis_index("tok")
    slots = slot_ranks(owners, seq * tok)
    routes = [Route(owners, slots, group, seq, tok, capacity) for group in range(2)]
    rounded = master.astype(BF)
    found = layer(tokens, cotangent, rounded, [(r.fetch, r.give) for r in routes])

    def any_owners(tokens, cotangent, rounded, *found):
        return layer(tokens, cotangent, rounded, [(r.fetch_any, r.give_any) for r in routes])

    result, grad_input, reduced = lax.cond(
        routes[0].fits & routes[1].fits,
        lambda tokens, cotangent, rounded, *found: found,
        any_owners,
        tokens,
        cotangent,
        rounded,
        *found,
    )
    mine = (owners == me)[None, :]
    numbers = jnp.arange(owners.shape[0], dtype=jnp.int32)[None, :]
    counts = jnp.sum(
        (mine & (numbers < jnp.array(LIMITS, jnp.int32)[:, None])).astype(jnp.int32), axis=1
    )
    kinds = jnp.sum(
        (jnp.arange(capacity, dtype=jnp.int32)[:, None] >= counts[None, :]).astype(jnp.int32), axis=1
    )
    rate_values, decay_values = rates_for(kinds, tokens.shape[1] * tok)
    first, second, updated = adam_update(
        reduced, first_moment, second_moment, master, rate_values, decay_values
    )
    return (result[None], grad_input[None], reduced, first, second, updated)


def layer(tokens, cotangent, rounded, routes):
    tok = lax.axis_size("tok")
    me_tok = lax.axis_index("tok")
    row_count = tokens.shape[1]
    seq_len = row_count * tok
    value_split = max(1, tok // HEADS)
    units = max(1, HEADS // tok)
    unit_width = DV // value_split
    slice_rows = D // tok
    ff_slice = ff_share(tok)
    qk_width = units * FD
    v_width = units * unit_width

    both = gather_rows(jnp.concatenate([tokens, cotangent]), tok)
    x_all, c_all = both[0].reshape(seq_len, D), both[1].reshape(seq_len, D)

    shard = routes[0][0](rounded)
    gain_one = shard[0, :D].astype(F32)
    gain_two = shard[0, D:].astype(F32)
    shard = shard[1:]
    a, b, c, _ = (MATRIX_BLOCKS[k] // tok for k in GROUPS[0])

    def spread(columns):
        wide = columns.reshape(slice_rows, tok // value_split, 1, qk_width)
        return jnp.broadcast_to(
            wide, (slice_rows, tok // value_split, value_split, qk_width)
        ).reshape(slice_rows, tok, qk_width)

    sent = jnp.concatenate(
        [
            spread(shard[:a].reshape(slice_rows, HEADS * FD)),
            spread(shard[a : a + b].reshape(slice_rows, HEADS * FD)),
            shard[a + b : a + b + c].reshape(slice_rows, tok, v_width),
        ],
        axis=-1,
    ).transpose(1, 0, 2)
    w_qkv = exchange(sent).reshape(D, -1)
    w_out = shard[a + b + c :].reshape(v_width, D)

    def padded(blocks):
        return jnp.pad(blocks.reshape(slice_rows, FF), ((0, 0), (0, tok * ff_slice - FF)))

    shard = routes[1][0](rounded)
    a = MATRIX_BLOCKS[4] // tok
    sent = jnp.concatenate(
        [
            columns_out(padded(shard[:a]), tok),
            columns_out(padded(shard[a : 2 * a]), tok),
        ],
        axis=-1,
    )
    w_gate_up = exchange(sent).reshape(D, -1)
    w_down = shard[2 * a :].reshape(ff_slice, D)

    normed_all, _ = normalize(x_all.astype(F32))
    hidden_one = (normed_all * gain_one).astype(BF)
    qkv = product(hidden_one, w_qkv).astype(BF)
    query = qkv[:, :qk_width].reshape(seq_len, units, FD).transpose(1, 0, 2)
    keys = qkv[:, qk_width : 2 * qk_width].reshape(seq_len, units, FD).transpose(1, 0, 2)
    values = qkv[:, 2 * qk_width :].reshape(seq_len, units, unit_width).transpose(1, 0, 2)
    place = jnp.arange(tok, dtype=jnp.int32)
    if tok == 8:
        place = place ^ me_tok
    index = (place[:, None] * row_count + jnp.arange(row_count, dtype=jnp.int32)[None, :]).reshape(-1)
    causal = (index[:, None] >= index[None, :])[None]
    inner = jnp.einsum("uif,ujf->uij", query, keys, preferred_element_type=F32) * (
        1.0 / math.sqrt(FD)
    )
    weight = jnp.where(causal, 1.0 + inner + 0.5 * inner * inner, 0.0)
    total = jnp.sum(weight, axis=2, keepdims=True)
    mixed_f = (
        jnp.einsum("uij,ujw->uiw", weight.astype(BF), values, preferred_element_type=F32) / total
    )
    mixed = mixed_f.astype(BF).transpose(1, 0, 2).reshape(seq_len, v_width)
    out = scatter_sum(product(mixed, w_out).reshape(1, tok, row_count, D), tok)[0]

    input_rows = tokens[0].astype(F32)
    middle = input_rows + out
    normed_two, scale_two = normalize(middle)
    hidden_two = gather_rows((normed_two * gain_two).astype(BF)[None], tok).reshape(seq_len, D)

    gate_up = product(hidden_two, w_gate_up)
    gate, up_proj = gate_up[:, :ff_slice], gate_up[:, ff_slice:]
    sigmoid = jax.nn.sigmoid(gate)
    activated = gate * sigmoid
    hidden = (activated * up_proj).astype(BF)
    grad_hidden = right_product(c_all, w_down)
    grad_gate = (grad_hidden * up_proj * sigmoid * (1.0 + gate * (1.0 - sigmoid))).astype(BF)
    grad_up = (grad_hidden * activated).astype(BF)
    grad_gate_up = jnp.concatenate([grad_gate, grad_up], axis=1)
    grad_two_terms = right_product(grad_gate_up, w_gate_up)
    grad_hidden_two = scatter_sum(grad_two_terms.reshape(1, tok, row_count, D), tok)[0]
    result_terms = product(hidden, w_down)

    grad_gain_two = jnp.sum(grad_hidden_two * normed_two, axis=0)
    grad_middle = cotangent[0].astype(F32) + norm_back(
        grad_hidden_two * gain_two, normed_two, scale_two
    )
    grad_mixer = gather_rows(grad_middle.astype(BF)[None], tok).reshape(seq_len, D)

    grad_w_down = left_product(hidden, c_all).astype(BF)
    grad_w_gate_up = left_product(hidden_two, grad_gate_up).astype(BF)
    back = exchange(grad_w_gate_up.reshape(tok, slice_rows, 2 * ff_slice))

    def flat(columns):
        rows = columns.transpose(1, 0, 2).reshape(slice_rows, tok * ff_slice)
        return rows[:, :FF].reshape(-1, BLK)

    back_gate, back_up = flat(back[..., :ff_slice]), flat(back[..., ff_slice:])
    reduced = routes[1][1](
        jnp.concatenate([back_gate, back_up, grad_w_down.reshape(-1, BLK)], axis=0)
    )

    grad_w_out = left_product(mixed, grad_mixer).astype(BF)
    grad_mixed = right_product(grad_mixer, w_out).astype(BF)
    grad_units = grad_mixed.reshape(seq_len, units, unit_width).transpose(1, 0, 2).astype(F32)
    grad_numer = (grad_units / total).astype(BF)
    grad_denom = -jnp.sum(grad_units * mixed_f, axis=-1, keepdims=True) / total
    grad_weight = (
        jnp.einsum("uiw,ujw->uij", grad_numer, values, preferred_element_type=F32) + grad_denom
    )
    grad_inner = (
        jnp.where(causal, grad_weight * (1.0 + inner), 0.0) * (1.0 / math.sqrt(FD))
    ).astype(BF)
    grad_query = jnp.einsum("uij,ujf->iuf", grad_inner, keys, preferred_element_type=F32)
    grad_keys = jnp.einsum("uij,uif->juf", grad_inner, query, preferred_element_type=F32)
    grad_values = jnp.einsum(
        "uij,uiw->juw", weight.astype(BF), grad_numer, preferred_element_type=F32
    )
    grad_qkv = jnp.concatenate(
        [
            grad_query.reshape(seq_len, -1),
            grad_keys.reshape(seq_len, -1),
            grad_values.reshape(seq_len, -1),
        ],
        axis=1,
    ).astype(BF)
    grad_w_qkv = left_product(hidden_one, grad_qkv).astype(BF)
    grad_one_terms = right_product(grad_qkv, w_qkv)
    terms = jnp.stack([result_terms, grad_one_terms]).reshape(2, tok, row_count, D)
    out_sum, grad_hidden_one = scatter_sum(terms, tok)
    result = (middle + out_sum).astype(BF)
    grad_gains = jnp.concatenate([jnp.sum(grad_one_terms * normed_all, axis=0), grad_gain_two])
    back = exchange(grad_w_qkv.reshape(tok, slice_rows, -1)).transpose(1, 0, 2)

    def gathered(columns):
        if value_split > 1:
            columns = jnp.sum(
                columns.reshape(slice_rows, tok // value_split, value_split, -1).astype(F32), axis=2
            ).astype(BF)
        return columns.reshape(-1, BLK)

    reduced = reduced + routes[0][1](
        jnp.concatenate(
            [
                grad_gains.astype(BF).reshape(1, BLK),
                gathered(back[..., :qk_width]),
                gathered(back[..., qk_width : 2 * qk_width]),
                back[..., 2 * qk_width :].reshape(-1, BLK),
                grad_w_out.reshape(-1, BLK),
            ],
            axis=0,
        )
    )

    normed_one, scale_one = normalize(input_rows)
    grad_input = grad_middle + norm_back(grad_hidden_one * gain_one, normed_one, scale_one)
    return result, grad_input.astype(BF), reduced


def solution(mesh):
    in_specs = (
        P("seq", "tok", None),
        P("seq", "tok", None),
        P(),
        P(("seq", "tok"), None),
        P(("seq", "tok"), None),
        P(("seq", "tok"), None),
    )
    out_specs = (
        P("seq", "tok", None),
        P("seq", "tok", None),
        P(("seq", "tok"), None),
        P(("seq", "tok"), None),
        P(("seq", "tok"), None),
        P(("seq", "tok"), None),
    )
    return jax.shard_map(step, mesh=mesh, in_specs=in_specs, out_specs=out_specs, check_vma=False)
```

```python
import math

import jax
import jax.numpy as jnp
from jax import lax
from jax.experimental import pallas as pl
from jax.experimental.pallas import tpu as pltpu
from jax.sharding import PartitionSpec as P


D = 1024
HEADS = 16
FD = 16
DV = 64
FF = 2752
STEP = 10
BLK = 2048

NORM_EPSILON = 1e-05
ADAM_EPSILON = 1e-08
BETA_ONE = 0.9
BETA_TWO = 0.95
DECAY_RATE = 0.1
BF = jnp.bfloat16
F32 = jnp.float32


MATRIX_BLOCKS = [
    D * HEADS * FD // BLK,
    D * HEADS * FD // BLK,
    D * HEADS * DV // BLK,
    HEADS * DV * D // BLK,
    D * FF // BLK,
    D * FF // BLK,
    FF * D // BLK,
]
MATRIX_STARTS = [1 + sum(MATRIX_BLOCKS[:k]) for k in range(len(MATRIX_BLOCKS))]
LIMITS = [1] + [MATRIX_STARTS[k] + MATRIX_BLOCKS[k] for k in range(len(MATRIX_BLOCKS))]
GROUPS = [(0, 1, 2, 3), (4, 5, 6)]


def product(left, right):
    return jnp.dot(left, right, preferred_element_type=F32)


def left_product(left, right):
    return lax.dot_general(left, right, (((0,), (0,)), ((), ())), preferred_element_type=F32)


def right_product(left, right):
    return lax.dot_general(left, right, (((1,), (1,)), ((), ())), preferred_element_type=F32)


def normalize(values):
    scale = lax.rsqrt(jnp.mean(values * values, axis=-1, keepdims=True) + NORM_EPSILON)
    return (values * scale, scale)


def norm_back(grad_hat, normed_rows, scale):
    return scale * (
        grad_hat - normed_rows * jnp.mean(grad_hat * normed_rows, axis=-1, keepdims=True)
    )


def swap(values, mask):
    return lax.ppermute(values, "tok", [(i, i ^ mask) for i in range(8)])


def exchange(values):
    return lax.all_to_all(values, "tok", 0, 0, tiled=True)


def gather_rows(rows):
    return lax.all_gather(rows, "tok", axis=0, tiled=True)


def scatter_sum(parts, tok):
    sent = parts.astype(BF).reshape(tok, -1, parts.shape[1])
    return jnp.sum(exchange(sent).astype(F32), axis=0)


def gather_of_eight(rows):
    count, height, width = rows.shape
    half = width // 2
    a, b = rows[:, :, :half], rows[:, :, half:]
    ax, by = swap(a, 2), swap(b, 4)
    a2, b2 = jnp.stack([a, ax], 1), jnp.stack([b, by], 1)
    ay, bx = swap(a2, 4), swap(b2, 2)
    first = jnp.concatenate([a2, ay], 1)
    second = jnp.stack([b, bx[:, 0], by, bx[:, 1]], 1)
    near = jnp.concatenate([first, second], -1).reshape(count, 4 * height, width)
    return near, swap(near, 1)


def scatter_of_eight(keep, send):
    many, height, width = keep.shape
    half = width // 2
    mine = keep.astype(F32) + swap(send, 1).astype(F32)
    mine = mine.reshape(many, 4, height // 4, width)
    a, b = mine[..., :half], mine[..., half:]
    got_a = swap(a[:, 2:].astype(BF), 4)
    got_b = swap(jnp.stack([b[:, 1], b[:, 3]], 1).astype(BF), 2)
    a = a[:, :2] + got_a.astype(F32)
    b = jnp.stack([b[:, 0], b[:, 2]], 1) + got_b.astype(F32)
    got_a = swap(a[:, 1].astype(BF), 2)
    got_b = swap(b[:, 1].astype(BF), 4)
    return jnp.concatenate([a[:, 0] + got_a.astype(F32), b[:, 0] + got_b.astype(F32)], -1)


def ff_share(tok):
    return round_up(FF / tok, 128)


def sharded(per_block, tok, group, fill):
    pieces = []
    if group == 0:
        first = jnp.broadcast_to(per_block[:1][None], (tok, 1))
        pieces.append(jnp.pad(first, ((0, 0), (0, 7)), constant_values=fill))
    for k in GROUPS[group]:
        piece = lax.slice_in_dim(per_block, MATRIX_STARTS[k], MATRIX_STARTS[k] + MATRIX_BLOCKS[k])
        if k == 6:
            missing = tok * ff_share(tok) * D // BLK - MATRIX_BLOCKS[k]
            piece = jnp.pad(piece, (0, missing), constant_values=fill)
        piece = piece.reshape(tok, -1)
        missing = -piece.shape[1] % 8
        pieces.append(jnp.pad(piece, ((0, 0), (0, missing)), constant_values=fill))
    return jnp.concatenate(pieces, axis=1)


def piece_of(shard, tok, group, k):
    offset = 0
    for other in (-1,) * (group == 0) + GROUPS[group]:
        if other == -1:
            count = 1
        elif other == 6:
            count = ff_share(tok) * D // BLK
        else:
            count = MATRIX_BLOCKS[other] // tok
        if other == k:
            return shard[offset : offset + count]
        offset += round_up(count, 8)


def joined(pieces):
    return jnp.concatenate([jnp.pad(p, ((0, -p.shape[0] % 8), (0, 0))) for p in pieces], axis=0)


def rotate(values, count):
    return lax.ppermute(values, "seq", [(i, (i + 1) % count) for i in range(count)])


def onehot(index, size):
    return (index[:, None] == jnp.arange(size, dtype=jnp.int32)[None, :]).astype(BF)


def before(size):
    rows = jnp.arange(size, dtype=jnp.int32)
    return (rows[:, None] < rows[None, :]).astype(BF)


def slot_ranks(owners, devices):
    count = owners.shape[0]
    chunks = -(-count // 128)
    padded = jnp.pad(owners, (0, chunks * 128 - count), constant_values=-1).reshape(chunks, 128)
    match = (
        padded[None] == jnp.arange(devices, dtype=jnp.int32)[:, None, None]
    ).astype(BF)
    within = jnp.einsum("ocl,lm->ocm", match, before(128), preferred_element_type=F32)
    totals = jnp.sum(match.astype(F32), axis=2)
    base = product(totals.astype(BF), before(chunks))
    ranks = jnp.sum(match.astype(F32) * (within + base[:, :, None]), axis=0)
    return ranks.reshape(-1)[:count].astype(jnp.int32)


def round_up(value, unit):
    return int(-(-value // unit) * unit)


class Route:
    def __init__(self, owners, slots, group, seq, tok, capacity):
        devices = seq * tok
        count = owners.shape[0]
        self.seq, self.tok, self.capacity, self.group = seq, tok, capacity, group
        owner = sharded(owners, tok, group, -1)
        slot = sharded(slots, tok, group, 0)
        size = owner.shape[1]
        self.size = size
        mean = capacity * size / count
        self.pair_cap = round_up(mean + 4.2 * math.sqrt(mean) + 1, 8)
        share = min(1.0, ((tok - 1) * count / devices + capacity) / count)
        mean = size * share
        self.row_cap = min(round_up(mean + 3.7 * math.sqrt(mean * (1 - share)), 8), round_up(size, 8))
        match = (owner[None] == jnp.arange(devices, dtype=jnp.int32)[:, None, None]).astype(BF)
        earlier = jnp.einsum("otl,lm->otm", match, before(size), preferred_element_type=F32)
        pair_rank = jnp.sum(match.astype(F32) * earlier, axis=0).astype(jnp.int32)
        owner_seq = jnp.where(owner >= 0, owner // tok, -1)
        earlier_seq = jnp.sum(earlier.reshape(seq, tok, tok, size), axis=1)
        match_seq = owner_seq[None] == jnp.arange(seq, dtype=jnp.int32)[:, None, None]
        row_rank = jnp.sum(jnp.where(match_seq, earlier_seq, 0.0), axis=0).astype(jnp.int32)
        self.fits = (jnp.max(pair_rank) < self.pair_cap) & (jnp.max(row_rank) < self.row_cap)
        me_seq, me_tok = lax.axis_index("seq"), lax.axis_index("tok")
        me = me_seq * tok + me_tok
        shard = jnp.arange(tok, dtype=jnp.int32)[:, None]
        place = jnp.where(pair_rank < self.pair_cap, shard * self.pair_cap + pair_rank, -1)
        self.own_slot = jnp.where(owner == me, slot, -1)
        self.has_gains = (owners[0] == me) & (jnp.arange(capacity, dtype=jnp.int32) == 0)
        once = 1 if group == 0 else 0
        own_slot = self.own_slot[:, once:].reshape(-1)
        hit = own_slot[None, :] == jnp.arange(capacity, dtype=jnp.int32)[:, None]
        target = (
            jnp.sum(jnp.where(hit, place[:, once:].reshape(-1)[None, :] + 1, 0), axis=1) - 1
        )
        columns = jnp.arange(tok * self.pair_cap, dtype=jnp.int32)[None, :]
        send = target[:, None] == columns
        if once:
            send = send | (self.has_gains[:, None] & (columns % self.pair_cap == 0))
        self.send = send.astype(BF)
        my_owner = lax.dynamic_index_in_dim(owner, me_tok, 0, keepdims=False)
        my_seq = lax.dynamic_index_in_dim(owner_seq, me_tok, 0, keepdims=False)
        my_pair = lax.dynamic_index_in_dim(pair_rank, me_tok, 0, keepdims=False)
        my_row = lax.dynamic_index_in_dim(row_rank, me_tok, 0, keepdims=False)
        arrive = jnp.where(
            (my_pair < self.pair_cap) & (my_owner >= 0),
            (my_owner % tok) * self.pair_cap + my_pair,
            -1,
        )
        from_pairs = onehot(arrive, tok * self.pair_cap)
        to_rows = onehot(jnp.where(my_seq == me_seq, my_row, -1), self.row_cap)
        self.compact = left_product(to_rows, from_pairs).astype(BF)
        my_place = jnp.where(
            (my_row < self.row_cap) & (my_owner >= 0), my_seq * self.row_cap + my_row, -1
        )
        self.place = onehot(my_place, seq * self.row_cap)
        self.place_back = (
            jnp.arange(seq * self.row_cap, dtype=jnp.int32)[:, None] == my_place[None, :]
        ).astype(BF)

    def fetch(self, rounded):
        packed = left_product(self.send, rounded).astype(BF)
        packed = exchange(packed)
        rows = product(self.compact, packed).astype(BF)
        rows = lax.all_gather(rows, "seq", axis=0, tiled=True)
        return self.place, rows

    def fetch_any(self, rounded):
        width = rounded.shape[1]
        own = self.own_slot.reshape(-1)
        mine = jnp.where(
            (own >= 0)[:, None], jnp.take(rounded, jnp.maximum(own, 0), axis=0), 0
        ).astype(BF)
        mine = lax.all_to_all(mine.reshape(self.tok, self.size, width), "tok", 0, 0, tiled=True)
        mine = jnp.sum(mine, axis=0)
        total = mine
        for _ in range(self.seq - 1):
            mine = rotate(mine, self.seq)
            total = total + mine
        return jnp.eye(self.size, dtype=BF), total

    def give(self, rows):
        rows = lax.psum_scatter(rows, "seq", scatter_dimension=0, tiled=True)
        packed = left_product(self.compact, rows).astype(BF)
        packed = exchange(packed)
        return product(self.send, packed)

    def give_any(self, rows):
        width = rows.shape[1]
        total = rows.astype(F32)
        passing = rows
        for _ in range(self.seq - 1):
            passing = rotate(passing, self.seq)
            total = total + passing.astype(F32)
        every = jnp.broadcast_to(total.astype(BF)[None], (self.tok, self.size, width))
        every = lax.all_to_all(every, "tok", 0, 0, tiled=True)
        once = 1 if self.group == 0 else 0
        own = self.own_slot[:, once:].reshape(-1)
        hit = own[None, :] == jnp.arange(self.capacity, dtype=jnp.int32)[:, None]
        index = jnp.sum(
            jnp.where(hit, jnp.arange(1, own.shape[0] + 1, dtype=jnp.int32)[None, :], 0), axis=1
        )
        taken = jnp.take(
            every[:, once:].reshape(-1, width), jnp.maximum(index - 1, 0), axis=0
        ).astype(F32)
        taken = jnp.where((index > 0)[:, None], taken, 0.0)
        if once:
            gains = jnp.sum(every[:, 0].astype(F32), axis=0)
            taken = jnp.where(self.has_gains[:, None], gains[None, :], taken)
        return taken


def rates_for(kinds, seq_len):
    out_std = 1.0 / math.sqrt(max(1, D * 16 // seq_len))
    matrix_rate = 3.0 / math.sqrt(D)
    rate_list = [
        1.0,
        matrix_rate,
        matrix_rate,
        matrix_rate,
        3.0 * out_std,
        matrix_rate,
        matrix_rate,
        3.0 / math.sqrt(FF),
        0.0,
    ]
    decay_list = [0.0] + [DECAY_RATE] * 7 + [0.0]
    chosen = (kinds[:, None] == jnp.arange(9, dtype=jnp.int32)[None, :]).astype(F32)
    rate_values = jnp.sum(chosen * jnp.array(rate_list, F32)[None, :], axis=1)
    decay_values = jnp.sum(chosen * jnp.array(decay_list, F32)[None, :], axis=1)
    return (rate_values, decay_values)


def adam_update(grads, moment_one, moment_two, weights, rate_values, decay_values):
    first = BETA_ONE * moment_one + (1.0 - BETA_ONE) * grads
    second = BETA_TWO * moment_two + (1.0 - BETA_TWO) * grads * grads
    first_hat = first / (1.0 - BETA_ONE**STEP)
    second_hat = second / (1.0 - BETA_TWO**STEP)
    updated = weights - rate_values[:, None] * (
        first_hat / (jnp.sqrt(second_hat) + ADAM_EPSILON) + decay_values[:, None] * weights
    )
    return (first, second, updated)


def columns_out(rows, split):
    return rows.reshape(rows.shape[0], split, -1).transpose(1, 0, 2)


def step(tokens, cotangent, owners, master, first_moment, second_moment):
    seq = lax.axis_size("seq")
    tok = lax.axis_size("tok")
    capacity = master.shape[0]
    me = lax.axis_index("seq") * tok + lax.axis_index("tok")
    slots = slot_ranks(owners, seq * tok)
    routes = [Route(owners, slots, group, seq, tok, capacity) for group in range(2)]
    rounded = master.astype(BF)
    layer = layer_of_eight if tok == 8 else layer_of_any
    found = layer(
        tokens, cotangent, rounded, [(r.fetch, r.place_back, r.give) for r in routes]
    )

    def any_owners(tokens, cotangent, rounded, *found):
        plain = [(r.fetch_any, jnp.eye(r.size, dtype=BF), r.give_any) for r in routes]
        return layer(tokens, cotangent, rounded, plain)

    result, grad_input, reduced = lax.cond(
        routes[0].fits & routes[1].fits,
        lambda tokens, cotangent, rounded, *found: found,
        any_owners,
        tokens,
        cotangent,
        rounded,
        *found,
    )
    mine = (owners == me)[None, :]
    numbers = jnp.arange(owners.shape[0], dtype=jnp.int32)[None, :]
    counts = jnp.sum(
        (mine & (numbers < jnp.array(LIMITS, jnp.int32)[:, None])).astype(jnp.int32), axis=1
    )
    kinds = jnp.sum(
        (jnp.arange(capacity, dtype=jnp.int32)[:, None] >= counts[None, :]).astype(jnp.int32), axis=1
    )
    rate_values, decay_values = rates_for(kinds, tokens.shape[1] * tok)
    first, second, updated = adam_update(
        reduced, first_moment, second_moment, master, rate_values, decay_values
    )
    return (result[None], grad_input[None], reduced, first, second, updated)


def call(kernel, outs, scratch=(), scalars=0, operands=0, flops=0, nbytes=0):
    return pl.pallas_call(
        kernel,
        out_shape=[jax.ShapeDtypeStruct(shape, kind) for shape, kind in outs],
        in_specs=[pl.BlockSpec(memory_space=pltpu.SMEM)] * scalars
        + [pl.BlockSpec(memory_space=pltpu.VMEM)] * (operands - scalars),
        scratch_shapes=[pltpu.VMEM(shape, kind) for shape, kind in scratch],
        compiler_params=pltpu.CompilerParams(vmem_limit_bytes=60 * 1024 * 1024),
        cost_estimate=pl.CostEstimate(flops=flops, bytes_accessed=nbytes, transcendentals=0),
    )


def dot(left, right):
    return jnp.dot(left, right, preferred_element_type=F32)


def low_lanes(shape):
    return lax.broadcasted_iota(jnp.int32, shape, 1) < 64


def unpack_ff(place_ref, rows_ref, sent_ref, down_ref, flat, wide, tall):
    for c in range(16):
        lanes = pl.ds(128 * c, 128)
        found = dot(place_ref[...], rows_ref[:, lanes])
        flat[0, pl.ds(c, 176, stride=16), :] = found[:176]
        flat[1, pl.ds(c, 176, stride=16), :] = found[176:352]
        tall[c % 8, pl.ds(c // 8, 192, stride=2), :] = found[352:]
    for k in range(8):
        down_ref[:, pl.ds(128 * k, 128)] = tall[k].astype(BF)
    low = low_lanes((64, 128))
    zero = jnp.zeros((64, 128), F32)
    for m in range(2):
        for k in range(24):
            if k > 21:
                wide[k] = jnp.zeros((128, 128), F32)
                continue
            even = flat[m, pl.ds(k, 64, stride=43), :]
            first = flat[m, pl.ds(21 + k, 64, stride=43), :]
            second = flat[m, pl.ds(22 + k, 64, stride=43), :] if k < 21 else zero
            if k == 21:
                even = jnp.where(low, even, 0.0)
            odd = pltpu.roll(jnp.where(low, second, first), 64, 1)
            wide[k, pl.ds(0, 64, stride=2), :] = even
            wide[k, pl.ds(1, 64, stride=2), :] = odd
        for k in range(24):
            sent_ref[k // 3, :, pl.ds(384 * m + 128 * (k % 3), 128)] = wide[k].astype(BF)


def pack_ff(place_ref, back_ref, down_ref, rows_ref, flat, wide, tall):
    low = low_lanes((64, 128))
    for m in range(2):
        flat[m, pl.ds(2752, 64), :] = jnp.zeros((64, 128), F32)
        for k in range(22):
            wide[k] = back_ref[k // 3, :, pl.ds(384 * m + 128 * (k % 3), 128)].astype(F32)

        def turned(k):
            return pltpu.roll(wide[k, pl.ds(1, 64, stride=2), :], 64, 1)

        for k in range(21):
            flat[m, pl.ds(k, 64, stride=43), :] = wide[k, pl.ds(0, 64, stride=2), :]
        after = turned(0)
        flat[m, pl.ds(21, 64, stride=43), :] = jnp.where(
            low, wide[21, pl.ds(0, 64, stride=2), :], after
        )
        for k in range(21):
            current, after = after, turned(k + 1)
            flat[m, pl.ds(22 + k, 64, stride=43), :] = jnp.where(low, current, after)
    for k in range(8):
        tall[k] = down_ref[:, pl.ds(128 * k, 128)].astype(F32)
    for c in range(16):
        grads = jnp.concatenate(
            [
                flat[0, pl.ds(c, 176, stride=16), :],
                flat[1, pl.ds(c, 176, stride=16), :],
                tall[c % 8, pl.ds(c // 8, 192, stride=2), :],
            ],
            axis=0,
        ).astype(BF)
        rows_ref[:, pl.ds(128 * c, 128)] = dot(place_ref[...], grads).astype(BF)


def unpack_mix(place_ref, rows_ref, gains_ref, sent_ref, out_ref, thin, tall):
    for c in range(16):
        lanes = pl.ds(128 * c, 128)
        found = dot(place_ref[...], rows_ref[:, lanes])
        gains_ref[:, lanes] = found[:8]
        thin[c % 2, pl.ds(c // 2, 16, stride=8), :] = found[8:24]
        thin[2 + c % 2, pl.ds(c // 2, 16, stride=8), :] = found[24:40]
        tall[c % 8, pl.ds(c // 8, 64, stride=2), :] = found[40:104]
        tall[8 + c % 8, pl.ds(c // 8, 64, stride=2), :] = found[104:]
    lane = lax.broadcasted_iota(jnp.int32, (128, 128), 1)
    for t in range(8):
        sent_ref[t, :, pl.ds(0, 128)] = tall[t].astype(BF)
        query, keys = thin[t // 4], thin[2 + t // 4]
        if t % 4 != 0:
            query = pltpu.roll(query, 128 - 32 * (t % 4), 1)
        if t % 4 != 1:
            keys = pltpu.roll(keys, (160 - 32 * (t % 4)) % 128, 1)
        both = jnp.where(lane < 32, query, jnp.where(lane < 64, keys, 0.0))
        sent_ref[t, :, pl.ds(128, 128)] = both.astype(BF)
        out_ref[:, pl.ds(128 * t, 128)] = tall[8 + t].astype(BF)


def pack_mix(place_ref, gains_ref, back_ref, out_ref, rows_ref, thin, tall):
    lane = lax.broadcasted_iota(jnp.int32, (128, 128), 1)
    for j in range(2):
        query = jnp.zeros((128, 128), F32)
        keys = jnp.zeros((128, 128), F32)
        for u in range(4):
            both = back_ref[4 * j + u, :, pl.ds(128, 128)].astype(F32)
            here = (lane >= 32 * u) & (lane < 32 * u + 32)
            moved = pltpu.roll(both, 32 * u, 1) if u else both
            query = jnp.where(here, moved, query)
            moved = pltpu.roll(both, (96 + 32 * u) % 128, 1) if u != 1 else both
            keys = jnp.where(here, moved, keys)
        thin[j] = query
        thin[2 + j] = keys
    for t in range(8):
        tall[t] = back_ref[t, :, pl.ds(0, 128)].astype(F32)
        tall[8 + t] = out_ref[:, pl.ds(128 * t, 128)].astype(F32)
    for c in range(16):
        lanes = pl.ds(128 * c, 128)
        grads = jnp.concatenate(
            [
                gains_ref[:, lanes],
                thin[c % 2, pl.ds(c // 2, 16, stride=8), :],
                thin[2 + c % 2, pl.ds(c // 2, 16, stride=8), :],
                tall[c % 8, pl.ds(c // 8, 64, stride=2), :],
                tall[8 + c % 8, pl.ds(c // 8, 64, stride=2), :],
            ],
            axis=0,
        ).astype(BF)
        rows_ref[:, lanes] = dot(place_ref[...], grads).astype(BF)


ROWS = 256


def feed_forward(h0, h1, c0, c1, w_in, w_down, hidden_ref, grad_ref, keep, send, result_keep, result_send):
    for half, (h_ref, c_ref, out, result) in enumerate(
        ((h0, c0, keep, result_keep), (h1, c1, send, result_send))
    ):

        def block(i, carry, half=half, h_ref=h_ref, c_ref=c_ref, out=out, result=result):
            here = pl.ds(pl.multiple_of(i * ROWS, ROWS), ROWS)
            there = pl.ds(pl.multiple_of(i * ROWS + 512 * half, ROWS), ROWS)
            gate_up = dot(h_ref[0, here, :], w_in[...])
            gate, up = gate_up[:, :384], gate_up[:, 384:]
            sigmoid = jax.nn.sigmoid(gate)
            active = gate * sigmoid
            hidden = (active * up).astype(BF)
            hidden_ref[there, :] = hidden
            grad_hidden = right_product(c_ref[1, here, :], w_down[...])
            grad_gate = grad_hidden * up * sigmoid * (1.0 + gate * (1.0 - sigmoid))
            grads = jnp.concatenate([grad_gate, grad_hidden * active], axis=1).astype(BF)
            grad_ref[there, :] = grads
            out[0, here, :] = right_product(grads, w_in[...]).astype(BF)
            result[here, :] = dot(hidden, w_down[...]).astype(BF)
            return carry

        lax.fori_loop(0, 512 // ROWS, block, 0)


def token_at(index, me):
    group = index >> 7
    far = ((group & 3) << 1) | (group >> 2)
    return ((far ^ me) << 7) | (index & 127)


def pair_weights(query, keys, first, me):
    inner = right_product(query, keys) * (1.0 / math.sqrt(FD))
    row = lax.broadcasted_iota(jnp.int32, inner.shape, 0) + first
    column = lax.broadcasted_iota(jnp.int32, inner.shape, 1)
    causal = token_at(row, me) >= token_at(column, me)
    return inner, jnp.where(causal, 1.0 + inner + 0.5 * inner * inner, 0.0), causal


def mix(me_ref, x0, x1, gain, w_in, w_out, hidden_ref, qkv, mixed_ref, mean_ref, total_ref, keep, send):
    me = me_ref[0]
    for half, x_ref in enumerate((x0, x1)):

        def block(i, carry, half=half, x_ref=x_ref):
            here = pl.ds(pl.multiple_of(i * ROWS, ROWS), ROWS)
            there = pl.ds(pl.multiple_of(i * ROWS + 512 * half, ROWS), ROWS)
            x = x_ref[0, here, :].astype(F32)
            scale = lax.rsqrt(jnp.mean(x * x, axis=1, keepdims=True) + NORM_EPSILON)
            hidden = (x * scale * gain[0:1, :]).astype(BF)
            hidden_ref[there, :] = hidden
            qkv[there, :] = dot(hidden, w_in[...]).astype(BF)
            return carry

        lax.fori_loop(0, 512 // ROWS, block, 0)
    for half, out in enumerate((keep, send)):

        def block(i, carry, half=half, out=out):
            first = pl.multiple_of(i * ROWS + 512 * half, ROWS)
            there = pl.ds(first, ROWS)
            means, totals = [], []
            for u in range(2):
                query = qkv[there, pl.ds(128, 128)][:, 16 * u : 16 * u + 16]
                keys = qkv[:, pl.ds(128, 128)][:, 32 + 16 * u : 48 + 16 * u]
                values = qkv[:, pl.ds(0, 128)][:, 64 * u : 64 * u + 64]
                _, weight, _ = pair_weights(query, keys, first, me)
                total = jnp.sum(weight, axis=1, keepdims=True)
                means.append(dot(weight.astype(BF), values) / total)
                totals.append(jnp.broadcast_to(total, (ROWS, 64)))
            mean = jnp.concatenate(means, axis=1)
            mean_ref[there, :] = mean
            total_ref[there, :] = jnp.concatenate(totals, axis=1)
            mixed = mean.astype(BF)
            mixed_ref[there, :] = mixed
            here = pl.ds(pl.multiple_of(i * ROWS, ROWS), ROWS)
            out[0, here, :] = dot(mixed, w_out[...]).astype(BF)
            return carry

        lax.fori_loop(0, 512 // ROWS, block, 0)


def mix_back(
    me_ref, m0, m1, x0, x1, w_in, w_out, qkv, mixed_ref, mean_ref, total_ref, result_keep, result_send,
    grad_ref, keep, send, gain_ref, out_grad, numer, denom, back_keys, back_values, back_out,
):
    me = me_ref[0]
    keep[0] = result_keep[...]
    send[0] = result_send[...]
    back_out[...] = jnp.zeros_like(back_out)
    for half, m_ref in enumerate((m0, m1)):

        def block(i, carry, half=half, m_ref=m_ref):
            here = pl.ds(pl.multiple_of(i * ROWS, ROWS), ROWS)
            there = pl.ds(pl.multiple_of(i * ROWS + 512 * half, ROWS), ROWS)
            grad = right_product(m_ref[0, here, :], w_out[...]).astype(BF).astype(F32)
            back_out[...] += left_product(mixed_ref[there, :], m_ref[0, here, :])
            total = total_ref[there, :]
            numer[there, :] = (grad / total).astype(BF)
            lean = grad * mean_ref[there, :]
            sums = [jnp.sum(lean[:, 64 * u : 64 * u + 64], axis=1, keepdims=True) for u in range(2)]
            wide = jnp.concatenate([jnp.broadcast_to(s, (ROWS, 64)) for s in sums], axis=1)
            denom[there, :] = -wide / total
            return carry

        lax.fori_loop(0, 512 // ROWS, block, 0)
    out_grad[...] = back_out[...].astype(BF)
    back_keys[...] = jnp.zeros_like(back_keys)
    back_values[...] = jnp.zeros_like(back_values)

    def pairs(i, carry):
        first = pl.multiple_of(i * ROWS, ROWS)
        there = pl.ds(first, ROWS)
        query_grads = []
        for u in range(2):
            query = qkv[there, pl.ds(128, 128)][:, 16 * u : 16 * u + 16]
            keys = qkv[:, pl.ds(128, 128)][:, 32 + 16 * u : 48 + 16 * u]
            values = qkv[:, pl.ds(0, 128)][:, 64 * u : 64 * u + 64]
            inner, weight, causal = pair_weights(query, keys, first, me)
            down = numer[there, :][:, 64 * u : 64 * u + 64]
            grad_weight = right_product(down, values) + denom[there, :][:, 64 * u : 64 * u + 1]
            grad_inner = (
                jnp.where(causal, grad_weight * (1.0 + inner), 0.0) * (1.0 / math.sqrt(FD))
            ).astype(BF)
            query_grads.append(dot(grad_inner, keys))
            back_keys[u] += left_product(grad_inner, query)
            back_values[u] += left_product(weight.astype(BF), down)
        grad_ref[there, pl.ds(128, 128)] = jnp.concatenate(
            query_grads + [jnp.zeros((ROWS, 96), F32)], axis=1
        ).astype(BF)
        return carry

    lax.fori_loop(0, 1024 // ROWS, pairs, 0)
    gain_ref[...] = jnp.zeros_like(gain_ref)
    for half, (x_ref, out) in enumerate(((x0, keep), (x1, send))):

        def block(i, carry, half=half, x_ref=x_ref, out=out):
            here = pl.ds(pl.multiple_of(i * ROWS, ROWS), ROWS)
            there = pl.ds(pl.multiple_of(i * ROWS + 512 * half, ROWS), ROWS)
            query_grad = grad_ref[there, pl.ds(128, 128)][:, :32]
            keys_grad = [back_keys[u, there, :].astype(BF) for u in range(2)]
            values_grad = [back_values[u, there, :].astype(BF) for u in range(2)]
            grads = jnp.concatenate(
                values_grad + [query_grad] + keys_grad + [jnp.zeros((ROWS, 64), BF)], axis=1
            )
            grad_ref[there, :] = grads
            terms = right_product(grads, w_in[...])
            out[1, here, :] = terms.astype(BF)
            x = x_ref[0, here, :].astype(F32)
            scale = lax.rsqrt(jnp.mean(x * x, axis=1, keepdims=True) + NORM_EPSILON)
            gain_ref[0:1, :] += jnp.sum(terms * (x * scale), axis=0, keepdims=True)
            return carry

        lax.fori_loop(0, 512 // ROWS, block, 0)


def layer_of_any(tokens, cotangent, rounded, routes):
    tok = lax.axis_size("tok")
    row_count = tokens.shape[1]
    seq_len = row_count * tok
    value_split = max(1, tok // HEADS)
    units = max(1, HEADS // tok)
    unit_width = DV // value_split
    slice_rows = D // tok
    ff_slice = ff_share(tok)
    qk_width = units * FD
    v_width = units * unit_width

    x_all, c_all = gather_rows(tokens[0]), gather_rows(cotangent[0])

    place, rows = routes[0][0](rounded)
    shard = product(place, rows).astype(BF)
    gain_one = shard[0, :D].astype(F32)
    gain_two = shard[0, D:].astype(F32)

    def spread(columns):
        wide = columns.reshape(slice_rows, tok // value_split, 1, qk_width)
        return jnp.broadcast_to(
            wide, (slice_rows, tok // value_split, value_split, qk_width)
        ).reshape(slice_rows, tok, qk_width)

    sent = jnp.concatenate(
        [
            spread(piece_of(shard, tok, 0, 0).reshape(slice_rows, HEADS * FD)),
            spread(piece_of(shard, tok, 0, 1).reshape(slice_rows, HEADS * FD)),
            piece_of(shard, tok, 0, 2).reshape(slice_rows, tok, v_width),
        ],
        axis=-1,
    ).transpose(1, 0, 2)
    w_qkv = exchange(sent).reshape(D, -1)
    w_out = piece_of(shard, tok, 0, 3).reshape(v_width, D)

    def padded(blocks):
        return jnp.pad(blocks.reshape(slice_rows, FF), ((0, 0), (0, tok * ff_slice - FF)))

    place, rows = routes[1][0](rounded)
    shard = product(place, rows).astype(BF)
    sent = jnp.concatenate(
        [
            columns_out(padded(piece_of(shard, tok, 1, 4)), tok),
            columns_out(padded(piece_of(shard, tok, 1, 5)), tok),
        ],
        axis=-1,
    )
    w_gate_up = exchange(sent).reshape(D, -1)
    w_down = piece_of(shard, tok, 1, 6).reshape(ff_slice, D)

    normed_all, _ = normalize(x_all.astype(F32))
    hidden_one = (normed_all * gain_one).astype(BF)
    qkv = product(hidden_one, w_qkv).astype(BF)
    query = qkv[:, :qk_width].reshape(seq_len, units, FD).transpose(1, 0, 2)
    keys = qkv[:, qk_width : 2 * qk_width].reshape(seq_len, units, FD).transpose(1, 0, 2)
    values = qkv[:, 2 * qk_width :].reshape(seq_len, units, unit_width).transpose(1, 0, 2)
    index = jnp.arange(seq_len, dtype=jnp.int32)
    causal = (index[:, None] >= index[None, :])[None]
    inner = jnp.einsum("uif,ujf->uij", query, keys, preferred_element_type=F32) * (
        1.0 / math.sqrt(FD)
    )
    weight = jnp.where(causal, 1.0 + inner + 0.5 * inner * inner, 0.0)
    total = jnp.sum(weight, axis=2, keepdims=True)
    mixed_f = (
        jnp.einsum("uij,ujw->uiw", weight.astype(BF), values, preferred_element_type=F32) / total
    )
    mixed = mixed_f.astype(BF).transpose(1, 0, 2).reshape(seq_len, v_width)
    out = scatter_sum(product(mixed, w_out), tok)

    input_rows = tokens[0].astype(F32)
    middle = input_rows + out
    normed_two, scale_two = normalize(middle)
    hidden_two = gather_rows((normed_two * gain_two).astype(BF))

    gate_up = product(hidden_two, w_gate_up)
    gate, up_proj = gate_up[:, :ff_slice], gate_up[:, ff_slice:]
    sigmoid = jax.nn.sigmoid(gate)
    activated = gate * sigmoid
    hidden = (activated * up_proj).astype(BF)
    grad_hidden = right_product(c_all, w_down)
    grad_gate = (grad_hidden * up_proj * sigmoid * (1.0 + gate * (1.0 - sigmoid))).astype(BF)
    grad_up = (grad_hidden * activated).astype(BF)
    grad_gate_up = jnp.concatenate([grad_gate, grad_up], axis=1)
    grad_two_terms = right_product(grad_gate_up, w_gate_up)
    grad_hidden_two = scatter_sum(grad_two_terms, tok)
    result_terms = product(hidden, w_down)

    grad_gain_two = jnp.sum(grad_hidden_two * normed_two, axis=0)
    grad_middle = cotangent[0].astype(F32) + norm_back(
        grad_hidden_two * gain_two, normed_two, scale_two
    )
    grad_mixer = gather_rows(grad_middle.astype(BF))

    grad_w_down = left_product(hidden, c_all).astype(BF)
    grad_w_gate_up = left_product(hidden_two, grad_gate_up).astype(BF)
    back = exchange(grad_w_gate_up.reshape(tok, slice_rows, 2 * ff_slice))

    def flat(columns):
        rows = columns.transpose(1, 0, 2).reshape(slice_rows, tok * ff_slice)
        return rows[:, :FF].reshape(-1, BLK)

    back_gate, back_up = flat(back[..., :ff_slice]), flat(back[..., ff_slice:])
    blocks = joined([back_gate, back_up, grad_w_down.reshape(-1, BLK)])
    reduced = routes[1][2](product(routes[1][1], blocks).astype(BF))

    grad_w_out = left_product(mixed, grad_mixer).astype(BF)
    grad_mixed = right_product(grad_mixer, w_out).astype(BF)
    grad_units = grad_mixed.reshape(seq_len, units, unit_width).transpose(1, 0, 2).astype(F32)
    grad_numer = (grad_units / total).astype(BF)
    grad_denom = -jnp.sum(grad_units * mixed_f, axis=-1, keepdims=True) / total
    grad_weight = (
        jnp.einsum("uiw,ujw->uij", grad_numer, values, preferred_element_type=F32) + grad_denom
    )
    grad_inner = (
        jnp.where(causal, grad_weight * (1.0 + inner), 0.0) * (1.0 / math.sqrt(FD))
    ).astype(BF)
    grad_query = jnp.einsum("uij,ujf->iuf", grad_inner, keys, preferred_element_type=F32)
    grad_keys = jnp.einsum("uij,uif->juf", grad_inner, query, preferred_element_type=F32)
    grad_values = jnp.einsum(
        "uij,uiw->juw", weight.astype(BF), grad_numer, preferred_element_type=F32
    )
    grad_qkv = jnp.concatenate(
        [
            grad_query.reshape(seq_len, -1),
            grad_keys.reshape(seq_len, -1),
            grad_values.reshape(seq_len, -1),
        ],
        axis=1,
    ).astype(BF)
    grad_w_qkv = left_product(hidden_one, grad_qkv).astype(BF)
    grad_one_terms = right_product(grad_qkv, w_qkv)
    grad_hidden_one = scatter_sum(grad_one_terms, tok)
    result = (middle + scatter_sum(result_terms, tok)).astype(BF)
    grad_gains = jnp.concatenate([jnp.sum(grad_one_terms * normed_all, axis=0), grad_gain_two])
    back = exchange(grad_w_qkv.reshape(tok, slice_rows, -1)).transpose(1, 0, 2)

    def gathered(columns):
        if value_split > 1:
            columns = jnp.sum(
                columns.reshape(slice_rows, tok // value_split, value_split, -1).astype(F32), axis=2
            ).astype(BF)
        return columns.reshape(-1, BLK)

    blocks = joined(
        [
            grad_gains.astype(BF).reshape(1, BLK),
            gathered(back[..., :qk_width]),
            gathered(back[..., qk_width : 2 * qk_width]),
            back[..., 2 * qk_width :].reshape(-1, BLK),
            grad_w_out.reshape(-1, BLK),
        ]
    )
    reduced = reduced + routes[0][2](product(routes[0][1], blocks).astype(BF))

    normed_one, scale_one = normalize(input_rows)
    grad_input = grad_middle + norm_back(grad_hidden_one * gain_one, normed_one, scale_one)
    return result, grad_input.astype(BF), reduced


def layer_of_eight(tokens, cotangent, rounded, routes):
    me_tok = lax.axis_index("tok").astype(jnp.int32).reshape(1)
    seq_len = 8 * tokens.shape[1]
    half = seq_len // 2
    x_near, x_far = gather_of_eight(jnp.concatenate([tokens, cotangent]))

    place, rows = routes[0][0](rounded)
    gains, sent, w_out = call(
        unpack_mix,
        [((8, BLK), F32), ((8, 128, 256), BF), ((128, D), BF)],
        [((4, 128, 128), F32), ((16, 128, 128), F32)],
        operands=2,
        flops=2 * place.shape[0] * place.shape[1] * BLK,
        nbytes=2 << 20,
    )(place, rows)
    w_qkv = exchange(sent).reshape(D, 256)
    place, rows = routes[1][0](rounded)
    sent, w_down = call(
        unpack_ff,
        [((8, 128, 768), BF), ((384, D), BF)],
        [((2, 2816, 128), F32), ((24, 128, 128), F32), ((8, 384, 128), F32)],
        operands=2,
        flops=2 * place.shape[0] * place.shape[1] * BLK,
        nbytes=6 << 20,
    )(place, rows)
    w_in = exchange(sent).reshape(D, 768)

    hidden_one, qkv, mixed, mean, total, keep, send = call(
        mix,
        [
            ((seq_len, D), BF),
            ((seq_len, 256), BF),
            ((seq_len, 128), BF),
            ((seq_len, 128), F32),
            ((seq_len, 128), F32),
            ((1, half, D), BF),
            ((1, half, D), BF),
        ],
        scalars=1,
        operands=6,
        flops=2 * seq_len * D * (256 + 128) + 4 * 2 * seq_len * seq_len * 256,
        nbytes=10 << 20,
    )(me_tok, x_near, x_far, gains[:, :D], w_qkv, w_out)
    out = scatter_of_eight(keep, send)[0]

    input_rows = tokens[0].astype(F32)
    middle = input_rows + out
    normed_two, scale_two = normalize(middle)
    gain_two = gains[0, D:]
    h_near, h_far = gather_of_eight((normed_two * gain_two).astype(BF)[None])

    hidden, grad_gate_up, keep, send, result_keep, result_send = call(
        feed_forward,
        [
            ((seq_len, 384), BF),
            ((seq_len, 768), BF),
            ((1, half, D), BF),
            ((1, half, D), BF),
            ((half, D), BF),
            ((half, D), BF),
        ],
        operands=6,
        flops=2 * seq_len * D * (768 * 2 + 384 * 2),
        nbytes=14 << 20,
    )(h_near, h_far, x_near, x_far, w_in, w_down)
    grad_hidden_two = scatter_of_eight(keep, send)[0]
    grad_gain_two = jnp.sum(grad_hidden_two * normed_two, axis=0)
    grad_middle = cotangent[0].astype(F32) + norm_back(
        grad_hidden_two * gain_two, normed_two, scale_two
    )
    m_near, m_far = gather_of_eight(grad_middle.astype(BF)[None])

    grad_w_in = left_product(jnp.concatenate([h_near[0], h_far[0]]), grad_gate_up).astype(BF)
    grad_w_down = left_product(hidden, jnp.concatenate([x_near[1], x_far[1]])).astype(BF)
    back = exchange(grad_w_in.reshape(8, 128, 768))
    (rows,) = call(
        pack_ff,
        [((routes[1][1].shape[0], BLK), BF)],
        [((2, 2816, 128), F32), ((24, 128, 128), F32), ((8, 384, 128), F32)],
        operands=3,
        flops=2 * routes[1][1].size * BLK,
        nbytes=6 << 20,
    )(routes[1][1], back, grad_w_down)
    reduced = routes[1][2](rows)

    grad_qkv, keep, send, gain_terms, grad_w_out = call(
        mix_back,
        [
            ((seq_len, 256), BF),
            ((2, half, D), BF),
            ((2, half, D), BF),
            ((8, D), F32),
            ((128, D), BF),
        ],
        [
            ((seq_len, 128), BF),
            ((seq_len, 128), F32),
            ((2, seq_len, 16), F32),
            ((2, seq_len, 64), F32),
            ((128, D), F32),
        ],
        scalars=1,
        operands=13,
        flops=2 * seq_len * D * (256 + 256) + 10 * 2 * seq_len * seq_len * 256,
        nbytes=20 << 20,
    )(
        me_tok, m_near, m_far, x_near, x_far, w_qkv, w_out, qkv, mixed, mean, total,
        result_keep, result_send,
    )
    grad_w_qkv = left_product(hidden_one, grad_qkv).astype(BF)
    back = exchange(grad_w_qkv.reshape(8, 128, 256))
    out_sum, grad_hidden_one = scatter_of_eight(keep, send)
    result = (middle + out_sum).astype(BF)
    grad_gains = jnp.concatenate([gain_terms[0], grad_gain_two])
    (rows,) = call(
        pack_mix,
        [((routes[0][1].shape[0], BLK), BF)],
        [((4, 128, 128), F32), ((16, 128, 128), F32)],
        operands=4,
        flops=2 * routes[0][1].size * BLK,
        nbytes=2 << 20,
    )(routes[0][1], jnp.pad(grad_gains[None], ((0, 7), (0, 0))), back, grad_w_out)
    reduced = reduced + routes[0][2](rows)

    normed_one, scale_one = normalize(input_rows)
    grad_input = grad_middle + norm_back(
        grad_hidden_one * gains[0, :D], normed_one, scale_one
    )
    return result, grad_input.astype(BF), reduced


def solution(mesh):
    in_specs = (
        P("seq", "tok", None),
        P("seq", "tok", None),
        P(),
        P(("seq", "tok"), None),
        P(("seq", "tok"), None),
        P(("seq", "tok"), None),
    )
    out_specs = (
        P("seq", "tok", None),
        P("seq", "tok", None),
        P(("seq", "tok"), None),
        P(("seq", "tok"), None),
        P(("seq", "tok"), None),
        P(("seq", "tok"), None),
    )
    return jax.shard_map(step, mesh=mesh, in_specs=in_specs, out_specs=out_specs, check_vma=False)
```

```python
import math

import jax
import jax.numpy as jnp
from jax import lax
from jax.experimental import pallas as pl
from jax.experimental.pallas import tpu as pltpu
from jax.sharding import PartitionSpec as P


D = 1024
HEADS = 16
FD = 16
DV = 64
FF = 2752
STEP = 10
BLK = 2048

NORM_EPSILON = 1e-05
ADAM_EPSILON = 1e-08
BETA_ONE = 0.9
BETA_TWO = 0.95
DECAY_RATE = 0.1
BF = jnp.bfloat16
F32 = jnp.float32


MATRIX_BLOCKS = [
    D * HEADS * FD // BLK,
    D * HEADS * FD // BLK,
    D * HEADS * DV // BLK,
    HEADS * DV * D // BLK,
    D * FF // BLK,
    D * FF // BLK,
    FF * D // BLK,
]
MATRIX_STARTS = [1 + sum(MATRIX_BLOCKS[:k]) for k in range(len(MATRIX_BLOCKS))]
LIMITS = [1] + [MATRIX_STARTS[k] + MATRIX_BLOCKS[k] for k in range(len(MATRIX_BLOCKS))]
GROUPS = [(0, 1, 2, 3), (4, 5, 6)]


def product(left, right):
    return jnp.dot(left, right, preferred_element_type=F32)


def left_product(left, right):
    return lax.dot_general(left, right, (((0,), (0,)), ((), ())), preferred_element_type=F32)


def right_product(left, right):
    return lax.dot_general(left, right, (((1,), (1,)), ((), ())), preferred_element_type=F32)


def normalize(values):
    scale = lax.rsqrt(jnp.mean(values * values, axis=-1, keepdims=True) + NORM_EPSILON)
    return (values * scale, scale)


def norm_back(grad_hat, normed_rows, scale):
    return scale * (
        grad_hat - normed_rows * jnp.mean(grad_hat * normed_rows, axis=-1, keepdims=True)
    )


def swap(values, mask):
    return lax.ppermute(values, "tok", [(i, i ^ mask) for i in range(8)])


def exchange(values):
    return lax.all_to_all(values, "tok", 0, 0, tiled=True)


def gather_rows(rows):
    return lax.all_gather(rows, "tok", axis=0, tiled=True)


def scatter_sum(parts, tok):
    sent = parts.astype(BF).reshape(tok, -1, parts.shape[1])
    return jnp.sum(exchange(sent).astype(F32), axis=0)


def gather_of_eight(rows):
    count, height, width = rows.shape
    half = width // 2
    a, b = rows[:, :, :half], rows[:, :, half:]
    ax, by = swap(a, 2), swap(b, 4)
    a2, b2 = jnp.stack([a, ax], 1), jnp.stack([b, by], 1)
    ay, bx = swap(a2, 4), swap(b2, 2)
    first = jnp.concatenate([a2, ay], 1)
    second = jnp.stack([b, bx[:, 0], by, bx[:, 1]], 1)
    near = jnp.concatenate([first, second], -1).reshape(count, 4 * height, width)
    return near, swap(near, 1)


def scatter_of_eight(keep, send):
    many, height, width = keep.shape
    half = width // 2
    mine = keep.astype(F32) + swap(send, 1).astype(F32)
    mine = mine.reshape(many, 4, height // 4, width)
    a, b = mine[..., :half], mine[..., half:]
    got_a = swap(a[:, 2:].astype(BF), 4)
    got_b = swap(jnp.stack([b[:, 1], b[:, 3]], 1).astype(BF), 2)
    a = a[:, :2] + got_a.astype(F32)
    b = jnp.stack([b[:, 0], b[:, 2]], 1) + got_b.astype(F32)
    got_a = swap(a[:, 1].astype(BF), 2)
    got_b = swap(b[:, 1].astype(BF), 4)
    return jnp.concatenate([a[:, 0] + got_a.astype(F32), b[:, 0] + got_b.astype(F32)], -1)


def ff_share(tok):
    return round_up(FF / tok, 128)


def sharded(per_block, tok, group, fill):
    pieces = []
    if group == 0:
        first = jnp.broadcast_to(per_block[:1][None], (tok, 1))
        pieces.append(jnp.pad(first, ((0, 0), (0, 7)), constant_values=fill))
    for k in GROUPS[group]:
        piece = lax.slice_in_dim(per_block, MATRIX_STARTS[k], MATRIX_STARTS[k] + MATRIX_BLOCKS[k])
        if k == 6:
            missing = tok * ff_share(tok) * D // BLK - MATRIX_BLOCKS[k]
            piece = jnp.pad(piece, (0, missing), constant_values=fill)
        piece = piece.reshape(tok, -1)
        missing = -piece.shape[1] % 8
        pieces.append(jnp.pad(piece, ((0, 0), (0, missing)), constant_values=fill))
    return jnp.concatenate(pieces, axis=1)


def piece_of(shard, tok, group, k):
    offset = 0
    for other in (-1,) * (group == 0) + GROUPS[group]:
        if other == -1:
            count = 1
        elif other == 6:
            count = ff_share(tok) * D // BLK
        else:
            count = MATRIX_BLOCKS[other] // tok
        if other == k:
            return shard[offset : offset + count]
        offset += round_up(count, 8)


def joined(pieces):
    return jnp.concatenate([jnp.pad(p, ((0, -p.shape[0] % 8), (0, 0))) for p in pieces], axis=0)


def rotate(values, count):
    return lax.ppermute(values, "seq", [(i, (i + 1) % count) for i in range(count)])


def onehot(index, size):
    return (index[:, None] == jnp.arange(size, dtype=jnp.int32)[None, :]).astype(BF)


def before(size):
    rows = jnp.arange(size, dtype=jnp.int32)
    return (rows[:, None] < rows[None, :]).astype(BF)


def slot_ranks(owners, devices):
    count = owners.shape[0]
    chunks = -(-count // 128)
    padded = jnp.pad(owners, (0, chunks * 128 - count), constant_values=-1).reshape(chunks, 128)
    match = (
        padded[None] == jnp.arange(devices, dtype=jnp.int32)[:, None, None]
    ).astype(BF)
    within = jnp.einsum("ocl,lm->ocm", match, before(128), preferred_element_type=F32)
    totals = jnp.sum(match.astype(F32), axis=2)
    base = product(totals.astype(BF), before(chunks))
    ranks = jnp.sum(match.astype(F32) * (within + base[:, :, None]), axis=0)
    return ranks.reshape(-1)[:count].astype(jnp.int32)


def round_up(value, unit):
    return int(-(-value // unit) * unit)


class Route:
    def __init__(self, owners, slots, group, seq, tok, capacity):
        devices = seq * tok
        count = owners.shape[0]
        self.seq, self.tok, self.capacity, self.group = seq, tok, capacity, group
        owner = sharded(owners, tok, group, -1)
        slot = sharded(slots, tok, group, 0)
        size = owner.shape[1]
        self.size = size
        mean = capacity * size / count
        self.pair_cap = round_up(mean + 4.2 * math.sqrt(mean) + 1, 8)
        share = min(1.0, ((tok - 1) * count / devices + capacity) / count)
        mean = size * share
        self.row_cap = min(round_up(mean + 3.7 * math.sqrt(mean * (1 - share)), 8), round_up(size, 8))
        match = (owner[None] == jnp.arange(devices, dtype=jnp.int32)[:, None, None]).astype(BF)
        earlier = jnp.einsum("otl,lm->otm", match, before(size), preferred_element_type=F32)
        pair_rank = jnp.sum(match.astype(F32) * earlier, axis=0).astype(jnp.int32)
        owner_seq = jnp.where(owner >= 0, owner // tok, -1)
        earlier_seq = jnp.sum(earlier.reshape(seq, tok, tok, size), axis=1)
        match_seq = owner_seq[None] == jnp.arange(seq, dtype=jnp.int32)[:, None, None]
        row_rank = jnp.sum(jnp.where(match_seq, earlier_seq, 0.0), axis=0).astype(jnp.int32)
        self.fits = (jnp.max(pair_rank) < self.pair_cap) & (jnp.max(row_rank) < self.row_cap)
        me_seq, me_tok = lax.axis_index("seq"), lax.axis_index("tok")
        me = me_seq * tok + me_tok
        shard = jnp.arange(tok, dtype=jnp.int32)[:, None]
        place = jnp.where(pair_rank < self.pair_cap, shard * self.pair_cap + pair_rank, -1)
        self.own_slot = jnp.where(owner == me, slot, -1)
        self.has_gains = (owners[0] == me) & (jnp.arange(capacity, dtype=jnp.int32) == 0)
        once = 1 if group == 0 else 0
        own_slot = self.own_slot[:, once:].reshape(-1)
        hit = own_slot[None, :] == jnp.arange(capacity, dtype=jnp.int32)[:, None]
        target = (
            jnp.sum(jnp.where(hit, place[:, once:].reshape(-1)[None, :] + 1, 0), axis=1) - 1
        )
        columns = jnp.arange(tok * self.pair_cap, dtype=jnp.int32)[None, :]
        send = target[:, None] == columns
        if once:
            send = send | (self.has_gains[:, None] & (columns % self.pair_cap == 0))
        self.send = send.astype(BF)
        my_owner = lax.dynamic_index_in_dim(owner, me_tok, 0, keepdims=False)
        my_seq = lax.dynamic_index_in_dim(owner_seq, me_tok, 0, keepdims=False)
        my_pair = lax.dynamic_index_in_dim(pair_rank, me_tok, 0, keepdims=False)
        my_row = lax.dynamic_index_in_dim(row_rank, me_tok, 0, keepdims=False)
        arrive = jnp.where(
            (my_pair < self.pair_cap) & (my_owner >= 0),
            (my_owner % tok) * self.pair_cap + my_pair,
            -1,
        )
        from_pairs = onehot(arrive, tok * self.pair_cap)
        to_rows = onehot(jnp.where(my_seq == me_seq, my_row, -1), self.row_cap)
        self.compact = left_product(to_rows, from_pairs).astype(BF)
        my_place = jnp.where(
            (my_row < self.row_cap) & (my_owner >= 0), my_seq * self.row_cap + my_row, -1
        )
        self.place = onehot(my_place, seq * self.row_cap)
        self.place_back = (
            jnp.arange(seq * self.row_cap, dtype=jnp.int32)[:, None] == my_place[None, :]
        ).astype(BF)

    def fetch(self, rounded):
        packed = left_product(self.send, rounded).astype(BF)
        packed = exchange(packed)
        rows = product(self.compact, packed).astype(BF)
        rows = lax.all_gather(rows, "seq", axis=0, tiled=True)
        return self.place, rows

    def fetch_any(self, rounded):
        width = rounded.shape[1]
        own = self.own_slot.reshape(-1)
        mine = jnp.where(
            (own >= 0)[:, None], jnp.take(rounded, jnp.maximum(own, 0), axis=0), 0
        ).astype(BF)
        mine = lax.all_to_all(mine.reshape(self.tok, self.size, width), "tok", 0, 0, tiled=True)
        mine = jnp.sum(mine, axis=0)
        total = mine
        for _ in range(self.seq - 1):
            mine = rotate(mine, self.seq)
            total = total + mine
        return jnp.eye(self.size, dtype=BF), total

    def give(self, rows):
        rows = lax.psum_scatter(rows, "seq", scatter_dimension=0, tiled=True)
        packed = left_product(self.compact, rows).astype(BF)
        packed = exchange(packed)
        return packed

    def give_any(self, rows):
        width = rows.shape[1]
        total = rows.astype(F32)
        passing = rows
        for _ in range(self.seq - 1):
            passing = rotate(passing, self.seq)
            total = total + passing.astype(F32)
        every = jnp.broadcast_to(total.astype(BF)[None], (self.tok, self.size, width))
        every = lax.all_to_all(every, "tok", 0, 0, tiled=True)
        once = 1 if self.group == 0 else 0
        own = self.own_slot[:, once:].reshape(-1)
        hit = own[None, :] == jnp.arange(self.capacity, dtype=jnp.int32)[:, None]
        index = jnp.sum(
            jnp.where(hit, jnp.arange(1, own.shape[0] + 1, dtype=jnp.int32)[None, :], 0), axis=1
        )
        taken = jnp.take(
            every[:, once:].reshape(-1, width), jnp.maximum(index - 1, 0), axis=0
        ).astype(F32)
        taken = jnp.where((index > 0)[:, None], taken, 0.0)
        if once:
            gains = jnp.sum(every[:, 0].astype(F32), axis=0)
            taken = jnp.where(self.has_gains[:, None], gains[None, :], taken)
        return taken


def rates_for(kinds, seq_len):
    out_std = 1.0 / math.sqrt(max(1, D * 16 // seq_len))
    matrix_rate = 3.0 / math.sqrt(D)
    rate_list = [
        1.0,
        matrix_rate,
        matrix_rate,
        matrix_rate,
        3.0 * out_std,
        matrix_rate,
        matrix_rate,
        3.0 / math.sqrt(FF),
        0.0,
    ]
    decay_list = [0.0] + [DECAY_RATE] * 7 + [0.0]
    chosen = (kinds[:, None] == jnp.arange(9, dtype=jnp.int32)[None, :]).astype(F32)
    rate_values = jnp.sum(chosen * jnp.array(rate_list, F32)[None, :], axis=1)
    decay_values = jnp.sum(chosen * jnp.array(decay_list, F32)[None, :], axis=1)
    return (rate_values, decay_values)


def adam_update(grads, moment_one, moment_two, weights, rate_values, decay_values):
    first = BETA_ONE * moment_one + (1.0 - BETA_ONE) * grads
    second = BETA_TWO * moment_two + (1.0 - BETA_TWO) * grads * grads
    first_hat = first / (1.0 - BETA_ONE**STEP)
    second_hat = second / (1.0 - BETA_TWO**STEP)
    updated = weights - rate_values[:, None] * (
        first_hat / (jnp.sqrt(second_hat) + ADAM_EPSILON) + decay_values[:, None] * weights
    )
    return (first, second, updated)


def columns_out(rows, split):
    return rows.reshape(rows.shape[0], split, -1).transpose(1, 0, 2)


def step(tokens, cotangent, owners, master, first_moment, second_moment):
    seq = lax.axis_size("seq")
    tok = lax.axis_size("tok")
    capacity = master.shape[0]
    me = lax.axis_index("seq") * tok + lax.axis_index("tok")
    slots = slot_ranks(owners, seq * tok)
    routes = [Route(owners, slots, group, seq, tok, capacity) for group in range(2)]
    rounded = master.astype(BF)
    layer = layer_of_eight if tok == 8 else layer_of_any
    result, grad_input, packed = layer(
        tokens, cotangent, rounded, [(r.fetch, r.place_back, r.give) for r in routes]
    )
    mine = (owners == me)[None, :]
    numbers = jnp.arange(owners.shape[0], dtype=jnp.int32)[None, :]
    counts = jnp.sum(
        (mine & (numbers < jnp.array(LIMITS, jnp.int32)[:, None])).astype(jnp.int32), axis=1
    )
    kinds = jnp.sum(
        (jnp.arange(capacity, dtype=jnp.int32)[:, None] >= counts[None, :]).astype(jnp.int32),
        axis=1,
    )
    rates = rates_for(kinds, tokens.shape[1] * tok)
    held = (first_moment, second_moment, master)
    found = (result, grad_input) + owned_update(routes, packed, held, rates)

    def any_owners(carried):
        plain = [(r.fetch_any, jnp.eye(r.size, dtype=BF), r.give_any) for r in routes]
        result, grad_input, parts = layer(tokens, cotangent, rounded, plain)
        reduced = parts[0] + parts[1]
        updated = adam_update(reduced, *held, *rates)
        return (jnp.int32(1), result, grad_input, reduced) + updated

    missing = jnp.where(routes[0].fits & routes[1].fits, 1, 0).astype(jnp.int32)
    found = lax.while_loop(lambda carried: carried[0] == 0, any_owners, (missing,) + found)
    _, result, grad_input, reduced, first, second, updated = found
    return (result[None], grad_input[None], reduced, first, second, updated)


def call(kernel, outs, scratch=(), scalars=0, operands=0, flops=0, nbytes=0):
    return pl.pallas_call(
        kernel,
        out_shape=[jax.ShapeDtypeStruct(shape, kind) for shape, kind in outs],
        in_specs=[pl.BlockSpec(memory_space=pltpu.SMEM)] * scalars
        + [pl.BlockSpec(memory_space=pltpu.VMEM)] * (operands - scalars),
        scratch_shapes=[pltpu.VMEM(shape, kind) for shape, kind in scratch],
        compiler_params=pltpu.CompilerParams(vmem_limit_bytes=60 * 1024 * 1024),
        cost_estimate=pl.CostEstimate(flops=flops, bytes_accessed=nbytes, transcendentals=0),
    )


def dot(left, right):
    return jnp.dot(left, right, preferred_element_type=F32)


def low_lanes(shape):
    return lax.broadcasted_iota(jnp.int32, shape, 1) < 64


def unpack_ff(place_ref, rows_ref, sent_ref, down_ref, flat, wide, tall):
    for c in range(16):
        lanes = pl.ds(128 * c, 128)
        found = dot(place_ref[...], rows_ref[:, lanes])
        flat[0, pl.ds(c, 176, stride=16), :] = found[:176]
        flat[1, pl.ds(c, 176, stride=16), :] = found[176:352]
        tall[c % 8, pl.ds(c // 8, 192, stride=2), :] = found[352:]
    for k in range(8):
        down_ref[:, pl.ds(128 * k, 128)] = tall[k].astype(BF)
    low = low_lanes((64, 128))
    zero = jnp.zeros((64, 128), F32)
    for m in range(2):
        for k in range(24):
            if k > 21:
                wide[k] = jnp.zeros((128, 128), F32)
                continue
            even = flat[m, pl.ds(k, 64, stride=43), :]
            first = flat[m, pl.ds(21 + k, 64, stride=43), :]
            second = flat[m, pl.ds(22 + k, 64, stride=43), :] if k < 21 else zero
            if k == 21:
                even = jnp.where(low, even, 0.0)
            odd = pltpu.roll(jnp.where(low, second, first), 64, 1)
            wide[k, pl.ds(0, 64, stride=2), :] = even
            wide[k, pl.ds(1, 64, stride=2), :] = odd
        for k in range(24):
            sent_ref[k // 3, :, pl.ds(384 * m + 128 * (k % 3), 128)] = wide[k].astype(BF)


def pack_ff(place_ref, back_ref, down_ref, rows_ref, flat, wide, tall):
    low = low_lanes((64, 128))
    for m in range(2):
        flat[m, pl.ds(2752, 64), :] = jnp.zeros((64, 128), F32)
        for k in range(22):
            wide[k] = back_ref[k // 3, :, pl.ds(384 * m + 128 * (k % 3), 128)].astype(F32)

        def turned(k):
            return pltpu.roll(wide[k, pl.ds(1, 64, stride=2), :], 64, 1)

        for k in range(21):
            flat[m, pl.ds(k, 64, stride=43), :] = wide[k, pl.ds(0, 64, stride=2), :]
        after = turned(0)
        flat[m, pl.ds(21, 64, stride=43), :] = jnp.where(
            low, wide[21, pl.ds(0, 64, stride=2), :], after
        )
        for k in range(21):
            current, after = after, turned(k + 1)
            flat[m, pl.ds(22 + k, 64, stride=43), :] = jnp.where(low, current, after)
    for k in range(8):
        tall[k] = down_ref[:, pl.ds(128 * k, 128)].astype(F32)
    for c in range(16):
        grads = jnp.concatenate(
            [
                flat[0, pl.ds(c, 176, stride=16), :],
                flat[1, pl.ds(c, 176, stride=16), :],
                tall[c % 8, pl.ds(c // 8, 192, stride=2), :],
            ],
            axis=0,
        ).astype(BF)
        rows_ref[:, pl.ds(128 * c, 128)] = dot(place_ref[...], grads).astype(BF)


def unpack_mix(place_ref, rows_ref, gains_ref, sent_ref, out_ref, thin, tall):
    for c in range(16):
        lanes = pl.ds(128 * c, 128)
        found = dot(place_ref[...], rows_ref[:, lanes])
        gains_ref[:, lanes] = found[:8]
        thin[c % 2, pl.ds(c // 2, 16, stride=8), :] = found[8:24]
        thin[2 + c % 2, pl.ds(c // 2, 16, stride=8), :] = found[24:40]
        tall[c % 8, pl.ds(c // 8, 64, stride=2), :] = found[40:104]
        tall[8 + c % 8, pl.ds(c // 8, 64, stride=2), :] = found[104:]
    lane = lax.broadcasted_iota(jnp.int32, (128, 128), 1)
    for t in range(8):
        sent_ref[t, :, pl.ds(0, 128)] = tall[t].astype(BF)
        query, keys = thin[t // 4], thin[2 + t // 4]
        if t % 4 != 0:
            query = pltpu.roll(query, 128 - 32 * (t % 4), 1)
        if t % 4 != 1:
            keys = pltpu.roll(keys, (160 - 32 * (t % 4)) % 128, 1)
        both = jnp.where(lane < 32, query, jnp.where(lane < 64, keys, 0.0))
        sent_ref[t, :, pl.ds(128, 128)] = both.astype(BF)
        out_ref[:, pl.ds(128 * t, 128)] = tall[8 + t].astype(BF)


def pack_mix(place_ref, gains_ref, back_ref, out_ref, rows_ref, thin, tall):
    lane = lax.broadcasted_iota(jnp.int32, (128, 128), 1)
    for j in range(2):
        query = jnp.zeros((128, 128), F32)
        keys = jnp.zeros((128, 128), F32)
        for u in range(4):
            both = back_ref[4 * j + u, :, pl.ds(128, 128)].astype(F32)
            here = (lane >= 32 * u) & (lane < 32 * u + 32)
            moved = pltpu.roll(both, 32 * u, 1) if u else both
            query = jnp.where(here, moved, query)
            moved = pltpu.roll(both, (96 + 32 * u) % 128, 1) if u != 1 else both
            keys = jnp.where(here, moved, keys)
        thin[j] = query
        thin[2 + j] = keys
    for t in range(8):
        tall[t] = back_ref[t, :, pl.ds(0, 128)].astype(F32)
        tall[8 + t] = out_ref[:, pl.ds(128 * t, 128)].astype(F32)
    for c in range(16):
        lanes = pl.ds(128 * c, 128)
        grads = jnp.concatenate(
            [
                gains_ref[:, lanes],
                thin[c % 2, pl.ds(c // 2, 16, stride=8), :],
                thin[2 + c % 2, pl.ds(c // 2, 16, stride=8), :],
                tall[c % 8, pl.ds(c // 8, 64, stride=2), :],
                tall[8 + c % 8, pl.ds(c // 8, 64, stride=2), :],
            ],
            axis=0,
        ).astype(BF)
        rows_ref[:, lanes] = dot(place_ref[...], grads).astype(BF)


def select_update(
    send0, send1, near, far, first, second, weights, rates, decays, out0, out1, out2, out3
):
    grads = dot(send0[...], near[...]) + dot(send1[...], far[...])
    out0[...] = grads
    updated = adam_update(
        grads, first[...], second[...], weights[...], rates[...][:, 0], decays[...][:, 0]
    )
    out1[...], out2[...], out3[...] = updated


def owned_update(routes, packed, held, rates):
    capacity, width = held[0].shape
    columns = 256

    def whole(array):
        return pl.BlockSpec(array.shape, lambda i: (0, 0))

    def part(array):
        return pl.BlockSpec((array.shape[0], columns), lambda i: (0, i))

    rates = [values[:, None] for values in rates]
    return tuple(
        pl.pallas_call(
            select_update,
            out_shape=[jax.ShapeDtypeStruct((capacity, width), F32)] * 4,
            grid=(width // columns,),
            in_specs=[whole(routes[0].send), whole(routes[1].send)]
            + [part(array) for array in (*packed, *held)]
            + [whole(rates[0]), whole(rates[1])],
            out_specs=[part(held[0])] * 4,
            cost_estimate=pl.CostEstimate(
                flops=2 * capacity * width * 576, bytes_accessed=16 << 20, transcendentals=0
            ),
        )(routes[0].send, routes[1].send, *packed, *held, *rates)
    )


ROWS = 256


def feed_forward(h0, h1, c0, c1, w_in, w_down, hidden_ref, grad_ref, keep, send, result_keep, result_send):
    for half, (h_ref, c_ref, out, result) in enumerate(
        ((h0, c0, keep, result_keep), (h1, c1, send, result_send))
    ):

        def block(i, carry, half=half, h_ref=h_ref, c_ref=c_ref, out=out, result=result):
            here = pl.ds(pl.multiple_of(i * ROWS, ROWS), ROWS)
            there = pl.ds(pl.multiple_of(i * ROWS + 512 * half, ROWS), ROWS)
            gate_up = dot(h_ref[0, here, :], w_in[...])
            gate, up = gate_up[:, :384], gate_up[:, 384:]
            sigmoid = jax.nn.sigmoid(gate)
            active = gate * sigmoid
            hidden = (active * up).astype(BF)
            hidden_ref[there, :] = hidden
            grad_hidden = right_product(c_ref[1, here, :], w_down[...])
            grad_gate = grad_hidden * up * sigmoid * (1.0 + gate * (1.0 - sigmoid))
            grads = jnp.concatenate([grad_gate, grad_hidden * active], axis=1).astype(BF)
            grad_ref[there, :] = grads
            out[0, here, :] = right_product(grads, w_in[...]).astype(BF)
            result[here, :] = dot(hidden, w_down[...]).astype(BF)
            return carry

        lax.fori_loop(0, 512 // ROWS, block, 0)


def token_at(index, me):
    group = index >> 7
    far = ((group & 3) << 1) | (group >> 2)
    return ((far ^ me) << 7) | (index & 127)


def pair_weights(query, keys, first, me):
    inner = right_product(query, keys) * (1.0 / math.sqrt(FD))
    row = lax.broadcasted_iota(jnp.int32, inner.shape, 0) + first
    column = lax.broadcasted_iota(jnp.int32, inner.shape, 1)
    causal = token_at(row, me) >= token_at(column, me)
    return inner, jnp.where(causal, 1.0 + inner + 0.5 * inner * inner, 0.0), causal


def mix(me_ref, x0, x1, gain, w_in, w_out, hidden_ref, qkv, mixed_ref, mean_ref, total_ref, keep, send):
    me = me_ref[0]
    for half, x_ref in enumerate((x0, x1)):

        def block(i, carry, half=half, x_ref=x_ref):
            here = pl.ds(pl.multiple_of(i * ROWS, ROWS), ROWS)
            there = pl.ds(pl.multiple_of(i * ROWS + 512 * half, ROWS), ROWS)
            x = x_ref[0, here, :].astype(F32)
            scale = lax.rsqrt(jnp.mean(x * x, axis=1, keepdims=True) + NORM_EPSILON)
            hidden = (x * scale * gain[0:1, :]).astype(BF)
            hidden_ref[there, :] = hidden
            qkv[there, :] = dot(hidden, w_in[...]).astype(BF)
            return carry

        lax.fori_loop(0, 512 // ROWS, block, 0)
    for half, out in enumerate((keep, send)):

        def block(i, carry, half=half, out=out):
            first = pl.multiple_of(i * ROWS + 512 * half, ROWS)
            there = pl.ds(first, ROWS)
            means, totals = [], []
            for u in range(2):
                query = qkv[there, pl.ds(128, 128)][:, 16 * u : 16 * u + 16]
                keys = qkv[:, pl.ds(128, 128)][:, 32 + 16 * u : 48 + 16 * u]
                values = qkv[:, pl.ds(0, 128)][:, 64 * u : 64 * u + 64]
                _, weight, _ = pair_weights(query, keys, first, me)
                total = jnp.sum(weight, axis=1, keepdims=True)
                means.append(dot(weight.astype(BF), values) / total)
                totals.append(jnp.broadcast_to(total, (ROWS, 64)))
            mean = jnp.concatenate(means, axis=1)
            mean_ref[there, :] = mean
            total_ref[there, :] = jnp.concatenate(totals, axis=1)
            mixed = mean.astype(BF)
            mixed_ref[there, :] = mixed
            here = pl.ds(pl.multiple_of(i * ROWS, ROWS), ROWS)
            out[0, here, :] = dot(mixed, w_out[...]).astype(BF)
            return carry

        lax.fori_loop(0, 512 // ROWS, block, 0)


def mix_back(
    me_ref, m0, m1, x0, x1, w_in, w_out, qkv, mixed_ref, mean_ref, total_ref, result_keep, result_send,
    grad_ref, keep, send, gain_ref, out_grad, numer, denom, back_keys, back_values, back_out,
):
    me = me_ref[0]
    keep[0] = result_keep[...]
    send[0] = result_send[...]
    back_out[...] = jnp.zeros_like(back_out)
    for half, m_ref in enumerate((m0, m1)):

        def block(i, carry, half=half, m_ref=m_ref):
            here = pl.ds(pl.multiple_of(i * ROWS, ROWS), ROWS)
            there = pl.ds(pl.multiple_of(i * ROWS + 512 * half, ROWS), ROWS)
            grad = right_product(m_ref[0, here, :], w_out[...]).astype(BF).astype(F32)
            back_out[...] += left_product(mixed_ref[there, :], m_ref[0, here, :])
            total = total_ref[there, :]
            numer[there, :] = (grad / total).astype(BF)
            lean = grad * mean_ref[there, :]
            sums = [jnp.sum(lean[:, 64 * u : 64 * u + 64], axis=1, keepdims=True) for u in range(2)]
            wide = jnp.concatenate([jnp.broadcast_to(s, (ROWS, 64)) for s in sums], axis=1)
            denom[there, :] = -wide / total
            return carry

        lax.fori_loop(0, 512 // ROWS, block, 0)
    out_grad[...] = back_out[...].astype(BF)
    back_keys[...] = jnp.zeros_like(back_keys)
    back_values[...] = jnp.zeros_like(back_values)

    def pairs(i, carry):
        first = pl.multiple_of(i * ROWS, ROWS)
        there = pl.ds(first, ROWS)
        query_grads = []
        for u in range(2):
            query = qkv[there, pl.ds(128, 128)][:, 16 * u : 16 * u + 16]
            keys = qkv[:, pl.ds(128, 128)][:, 32 + 16 * u : 48 + 16 * u]
            values = qkv[:, pl.ds(0, 128)][:, 64 * u : 64 * u + 64]
            inner, weight, causal = pair_weights(query, keys, first, me)
            down = numer[there, :][:, 64 * u : 64 * u + 64]
            grad_weight = right_product(down, values) + denom[there, :][:, 64 * u : 64 * u + 1]
            grad_inner = (
                jnp.where(causal, grad_weight * (1.0 + inner), 0.0) * (1.0 / math.sqrt(FD))
            ).astype(BF)
            query_grads.append(dot(grad_inner, keys))
            back_keys[u] += left_product(grad_inner, query)
            back_values[u] += left_product(weight.astype(BF), down)
        grad_ref[there, pl.ds(128, 128)] = jnp.concatenate(
            query_grads + [jnp.zeros((ROWS, 96), F32)], axis=1
        ).astype(BF)
        return carry

    lax.fori_loop(0, 1024 // ROWS, pairs, 0)
    gain_ref[...] = jnp.zeros_like(gain_ref)
    for half, (x_ref, out) in enumerate(((x0, keep), (x1, send))):

        def block(i, carry, half=half, x_ref=x_ref, out=out):
            here = pl.ds(pl.multiple_of(i * ROWS, ROWS), ROWS)
            there = pl.ds(pl.multiple_of(i * ROWS + 512 * half, ROWS), ROWS)
            query_grad = grad_ref[there, pl.ds(128, 128)][:, :32]
            keys_grad = [back_keys[u, there, :].astype(BF) for u in range(2)]
            values_grad = [back_values[u, there, :].astype(BF) for u in range(2)]
            grads = jnp.concatenate(
                values_grad + [query_grad] + keys_grad + [jnp.zeros((ROWS, 64), BF)], axis=1
            )
            grad_ref[there, :] = grads
            terms = right_product(grads, w_in[...])
            out[1, here, :] = terms.astype(BF)
            x = x_ref[0, here, :].astype(F32)
            scale = lax.rsqrt(jnp.mean(x * x, axis=1, keepdims=True) + NORM_EPSILON)
            gain_ref[0:1, :] += jnp.sum(terms * (x * scale), axis=0, keepdims=True)
            return carry

        lax.fori_loop(0, 512 // ROWS, block, 0)


def layer_of_any(tokens, cotangent, rounded, routes):
    tok = lax.axis_size("tok")
    row_count = tokens.shape[1]
    seq_len = row_count * tok
    value_split = max(1, tok // HEADS)
    units = max(1, HEADS // tok)
    unit_width = DV // value_split
    slice_rows = D // tok
    ff_slice = ff_share(tok)
    qk_width = units * FD
    v_width = units * unit_width

    x_all, c_all = gather_rows(tokens[0]), gather_rows(cotangent[0])

    place, rows = routes[0][0](rounded)
    shard = product(place, rows).astype(BF)
    gain_one = shard[0, :D].astype(F32)
    gain_two = shard[0, D:].astype(F32)

    def spread(columns):
        wide = columns.reshape(slice_rows, tok // value_split, 1, qk_width)
        return jnp.broadcast_to(
            wide, (slice_rows, tok // value_split, value_split, qk_width)
        ).reshape(slice_rows, tok, qk_width)

    sent = jnp.concatenate(
        [
            spread(piece_of(shard, tok, 0, 0).reshape(slice_rows, HEADS * FD)),
            spread(piece_of(shard, tok, 0, 1).reshape(slice_rows, HEADS * FD)),
            piece_of(shard, tok, 0, 2).reshape(slice_rows, tok, v_width),
        ],
        axis=-1,
    ).transpose(1, 0, 2)
    w_qkv = exchange(sent).reshape(D, -1)
    w_out = piece_of(shard, tok, 0, 3).reshape(v_width, D)

    def padded(blocks):
        return jnp.pad(blocks.reshape(slice_rows, FF), ((0, 0), (0, tok * ff_slice - FF)))

    place, rows = routes[1][0](rounded)
    shard = product(place, rows).astype(BF)
    sent = jnp.concatenate(
        [
            columns_out(padded(piece_of(shard, tok, 1, 4)), tok),
            columns_out(padded(piece_of(shard, tok, 1, 5)), tok),
        ],
        axis=-1,
    )
    w_gate_up = exchange(sent).reshape(D, -1)
    w_down = piece_of(shard, tok, 1, 6).reshape(ff_slice, D)

    normed_all, _ = normalize(x_all.astype(F32))
    hidden_one = (normed_all * gain_one).astype(BF)
    qkv = product(hidden_one, w_qkv).astype(BF)
    query = qkv[:, :qk_width].reshape(seq_len, units, FD).transpose(1, 0, 2)
    keys = qkv[:, qk_width : 2 * qk_width].reshape(seq_len, units, FD).transpose(1, 0, 2)
    values = qkv[:, 2 * qk_width :].reshape(seq_len, units, unit_width).transpose(1, 0, 2)
    index = jnp.arange(seq_len, dtype=jnp.int32)
    causal = (index[:, None] >= index[None, :])[None]
    inner = jnp.einsum("uif,ujf->uij", query, keys, preferred_element_type=F32) * (
        1.0 / math.sqrt(FD)
    )
    weight = jnp.where(causal, 1.0 + inner + 0.5 * inner * inner, 0.0)
    total = jnp.sum(weight, axis=2, keepdims=True)
    mixed_f = (
        jnp.einsum("uij,ujw->uiw", weight.astype(BF), values, preferred_element_type=F32) / total
    )
    mixed = mixed_f.astype(BF).transpose(1, 0, 2).reshape(seq_len, v_width)
    out = scatter_sum(product(mixed, w_out), tok)

    input_rows = tokens[0].astype(F32)
    middle = input_rows + out
    normed_two, scale_two = normalize(middle)
    hidden_two = gather_rows((normed_two * gain_two).astype(BF))

    gate_up = product(hidden_two, w_gate_up)
    gate, up_proj = gate_up[:, :ff_slice], gate_up[:, ff_slice:]
    sigmoid = jax.nn.sigmoid(gate)
    activated = gate * sigmoid
    hidden = (activated * up_proj).astype(BF)
    grad_hidden = right_product(c_all, w_down)
    grad_gate = (grad_hidden * up_proj * sigmoid * (1.0 + gate * (1.0 - sigmoid))).astype(BF)
    grad_up = (grad_hidden * activated).astype(BF)
    grad_gate_up = jnp.concatenate([grad_gate, grad_up], axis=1)
    grad_two_terms = right_product(grad_gate_up, w_gate_up)
    grad_hidden_two = scatter_sum(grad_two_terms, tok)
    result_terms = product(hidden, w_down)

    grad_gain_two = jnp.sum(grad_hidden_two * normed_two, axis=0)
    grad_middle = cotangent[0].astype(F32) + norm_back(
        grad_hidden_two * gain_two, normed_two, scale_two
    )
    grad_mixer = gather_rows(grad_middle.astype(BF))

    grad_w_down = left_product(hidden, c_all).astype(BF)
    grad_w_gate_up = left_product(hidden_two, grad_gate_up).astype(BF)
    back = exchange(grad_w_gate_up.reshape(tok, slice_rows, 2 * ff_slice))

    def flat(columns):
        rows = columns.transpose(1, 0, 2).reshape(slice_rows, tok * ff_slice)
        return rows[:, :FF].reshape(-1, BLK)

    back_gate, back_up = flat(back[..., :ff_slice]), flat(back[..., ff_slice:])
    blocks = joined([back_gate, back_up, grad_w_down.reshape(-1, BLK)])
    far = routes[1][2](product(routes[1][1], blocks).astype(BF))

    grad_w_out = left_product(mixed, grad_mixer).astype(BF)
    grad_mixed = right_product(grad_mixer, w_out).astype(BF)
    grad_units = grad_mixed.reshape(seq_len, units, unit_width).transpose(1, 0, 2).astype(F32)
    grad_numer = (grad_units / total).astype(BF)
    grad_denom = -jnp.sum(grad_units * mixed_f, axis=-1, keepdims=True) / total
    grad_weight = (
        jnp.einsum("uiw,ujw->uij", grad_numer, values, preferred_element_type=F32) + grad_denom
    )
    grad_inner = (
        jnp.where(causal, grad_weight * (1.0 + inner), 0.0) * (1.0 / math.sqrt(FD))
    ).astype(BF)
    grad_query = jnp.einsum("uij,ujf->iuf", grad_inner, keys, preferred_element_type=F32)
    grad_keys = jnp.einsum("uij,uif->juf", grad_inner, query, preferred_element_type=F32)
    grad_values = jnp.einsum(
        "uij,uiw->juw", weight.astype(BF), grad_numer, preferred_element_type=F32
    )
    grad_qkv = jnp.concatenate(
        [
            grad_query.reshape(seq_len, -1),
            grad_keys.reshape(seq_len, -1),
            grad_values.reshape(seq_len, -1),
        ],
        axis=1,
    ).astype(BF)
    grad_w_qkv = left_product(hidden_one, grad_qkv).astype(BF)
    grad_one_terms = right_product(grad_qkv, w_qkv)
    grad_hidden_one = scatter_sum(grad_one_terms, tok)
    result = (middle + scatter_sum(result_terms, tok)).astype(BF)
    grad_gains = jnp.concatenate([jnp.sum(grad_one_terms * normed_all, axis=0), grad_gain_two])
    back = exchange(grad_w_qkv.reshape(tok, slice_rows, -1)).transpose(1, 0, 2)

    def gathered(columns):
        if value_split > 1:
            columns = jnp.sum(
                columns.reshape(slice_rows, tok // value_split, value_split, -1).astype(F32), axis=2
            ).astype(BF)
        return columns.reshape(-1, BLK)

    blocks = joined(
        [
            grad_gains.astype(BF).reshape(1, BLK),
            gathered(back[..., :qk_width]),
            gathered(back[..., qk_width : 2 * qk_width]),
            back[..., 2 * qk_width :].reshape(-1, BLK),
            grad_w_out.reshape(-1, BLK),
        ]
    )
    near = routes[0][2](product(routes[0][1], blocks).astype(BF))

    normed_one, scale_one = normalize(input_rows)
    grad_input = grad_middle + norm_back(grad_hidden_one * gain_one, normed_one, scale_one)
    return result, grad_input.astype(BF), (near, far)


def layer_of_eight(tokens, cotangent, rounded, routes):
    me_tok = lax.axis_index("tok").astype(jnp.int32).reshape(1)
    seq_len = 8 * tokens.shape[1]
    half = seq_len // 2
    x_near, x_far = gather_of_eight(jnp.concatenate([tokens, cotangent]))

    place, rows = routes[0][0](rounded)
    gains, sent, w_out = call(
        unpack_mix,
        [((8, BLK), F32), ((8, 128, 256), BF), ((128, D), BF)],
        [((4, 128, 128), F32), ((16, 128, 128), F32)],
        operands=2,
        flops=2 * place.shape[0] * place.shape[1] * BLK,
        nbytes=2 << 20,
    )(place, rows)
    w_qkv = exchange(sent).reshape(D, 256)
    place, rows = routes[1][0](rounded)
    sent, w_down = call(
        unpack_ff,
        [((8, 128, 768), BF), ((384, D), BF)],
        [((2, 2816, 128), F32), ((24, 128, 128), F32), ((8, 384, 128), F32)],
        operands=2,
        flops=2 * place.shape[0] * place.shape[1] * BLK,
        nbytes=6 << 20,
    )(place, rows)
    w_in = exchange(sent).reshape(D, 768)

    hidden_one, qkv, mixed, mean, total, keep, send = call(
        mix,
        [
            ((seq_len, D), BF),
            ((seq_len, 256), BF),
            ((seq_len, 128), BF),
            ((seq_len, 128), F32),
            ((seq_len, 128), F32),
            ((1, half, D), BF),
            ((1, half, D), BF),
        ],
        scalars=1,
        operands=6,
        flops=2 * seq_len * D * (256 + 128) + 4 * 2 * seq_len * seq_len * 256,
        nbytes=10 << 20,
    )(me_tok, x_near, x_far, gains[:, :D], w_qkv, w_out)
    out = scatter_of_eight(keep, send)[0]

    input_rows = tokens[0].astype(F32)
    middle = input_rows + out
    normed_two, scale_two = normalize(middle)
    gain_two = gains[0, D:]
    h_near, h_far = gather_of_eight((normed_two * gain_two).astype(BF)[None])

    hidden, grad_gate_up, keep, send, result_keep, result_send = call(
        feed_forward,
        [
            ((seq_len, 384), BF),
            ((seq_len, 768), BF),
            ((1, half, D), BF),
            ((1, half, D), BF),
            ((half, D), BF),
            ((half, D), BF),
        ],
        operands=6,
        flops=2 * seq_len * D * (768 * 2 + 384 * 2),
        nbytes=14 << 20,
    )(h_near, h_far, x_near, x_far, w_in, w_down)
    grad_hidden_two = scatter_of_eight(keep, send)[0]
    grad_gain_two = jnp.sum(grad_hidden_two * normed_two, axis=0)
    grad_middle = cotangent[0].astype(F32) + norm_back(
        grad_hidden_two * gain_two, normed_two, scale_two
    )
    m_near, m_far = gather_of_eight(grad_middle.astype(BF)[None])

    grad_w_in = left_product(jnp.concatenate([h_near[0], h_far[0]]), grad_gate_up).astype(BF)
    grad_w_down = left_product(hidden, jnp.concatenate([x_near[1], x_far[1]])).astype(BF)
    back = exchange(grad_w_in.reshape(8, 128, 768))
    (rows,) = call(
        pack_ff,
        [((routes[1][1].shape[0], BLK), BF)],
        [((2, 2816, 128), F32), ((24, 128, 128), F32), ((8, 384, 128), F32)],
        operands=3,
        flops=2 * routes[1][1].size * BLK,
        nbytes=6 << 20,
    )(routes[1][1], back, grad_w_down)
    far = routes[1][2](rows)

    grad_qkv, keep, send, gain_terms, grad_w_out = call(
        mix_back,
        [
            ((seq_len, 256), BF),
            ((2, half, D), BF),
            ((2, half, D), BF),
            ((8, D), F32),
            ((128, D), BF),
        ],
        [
            ((seq_len, 128), BF),
            ((seq_len, 128), F32),
            ((2, seq_len, 16), F32),
            ((2, seq_len, 64), F32),
            ((128, D), F32),
        ],
        scalars=1,
        operands=13,
        flops=2 * seq_len * D * (256 + 256) + 10 * 2 * seq_len * seq_len * 256,
        nbytes=20 << 20,
    )(
        me_tok, m_near, m_far, x_near, x_far, w_qkv, w_out, qkv, mixed, mean, total,
        result_keep, result_send,
    )
    grad_w_qkv = left_product(hidden_one, grad_qkv).astype(BF)
    back = exchange(grad_w_qkv.reshape(8, 128, 256))
    out_sum, grad_hidden_one = scatter_of_eight(keep, send)
    result = (middle + out_sum).astype(BF)
    grad_gains = jnp.concatenate([gain_terms[0], grad_gain_two])
    (rows,) = call(
        pack_mix,
        [((routes[0][1].shape[0], BLK), BF)],
        [((4, 128, 128), F32), ((16, 128, 128), F32)],
        operands=4,
        flops=2 * routes[0][1].size * BLK,
        nbytes=2 << 20,
    )(routes[0][1], jnp.pad(grad_gains[None], ((0, 7), (0, 0))), back, grad_w_out)
    near = routes[0][2](rows)

    normed_one, scale_one = normalize(input_rows)
    grad_input = grad_middle + norm_back(
        grad_hidden_one * gains[0, :D], normed_one, scale_one
    )
    return result, grad_input.astype(BF), (near, far)


def solution(mesh):
    in_specs = (
        P("seq", "tok", None),
        P("seq", "tok", None),
        P(),
        P(("seq", "tok"), None),
        P(("seq", "tok"), None),
        P(("seq", "tok"), None),
    )
    out_specs = (
        P("seq", "tok", None),
        P("seq", "tok", None),
        P(("seq", "tok"), None),
        P(("seq", "tok"), None),
        P(("seq", "tok"), None),
        P(("seq", "tok"), None),
    )
    return jax.shard_map(step, mesh=mesh, in_specs=in_specs, out_specs=out_specs, check_vma=False)
```

```python
import math

import jax
import jax.numpy as jnp
from jax import lax
from jax.experimental import pallas as pl
from jax.experimental.pallas import tpu as pltpu
from jax.sharding import PartitionSpec as P


D = 1024
HEADS = 16
FD = 16
DV = 64
FF = 2752
STEP = 10
BLK = 2048

NORM_EPSILON = 1e-05
ADAM_EPSILON = 1e-08
BETA_ONE = 0.9
BETA_TWO = 0.95
DECAY_RATE = 0.1
BF = jnp.bfloat16
F32 = jnp.float32


MATRIX_BLOCKS = [
    D * HEADS * FD // BLK,
    D * HEADS * FD // BLK,
    D * HEADS * DV // BLK,
    HEADS * DV * D // BLK,
    D * FF // BLK,
    D * FF // BLK,
    FF * D // BLK,
]
MATRIX_STARTS = [1 + sum(MATRIX_BLOCKS[:k]) for k in range(len(MATRIX_BLOCKS))]
LIMITS = [1] + [MATRIX_STARTS[k] + MATRIX_BLOCKS[k] for k in range(len(MATRIX_BLOCKS))]
GROUPS = [(0, 1, 2, 3), (4, 5, 6)]


def product(left, right):
    return jnp.dot(left, right, preferred_element_type=F32)


def left_product(left, right):
    return lax.dot_general(left, right, (((0,), (0,)), ((), ())), preferred_element_type=F32)


def right_product(left, right):
    return lax.dot_general(left, right, (((1,), (1,)), ((), ())), preferred_element_type=F32)


def normalize(values):
    scale = lax.rsqrt(jnp.mean(values * values, axis=-1, keepdims=True) + NORM_EPSILON)
    return (values * scale, scale)


def norm_back(grad_hat, normed_rows, scale):
    return scale * (
        grad_hat - normed_rows * jnp.mean(grad_hat * normed_rows, axis=-1, keepdims=True)
    )


def swap(values, mask):
    return lax.ppermute(values, "tok", [(i, i ^ mask) for i in range(8)])


def exchange(values):
    return lax.all_to_all(values, "tok", 0, 0, tiled=True)


def gather_rows(rows):
    return lax.all_gather(rows, "tok", axis=0, tiled=True)


def scatter_sum(parts, tok):
    sent = parts.astype(BF).reshape(tok, -1, parts.shape[1])
    return jnp.sum(exchange(sent).astype(F32), axis=0)


def gather_of_eight(rows):
    count, height, width = rows.shape
    half = width // 2
    a, b = rows[:, :, :half], rows[:, :, half:]
    ax, by = swap(a, 2), swap(b, 4)
    a2, b2 = jnp.stack([a, ax], 1), jnp.stack([b, by], 1)
    ay, bx = swap(a2, 4), swap(b2, 2)
    first = jnp.concatenate([a2, ay], 1)
    second = jnp.stack([b, bx[:, 0], by, bx[:, 1]], 1)
    near = jnp.concatenate([first, second], -1).reshape(count, 4 * height, width)
    return near, swap(near, 1)


def scatter_of_eight(keep, send):
    many, height, width = keep.shape
    half = width // 2
    mine = keep.astype(F32) + swap(send, 1).astype(F32)
    mine = mine.reshape(many, 4, height // 4, width)
    a, b = mine[..., :half], mine[..., half:]
    got_a = swap(a[:, 2:].astype(BF), 4)
    got_b = swap(jnp.stack([b[:, 1], b[:, 3]], 1).astype(BF), 2)
    a = a[:, :2] + got_a.astype(F32)
    b = jnp.stack([b[:, 0], b[:, 2]], 1) + got_b.astype(F32)
    got_a = swap(a[:, 1].astype(BF), 2)
    got_b = swap(b[:, 1].astype(BF), 4)
    return jnp.concatenate([a[:, 0] + got_a.astype(F32), b[:, 0] + got_b.astype(F32)], -1)


def ff_share(tok):
    return round_up(FF / tok, 128)


def sharded(per_block, tok, group, fill):
    pieces = []
    if group == 0:
        first = jnp.broadcast_to(per_block[:1][None], (tok, 1))
        pieces.append(jnp.pad(first, ((0, 0), (0, 7)), constant_values=fill))
    for k in GROUPS[group]:
        piece = lax.slice_in_dim(per_block, MATRIX_STARTS[k], MATRIX_STARTS[k] + MATRIX_BLOCKS[k])
        if k == 6:
            missing = tok * ff_share(tok) * D // BLK - MATRIX_BLOCKS[k]
            piece = jnp.pad(piece, (0, missing), constant_values=fill)
        piece = piece.reshape(tok, -1)
        missing = -piece.shape[1] % 8
        pieces.append(jnp.pad(piece, ((0, 0), (0, missing)), constant_values=fill))
    return jnp.concatenate(pieces, axis=1)


def piece_of(shard, tok, group, k):
    offset = 0
    for other in (-1,) * (group == 0) + GROUPS[group]:
        if other == -1:
            count = 1
        elif other == 6:
            count = ff_share(tok) * D // BLK
        else:
            count = MATRIX_BLOCKS[other] // tok
        if other == k:
            return shard[offset : offset + count]
        offset += round_up(count, 8)


def joined(pieces):
    return jnp.concatenate([jnp.pad(p, ((0, -p.shape[0] % 8), (0, 0))) for p in pieces], axis=0)


def selected(places, blocks):
    found, at = [], 0
    for place in places:
        found.append(product(place, blocks[at : at + place.shape[1]]).astype(BF))
        at += place.shape[1]
    return found


def rotate(values, count):
    return lax.ppermute(values, "seq", [(i, (i + 1) % count) for i in range(count)])


def onehot(index, size):
    return (index[:, None] == jnp.arange(size, dtype=jnp.int32)[None, :]).astype(BF)


def before(size):
    rows = jnp.arange(size, dtype=jnp.int32)
    return (rows[:, None] < rows[None, :]).astype(BF)


def slot_ranks(owners, devices):
    count = owners.shape[0]
    chunks = -(-count // 128)
    padded = jnp.pad(owners, (0, chunks * 128 - count), constant_values=-1).reshape(chunks, 128)
    match = (
        padded[None] == jnp.arange(devices, dtype=jnp.int32)[:, None, None]
    ).astype(BF)
    within = jnp.einsum("ocl,lm->ocm", match, before(128), preferred_element_type=F32)
    totals = jnp.sum(match.astype(F32), axis=2)
    base = product(totals.astype(BF), before(chunks))
    ranks = jnp.sum(match.astype(F32) * (within + base[:, :, None]), axis=0)
    return ranks.reshape(-1)[:count].astype(jnp.int32)


def round_up(value, unit):
    return int(-(-value // unit) * unit)


class Route:
    def __init__(self, owners, slots, group, seq, tok, capacity):
        devices = seq * tok
        count = owners.shape[0]
        self.seq, self.tok, self.capacity, self.group = seq, tok, capacity, group
        owner = sharded(owners, tok, group, -1)
        slot = sharded(slots, tok, group, 0)
        size = owner.shape[1]
        self.size = size
        mean = capacity * size / count
        self.pair_cap = round_up(mean + 4.2 * math.sqrt(mean) + 1, 8)
        share = min(1.0, ((tok - 1) * count / devices + capacity) / count)
        cuts = [0, size] if group == 0 else [0, size - ff_share(tok) * D // BLK, size]
        self.cuts = list(zip(cuts[:-1], cuts[1:], strict=True))
        self.row_caps = []
        for start, end in self.cuts:
            mean = (end - start) * share
            cap = round_up(mean + 3.7 * math.sqrt(mean * (1 - share)), 8)
            self.row_caps.append(min(cap, end - start))
        match = (owner[None] == jnp.arange(devices, dtype=jnp.int32)[:, None, None]).astype(BF)
        earlier = jnp.einsum("otl,lm->otm", match, before(size), preferred_element_type=F32)
        pair_rank = jnp.sum(match.astype(F32) * earlier, axis=0).astype(jnp.int32)
        owner_seq = jnp.where(owner >= 0, owner // tok, -1)
        earlier_seq = jnp.sum(earlier.reshape(seq, tok, tok, size), axis=1)
        match_seq = owner_seq[None] == jnp.arange(seq, dtype=jnp.int32)[:, None, None]
        self.fits = jnp.max(pair_rank) < self.pair_cap
        row_ranks = []
        for (start, end), cap in zip(self.cuts, self.row_caps, strict=True):
            part = earlier_seq[:, :, start:end] - earlier_seq[:, :, start : start + 1]
            rank = jnp.sum(jnp.where(match_seq[:, :, start:end], part, 0.0), axis=0)
            rank = rank.astype(jnp.int32)
            self.fits = self.fits & (jnp.max(rank) < cap)
            row_ranks.append(jnp.where(rank < cap, rank, -1))
        row_rank = jnp.concatenate(row_ranks, axis=1)
        me_seq, me_tok = lax.axis_index("seq"), lax.axis_index("tok")
        me = me_seq * tok + me_tok
        shard = jnp.arange(tok, dtype=jnp.int32)[:, None]
        place = jnp.where(pair_rank < self.pair_cap, shard * self.pair_cap + pair_rank, -1)
        self.own_slot = jnp.where(owner == me, slot, -1)
        self.has_gains = (owners[0] == me) & (jnp.arange(capacity, dtype=jnp.int32) == 0)
        once = 1 if group == 0 else 0
        own_slot = self.own_slot[:, once:].reshape(-1)
        hit = own_slot[None, :] == jnp.arange(capacity, dtype=jnp.int32)[:, None]
        target = (
            jnp.sum(jnp.where(hit, place[:, once:].reshape(-1)[None, :] + 1, 0), axis=1) - 1
        )
        columns = jnp.arange(tok * self.pair_cap, dtype=jnp.int32)[None, :]
        send = target[:, None] == columns
        if once:
            send = send | (self.has_gains[:, None] & (columns % self.pair_cap == 0))
        self.send = send.astype(BF)
        my_owner = lax.dynamic_index_in_dim(owner, me_tok, 0, keepdims=False)
        my_seq = lax.dynamic_index_in_dim(owner_seq, me_tok, 0, keepdims=False)
        my_pair = lax.dynamic_index_in_dim(pair_rank, me_tok, 0, keepdims=False)
        my_row = lax.dynamic_index_in_dim(row_rank, me_tok, 0, keepdims=False)
        arrive = jnp.where(
            (my_pair < self.pair_cap) & (my_owner >= 0),
            (my_owner % tok) * self.pair_cap + my_pair,
            -1,
        )
        from_pairs = onehot(arrive, tok * self.pair_cap)
        offset = [sum(self.row_caps[:k]) for k in range(len(self.row_caps))]
        shift = jnp.concatenate(
            [
                jnp.full((end - start,), at, jnp.int32)
                for (start, end), at in zip(self.cuts, offset, strict=True)
            ]
        )
        to_rows = onehot(
            jnp.where((my_seq == me_seq) & (my_row >= 0), my_row + shift, -1), sum(self.row_caps)
        )
        self.compact = left_product(to_rows, from_pairs).astype(BF)
        self.places, self.places_back = [], []
        for (start, end), cap in zip(self.cuts, self.row_caps, strict=True):
            row, owner_of = my_row[start:end], my_owner[start:end]
            at = jnp.where((row >= 0) & (owner_of >= 0), my_seq[start:end] * cap + row, -1)
            self.places.append(onehot(at, seq * cap))
            every = jnp.arange(seq * cap, dtype=jnp.int32)[:, None]
            self.places_back.append((every == at[None, :]).astype(BF))

    def fetch(self, rounded):
        packed = left_product(self.send, rounded).astype(BF)
        packed = exchange(packed)
        rows = product(self.compact, packed).astype(BF)
        fetched, at = [], 0
        for place, cap in zip(self.places, self.row_caps, strict=True):
            part = lax.all_gather(rows[at : at + cap], "seq", axis=0, tiled=True)
            fetched.append((place, part))
            at += cap
        return fetched

    def fetch_any(self, rounded):
        width = rounded.shape[1]
        own = self.own_slot.reshape(-1)
        mine = jnp.where(
            (own >= 0)[:, None], jnp.take(rounded, jnp.maximum(own, 0), axis=0), 0
        ).astype(BF)
        mine = lax.all_to_all(mine.reshape(self.tok, self.size, width), "tok", 0, 0, tiled=True)
        mine = jnp.sum(mine, axis=0)
        total = mine
        for _ in range(self.seq - 1):
            mine = rotate(mine, self.seq)
            total = total + mine
        return [(jnp.eye(end - start, dtype=BF), total[start:end]) for start, end in self.cuts]

    def plain(self):
        eyes = [jnp.eye(end - start, dtype=BF) for start, end in self.cuts]
        return (self.fetch_any, eyes, self.give_any)

    def give(self, rows):
        rows = jnp.concatenate(
            [lax.psum_scatter(part, "seq", scatter_dimension=0, tiled=True) for part in rows]
        )
        packed = left_product(self.compact, rows).astype(BF)
        packed = exchange(packed)
        return packed

    def give_any(self, rows):
        rows = jnp.concatenate(rows)
        width = rows.shape[1]
        total = rows.astype(F32)
        passing = rows
        for _ in range(self.seq - 1):
            passing = rotate(passing, self.seq)
            total = total + passing.astype(F32)
        every = jnp.broadcast_to(total.astype(BF)[None], (self.tok, self.size, width))
        every = lax.all_to_all(every, "tok", 0, 0, tiled=True)
        once = 1 if self.group == 0 else 0
        own = self.own_slot[:, once:].reshape(-1)
        hit = own[None, :] == jnp.arange(self.capacity, dtype=jnp.int32)[:, None]
        index = jnp.sum(
            jnp.where(hit, jnp.arange(1, own.shape[0] + 1, dtype=jnp.int32)[None, :], 0), axis=1
        )
        taken = jnp.take(
            every[:, once:].reshape(-1, width), jnp.maximum(index - 1, 0), axis=0
        ).astype(F32)
        taken = jnp.where((index > 0)[:, None], taken, 0.0)
        if once:
            gains = jnp.sum(every[:, 0].astype(F32), axis=0)
            taken = jnp.where(self.has_gains[:, None], gains[None, :], taken)
        return taken


def rates_for(kinds, seq_len):
    out_std = 1.0 / math.sqrt(max(1, D * 16 // seq_len))
    matrix_rate = 3.0 / math.sqrt(D)
    rate_list = [
        1.0,
        matrix_rate,
        matrix_rate,
        matrix_rate,
        3.0 * out_std,
        matrix_rate,
        matrix_rate,
        3.0 / math.sqrt(FF),
        0.0,
    ]
    decay_list = [0.0] + [DECAY_RATE] * 7 + [0.0]
    chosen = (kinds[:, None] == jnp.arange(9, dtype=jnp.int32)[None, :]).astype(F32)
    rate_values = jnp.sum(chosen * jnp.array(rate_list, F32)[None, :], axis=1)
    decay_values = jnp.sum(chosen * jnp.array(decay_list, F32)[None, :], axis=1)
    return (rate_values, decay_values)


def adam_update(grads, moment_one, moment_two, weights, rate_values, decay_values):
    first = BETA_ONE * moment_one + (1.0 - BETA_ONE) * grads
    second = BETA_TWO * moment_two + (1.0 - BETA_TWO) * grads * grads
    first_hat = first / (1.0 - BETA_ONE**STEP)
    second_hat = second / (1.0 - BETA_TWO**STEP)
    updated = weights - rate_values[:, None] * (
        first_hat / (jnp.sqrt(second_hat) + ADAM_EPSILON) + decay_values[:, None] * weights
    )
    return (first, second, updated)


def columns_out(rows, split):
    return rows.reshape(rows.shape[0], split, -1).transpose(1, 0, 2)


def step(tokens, cotangent, owners, master, first_moment, second_moment):
    seq = lax.axis_size("seq")
    tok = lax.axis_size("tok")
    capacity = master.shape[0]
    me = lax.axis_index("seq") * tok + lax.axis_index("tok")
    slots = slot_ranks(owners, seq * tok)
    routes = [Route(owners, slots, group, seq, tok, capacity) for group in range(2)]
    rounded = master.astype(BF)
    layer = layer_of_eight if tok == 8 else layer_of_any
    result, grad_input, packed = layer(
        tokens, cotangent, rounded, [(r.fetch, r.places_back, r.give) for r in routes]
    )
    mine = (owners == me)[None, :]
    numbers = jnp.arange(owners.shape[0], dtype=jnp.int32)[None, :]
    counts = jnp.sum(
        (mine & (numbers < jnp.array(LIMITS, jnp.int32)[:, None])).astype(jnp.int32), axis=1
    )
    kinds = jnp.sum(
        (jnp.arange(capacity, dtype=jnp.int32)[:, None] >= counts[None, :]).astype(jnp.int32),
        axis=1,
    )
    rates = rates_for(kinds, tokens.shape[1] * tok)
    held = (first_moment, second_moment, master)
    found = (result, grad_input) + owned_update(routes, packed, held, rates)

    def any_owners(carried):
        result, grad_input, parts = layer(
            tokens, cotangent, rounded, [route.plain() for route in routes]
        )
        reduced = parts[0] + parts[1]
        updated = adam_update(reduced, *held, *rates)
        return (jnp.int32(1), result, grad_input, reduced) + updated

    missing = jnp.where(routes[0].fits & routes[1].fits, 1, 0).astype(jnp.int32)
    found = lax.while_loop(lambda carried: carried[0] == 0, any_owners, (missing,) + found)
    _, result, grad_input, reduced, first, second, updated = found
    return (result[None], grad_input[None], reduced, first, second, updated)


def call(kernel, outs, scratch=(), scalars=0, operands=0, flops=0, nbytes=0):
    return pl.pallas_call(
        kernel,
        out_shape=[jax.ShapeDtypeStruct(shape, kind) for shape, kind in outs],
        in_specs=[pl.BlockSpec(memory_space=pltpu.SMEM)] * scalars
        + [pl.BlockSpec(memory_space=pltpu.VMEM)] * (operands - scalars),
        scratch_shapes=[pltpu.VMEM(shape, kind) for shape, kind in scratch],
        compiler_params=pltpu.CompilerParams(vmem_limit_bytes=60 * 1024 * 1024),
        cost_estimate=pl.CostEstimate(flops=flops, bytes_accessed=nbytes, transcendentals=0),
    )


def dot(left, right):
    return jnp.dot(left, right, preferred_element_type=F32)


def low_lanes(shape):
    return lax.broadcasted_iota(jnp.int32, shape, 1) < 64


def unpack_ff(place_ref, rows_ref, sent_ref, flat, wide):
    for c in range(0, 16, 2):
        found = dot(place_ref[...], rows_ref[:, pl.ds(128 * c, 256)])
        for m in range(2):
            half = found[176 * m : 176 * m + 176]
            flat[m, pl.ds(c, 176, stride=16), :] = half[:, :128]
            flat[m, pl.ds(c + 1, 176, stride=16), :] = half[:, 128:]
    low = low_lanes((64, 128))
    zero = jnp.zeros((64, 128), F32)
    for m in range(2):
        for k in range(24):
            if k > 21:
                wide[k] = jnp.zeros((128, 128), F32)
                continue
            even = flat[m, pl.ds(k, 64, stride=43), :]
            first = flat[m, pl.ds(21 + k, 64, stride=43), :]
            second = flat[m, pl.ds(22 + k, 64, stride=43), :] if k < 21 else zero
            if k == 21:
                even = jnp.where(low, even, 0.0)
            odd = pltpu.roll(jnp.where(low, second, first), 64, 1)
            wide[k, pl.ds(0, 64, stride=2), :] = even
            wide[k, pl.ds(1, 64, stride=2), :] = odd
        for k in range(24):
            sent_ref[k // 3, :, pl.ds(384 * m + 128 * (k % 3), 128)] = wide[k].astype(BF)


def unpack_down(place_ref, rows_ref, down_ref, tall):
    for c in range(0, 16, 2):
        found = dot(place_ref[...], rows_ref[:, pl.ds(128 * c, 256)])
        tall[c % 8, pl.ds(c // 8, 192, stride=2), :] = found[:, :128]
        tall[c % 8 + 1, pl.ds(c // 8, 192, stride=2), :] = found[:, 128:]
    for k in range(8):
        down_ref[:, pl.ds(128 * k, 128)] = tall[k].astype(BF)


def pack_ff(place_ref, back_ref, rows_ref, flat, wide):
    low = low_lanes((64, 128))
    for m in range(2):
        flat[m, pl.ds(2752, 64), :] = jnp.zeros((64, 128), F32)
        for k in range(22):
            wide[k] = back_ref[k // 3, :, pl.ds(384 * m + 128 * (k % 3), 128)].astype(F32)

        def turned(k):
            return pltpu.roll(wide[k, pl.ds(1, 64, stride=2), :], 64, 1)

        for k in range(21):
            flat[m, pl.ds(k, 64, stride=43), :] = wide[k, pl.ds(0, 64, stride=2), :]
        after = turned(0)
        flat[m, pl.ds(21, 64, stride=43), :] = jnp.where(
            low, wide[21, pl.ds(0, 64, stride=2), :], after
        )
        for k in range(21):
            current, after = after, turned(k + 1)
            flat[m, pl.ds(22 + k, 64, stride=43), :] = jnp.where(low, current, after)
    for c in range(0, 16, 2):
        grads = jnp.concatenate(
            [
                jnp.concatenate([flat[m, pl.ds(c + h, 176, stride=16), :] for m in range(2)], axis=0)
                for h in range(2)
            ],
            axis=1,
        ).astype(BF)
        rows_ref[:, pl.ds(128 * c, 256)] = dot(place_ref[...], grads).astype(BF)


def pack_down(place_ref, down_ref, rows_ref, tall):
    for k in range(8):
        tall[k] = down_ref[:, pl.ds(128 * k, 128)].astype(F32)
    for c in range(0, 16, 2):
        grads = jnp.concatenate(
            [tall[c % 8 + h, pl.ds(c // 8, 192, stride=2), :] for h in range(2)], axis=1
        ).astype(BF)
        rows_ref[:, pl.ds(128 * c, 256)] = dot(place_ref[...], grads).astype(BF)


def unpack_mix(place_ref, rows_ref, gains_ref, sent_ref, out_ref, thin, tall):
    for c in range(16):
        lanes = pl.ds(128 * c, 128)
        found = dot(place_ref[...], rows_ref[:, lanes])
        gains_ref[:, lanes] = found[:8]
        thin[c % 2, pl.ds(c // 2, 16, stride=8), :] = found[8:24]
        thin[2 + c % 2, pl.ds(c // 2, 16, stride=8), :] = found[24:40]
        tall[c % 8, pl.ds(c // 8, 64, stride=2), :] = found[40:104]
        tall[8 + c % 8, pl.ds(c // 8, 64, stride=2), :] = found[104:]
    lane = lax.broadcasted_iota(jnp.int32, (128, 128), 1)
    for t in range(8):
        sent_ref[t, :, pl.ds(0, 128)] = tall[t].astype(BF)
        query, keys = thin[t // 4], thin[2 + t // 4]
        if t % 4 != 0:
            query = pltpu.roll(query, 128 - 32 * (t % 4), 1)
        if t % 4 != 1:
            keys = pltpu.roll(keys, (160 - 32 * (t % 4)) % 128, 1)
        both = jnp.where(lane < 32, query, jnp.where(lane < 64, keys, 0.0))
        sent_ref[t, :, pl.ds(128, 128)] = both.astype(BF)
        out_ref[:, pl.ds(128 * t, 128)] = tall[8 + t].astype(BF)


def pack_mix(place_ref, gains_ref, back_ref, out_ref, rows_ref, thin, tall):
    lane = lax.broadcasted_iota(jnp.int32, (128, 128), 1)
    for j in range(2):
        query = jnp.zeros((128, 128), F32)
        keys = jnp.zeros((128, 128), F32)
        for u in range(4):
            both = back_ref[4 * j + u, :, pl.ds(128, 128)].astype(F32)
            here = (lane >= 32 * u) & (lane < 32 * u + 32)
            moved = pltpu.roll(both, 32 * u, 1) if u else both
            query = jnp.where(here, moved, query)
            moved = pltpu.roll(both, (96 + 32 * u) % 128, 1) if u != 1 else both
            keys = jnp.where(here, moved, keys)
        thin[j] = query
        thin[2 + j] = keys
    for t in range(8):
        tall[t] = back_ref[t, :, pl.ds(0, 128)].astype(F32)
        tall[8 + t] = out_ref[:, pl.ds(128 * t, 128)].astype(F32)
    for c in range(16):
        lanes = pl.ds(128 * c, 128)
        grads = jnp.concatenate(
            [
                gains_ref[:, lanes],
                thin[c % 2, pl.ds(c // 2, 16, stride=8), :],
                thin[2 + c % 2, pl.ds(c // 2, 16, stride=8), :],
                tall[c % 8, pl.ds(c // 8, 64, stride=2), :],
                tall[8 + c % 8, pl.ds(c // 8, 64, stride=2), :],
            ],
            axis=0,
        ).astype(BF)
        rows_ref[:, lanes] = dot(place_ref[...], grads).astype(BF)


def select_update(
    send0, send1, near, far, first, second, weights, rates, decays, out0, out1, out2, out3
):
    grads = dot(send0[...], near[...]) + dot(send1[...], far[...])
    out0[...] = grads
    updated = adam_update(
        grads, first[...], second[...], weights[...], rates[...][:, 0], decays[...][:, 0]
    )
    out1[...], out2[...], out3[...] = updated


def owned_update(routes, packed, held, rates):
    capacity, width = held[0].shape
    columns = 256

    def whole(array):
        return pl.BlockSpec(array.shape, lambda i: (0, 0))

    def part(array):
        return pl.BlockSpec((array.shape[0], columns), lambda i: (0, i))

    rates = [values[:, None] for values in rates]
    return tuple(
        pl.pallas_call(
            select_update,
            out_shape=[jax.ShapeDtypeStruct((capacity, width), F32)] * 4,
            grid=(width // columns,),
            in_specs=[whole(routes[0].send), whole(routes[1].send)]
            + [part(array) for array in (*packed, *held)]
            + [whole(rates[0]), whole(rates[1])],
            out_specs=[part(held[0])] * 4,
            cost_estimate=pl.CostEstimate(
                flops=2 * capacity * width * 576, bytes_accessed=16 << 20, transcendentals=0
            ),
        )(routes[0].send, routes[1].send, *packed, *held, *rates)
    )


ROWS = 256


def feed_forward(h0, h1, c0, c1, w_in, w_down, hidden_ref, grad_ref, keep, send, result_keep, result_send):
    for half, (h_ref, c_ref, out, result) in enumerate(
        ((h0, c0, keep, result_keep), (h1, c1, send, result_send))
    ):

        def block(i, carry, half=half, h_ref=h_ref, c_ref=c_ref, out=out, result=result):
            here = pl.ds(pl.multiple_of(i * ROWS, ROWS), ROWS)
            there = pl.ds(pl.multiple_of(i * ROWS + 512 * half, ROWS), ROWS)
            gate_up = dot(h_ref[0, here, :], w_in[...])
            gate, up = gate_up[:, :384], gate_up[:, 384:]
            sigmoid = jax.nn.sigmoid(gate)
            active = gate * sigmoid
            hidden = (active * up).astype(BF)
            hidden_ref[there, :] = hidden
            grad_hidden = right_product(c_ref[1, here, :], w_down[...])
            grad_gate = grad_hidden * up * sigmoid * (1.0 + gate * (1.0 - sigmoid))
            grads = jnp.concatenate([grad_gate, grad_hidden * active], axis=1).astype(BF)
            grad_ref[there, :] = grads
            out[0, here, :] = right_product(grads, w_in[...]).astype(BF)
            result[here, :] = dot(hidden, w_down[...]).astype(BF)
            return carry

        lax.fori_loop(0, 512 // ROWS, block, 0)


def token_at(index, me):
    group = index >> 7
    far = ((group & 3) << 1) | (group >> 2)
    return ((far ^ me) << 7) | (index & 127)


def pair_weights(query, keys, first, me):
    inner = right_product(query, keys) * (1.0 / math.sqrt(FD))
    row = lax.broadcasted_iota(jnp.int32, (inner.shape[0], 1), 0) + first
    column = lax.broadcasted_iota(jnp.int32, (1, inner.shape[1]), 1)
    causal = token_at(row, me) >= token_at(column, me)
    return inner, jnp.where(causal, 1.0 + inner + 0.5 * inner * inner, 0.0), causal


def mix(me_ref, x0, x1, gain, w_in, w_out, hidden_ref, qkv, mixed_ref, mean_ref, total_ref, keep, send):
    me = me_ref[0]
    for half, x_ref in enumerate((x0, x1)):

        def block(i, carry, half=half, x_ref=x_ref):
            here = pl.ds(pl.multiple_of(i * ROWS, ROWS), ROWS)
            there = pl.ds(pl.multiple_of(i * ROWS + 512 * half, ROWS), ROWS)
            x = x_ref[0, here, :].astype(F32)
            scale = lax.rsqrt(jnp.mean(x * x, axis=1, keepdims=True) + NORM_EPSILON)
            hidden = (x * scale * gain[0:1, :]).astype(BF)
            hidden_ref[there, :] = hidden
            qkv[there, :] = dot(hidden, w_in[...]).astype(BF)
            return carry

        lax.fori_loop(0, 512 // ROWS, block, 0)
    for half, out in enumerate((keep, send)):

        def block(i, carry, half=half, out=out):
            first = pl.multiple_of(i * ROWS + 512 * half, ROWS)
            there = pl.ds(first, ROWS)
            means, totals = [], []
            for u in range(2):
                query = qkv[there, pl.ds(128, 128)][:, 16 * u : 16 * u + 16]
                keys = qkv[:, pl.ds(128, 128)][:, 32 + 16 * u : 48 + 16 * u]
                values = qkv[:, pl.ds(0, 128)][:, 64 * u : 64 * u + 64]
                _, weight, _ = pair_weights(query, keys, first, me)
                total = jnp.sum(weight, axis=1, keepdims=True)
                means.append(dot(weight.astype(BF), values) / total)
                totals.append(jnp.broadcast_to(total, (ROWS, 64)))
            mean = jnp.concatenate(means, axis=1)
            mean_ref[there, :] = mean
            total_ref[there, :] = jnp.concatenate(totals, axis=1)
            mixed = mean.astype(BF)
            mixed_ref[there, :] = mixed
            here = pl.ds(pl.multiple_of(i * ROWS, ROWS), ROWS)
            out[0, here, :] = dot(mixed, w_out[...]).astype(BF)
            return carry

        lax.fori_loop(0, 512 // ROWS, block, 0)


def mix_back(
    me_ref, m0, m1, x0, x1, w_in, w_out, qkv, mixed_ref, mean_ref, total_ref, result_keep, result_send,
    grad_ref, keep, send, gain_ref, out_grad, numer, denom, back_keys, back_values, back_out,
):
    me = me_ref[0]
    keep[0] = result_keep[...]
    send[0] = result_send[...]
    back_out[...] = jnp.zeros_like(back_out)
    for half, m_ref in enumerate((m0, m1)):

        def block(i, carry, half=half, m_ref=m_ref):
            here = pl.ds(pl.multiple_of(i * ROWS, ROWS), ROWS)
            there = pl.ds(pl.multiple_of(i * ROWS + 512 * half, ROWS), ROWS)
            grad = right_product(m_ref[0, here, :], w_out[...]).astype(BF).astype(F32)
            back_out[...] += left_product(mixed_ref[there, :], m_ref[0, here, :])
            total = total_ref[there, :]
            numer[there, :] = (grad / total).astype(BF)
            lean = grad * mean_ref[there, :]
            sums = [jnp.sum(lean[:, 64 * u : 64 * u + 64], axis=1, keepdims=True) for u in range(2)]
            wide = jnp.concatenate([jnp.broadcast_to(s, (ROWS, 64)) for s in sums], axis=1)
            denom[there, :] = -wide / total
            return carry

        lax.fori_loop(0, 512 // ROWS, block, 0)
    out_grad[...] = back_out[...].astype(BF)
    back_keys[...] = jnp.zeros_like(back_keys)
    back_values[...] = jnp.zeros_like(back_values)

    def pairs(i, carry):
        first = pl.multiple_of(i * ROWS, ROWS)
        there = pl.ds(first, ROWS)
        query_grads = []
        for u in range(2):
            query = qkv[there, pl.ds(128, 128)][:, 16 * u : 16 * u + 16]
            keys = qkv[:, pl.ds(128, 128)][:, 32 + 16 * u : 48 + 16 * u]
            values = qkv[:, pl.ds(0, 128)][:, 64 * u : 64 * u + 64]
            inner, weight, causal = pair_weights(query, keys, first, me)
            down = numer[there, :][:, 64 * u : 64 * u + 64]
            grad_weight = right_product(down, values) + denom[there, :][:, 64 * u : 64 * u + 1]
            grad_inner = (
                jnp.where(causal, grad_weight * (1.0 + inner), 0.0) * (1.0 / math.sqrt(FD))
            ).astype(BF)
            query_grads.append(dot(grad_inner, keys))
            back_keys[u] += left_product(grad_inner, query)
            back_values[u] += left_product(weight.astype(BF), down)
        grad_ref[there, pl.ds(128, 128)] = jnp.concatenate(
            query_grads + [jnp.zeros((ROWS, 96), F32)], axis=1
        ).astype(BF)
        return carry

    lax.fori_loop(0, 1024 // ROWS, pairs, 0)
    gain_ref[...] = jnp.zeros_like(gain_ref)
    for half, (x_ref, out) in enumerate(((x0, keep), (x1, send))):

        def block(i, carry, half=half, x_ref=x_ref, out=out):
            here = pl.ds(pl.multiple_of(i * ROWS, ROWS), ROWS)
            there = pl.ds(pl.multiple_of(i * ROWS + 512 * half, ROWS), ROWS)
            query_grad = grad_ref[there, pl.ds(128, 128)][:, :32]
            keys_grad = [back_keys[u, there, :].astype(BF) for u in range(2)]
            values_grad = [back_values[u, there, :].astype(BF) for u in range(2)]
            grads = jnp.concatenate(
                values_grad + [query_grad] + keys_grad + [jnp.zeros((ROWS, 64), BF)], axis=1
            )
            grad_ref[there, :] = grads
            terms = right_product(grads, w_in[...])
            out[1, here, :] = terms.astype(BF)
            x = x_ref[0, here, :].astype(F32)
            scale = lax.rsqrt(jnp.mean(x * x, axis=1, keepdims=True) + NORM_EPSILON)
            gain_ref[0:1, :] += jnp.sum(terms * (x * scale), axis=0, keepdims=True)
            return carry

        lax.fori_loop(0, 512 // ROWS, block, 0)


def layer_of_any(tokens, cotangent, rounded, routes):
    tok = lax.axis_size("tok")
    row_count = tokens.shape[1]
    seq_len = row_count * tok
    value_split = max(1, tok // HEADS)
    units = max(1, HEADS // tok)
    unit_width = DV // value_split
    slice_rows = D // tok
    ff_slice = ff_share(tok)
    qk_width = units * FD
    v_width = units * unit_width

    x_all, c_all = gather_rows(tokens[0]), gather_rows(cotangent[0])

    shard = jnp.concatenate([product(*part).astype(BF) for part in routes[0][0](rounded)])
    gain_one = shard[0, :D].astype(F32)
    gain_two = shard[0, D:].astype(F32)

    def spread(columns):
        wide = columns.reshape(slice_rows, tok // value_split, 1, qk_width)
        return jnp.broadcast_to(
            wide, (slice_rows, tok // value_split, value_split, qk_width)
        ).reshape(slice_rows, tok, qk_width)

    sent = jnp.concatenate(
        [
            spread(piece_of(shard, tok, 0, 0).reshape(slice_rows, HEADS * FD)),
            spread(piece_of(shard, tok, 0, 1).reshape(slice_rows, HEADS * FD)),
            piece_of(shard, tok, 0, 2).reshape(slice_rows, tok, v_width),
        ],
        axis=-1,
    ).transpose(1, 0, 2)
    w_qkv = exchange(sent).reshape(D, -1)
    w_out = piece_of(shard, tok, 0, 3).reshape(v_width, D)

    def padded(blocks):
        return jnp.pad(blocks.reshape(slice_rows, FF), ((0, 0), (0, tok * ff_slice - FF)))

    shard = jnp.concatenate([product(*part).astype(BF) for part in routes[1][0](rounded)])
    sent = jnp.concatenate(
        [
            columns_out(padded(piece_of(shard, tok, 1, 4)), tok),
            columns_out(padded(piece_of(shard, tok, 1, 5)), tok),
        ],
        axis=-1,
    )
    w_gate_up = exchange(sent).reshape(D, -1)
    w_down = piece_of(shard, tok, 1, 6).reshape(ff_slice, D)

    normed_all, _ = normalize(x_all.astype(F32))
    hidden_one = (normed_all * gain_one).astype(BF)
    qkv = product(hidden_one, w_qkv).astype(BF)
    query = qkv[:, :qk_width].reshape(seq_len, units, FD).transpose(1, 0, 2)
    keys = qkv[:, qk_width : 2 * qk_width].reshape(seq_len, units, FD).transpose(1, 0, 2)
    values = qkv[:, 2 * qk_width :].reshape(seq_len, units, unit_width).transpose(1, 0, 2)
    index = jnp.arange(seq_len, dtype=jnp.int32)
    causal = (index[:, None] >= index[None, :])[None]
    inner = jnp.einsum("uif,ujf->uij", query, keys, preferred_element_type=F32) * (
        1.0 / math.sqrt(FD)
    )
    weight = jnp.where(causal, 1.0 + inner + 0.5 * inner * inner, 0.0)
    total = jnp.sum(weight, axis=2, keepdims=True)
    mixed_f = (
        jnp.einsum("uij,ujw->uiw", weight.astype(BF), values, preferred_element_type=F32) / total
    )
    mixed = mixed_f.astype(BF).transpose(1, 0, 2).reshape(seq_len, v_width)
    out = scatter_sum(product(mixed, w_out), tok)

    input_rows = tokens[0].astype(F32)
    middle = input_rows + out
    normed_two, scale_two = normalize(middle)
    hidden_two = gather_rows((normed_two * gain_two).astype(BF))

    gate_up = product(hidden_two, w_gate_up)
    gate, up_proj = gate_up[:, :ff_slice], gate_up[:, ff_slice:]
    sigmoid = jax.nn.sigmoid(gate)
    activated = gate * sigmoid
    hidden = (activated * up_proj).astype(BF)
    grad_hidden = right_product(c_all, w_down)
    grad_gate = (grad_hidden * up_proj * sigmoid * (1.0 + gate * (1.0 - sigmoid))).astype(BF)
    grad_up = (grad_hidden * activated).astype(BF)
    grad_gate_up = jnp.concatenate([grad_gate, grad_up], axis=1)
    grad_two_terms = right_product(grad_gate_up, w_gate_up)
    grad_hidden_two = scatter_sum(grad_two_terms, tok)
    result_terms = product(hidden, w_down)

    grad_gain_two = jnp.sum(grad_hidden_two * normed_two, axis=0)
    grad_middle = cotangent[0].astype(F32) + norm_back(
        grad_hidden_two * gain_two, normed_two, scale_two
    )
    grad_mixer = gather_rows(grad_middle.astype(BF))

    grad_w_down = left_product(hidden, c_all).astype(BF)
    grad_w_gate_up = left_product(hidden_two, grad_gate_up).astype(BF)
    back = exchange(grad_w_gate_up.reshape(tok, slice_rows, 2 * ff_slice))

    def flat(columns):
        rows = columns.transpose(1, 0, 2).reshape(slice_rows, tok * ff_slice)
        return rows[:, :FF].reshape(-1, BLK)

    back_gate, back_up = flat(back[..., :ff_slice]), flat(back[..., ff_slice:])
    blocks = joined([back_gate, back_up, grad_w_down.reshape(-1, BLK)])
    far = routes[1][2](selected(routes[1][1], blocks))

    grad_w_out = left_product(mixed, grad_mixer).astype(BF)
    grad_mixed = right_product(grad_mixer, w_out).astype(BF)
    grad_units = grad_mixed.reshape(seq_len, units, unit_width).transpose(1, 0, 2).astype(F32)
    grad_numer = (grad_units / total).astype(BF)
    grad_denom = -jnp.sum(grad_units * mixed_f, axis=-1, keepdims=True) / total
    grad_weight = (
        jnp.einsum("uiw,ujw->uij", grad_numer, values, preferred_element_type=F32) + grad_denom
    )
    grad_inner = (
        jnp.where(causal, grad_weight * (1.0 + inner), 0.0) * (1.0 / math.sqrt(FD))
    ).astype(BF)
    grad_query = jnp.einsum("uij,ujf->iuf", grad_inner, keys, preferred_element_type=F32)
    grad_keys = jnp.einsum("uij,uif->juf", grad_inner, query, preferred_element_type=F32)
    grad_values = jnp.einsum(
        "uij,uiw->juw", weight.astype(BF), grad_numer, preferred_element_type=F32
    )
    grad_qkv = jnp.concatenate(
        [
            grad_query.reshape(seq_len, -1),
            grad_keys.reshape(seq_len, -1),
            grad_values.reshape(seq_len, -1),
        ],
        axis=1,
    ).astype(BF)
    grad_w_qkv = left_product(hidden_one, grad_qkv).astype(BF)
    grad_one_terms = right_product(grad_qkv, w_qkv)
    grad_hidden_one = scatter_sum(grad_one_terms, tok)
    result = (middle + scatter_sum(result_terms, tok)).astype(BF)
    grad_gains = jnp.concatenate([jnp.sum(grad_one_terms * normed_all, axis=0), grad_gain_two])
    back = exchange(grad_w_qkv.reshape(tok, slice_rows, -1)).transpose(1, 0, 2)

    def gathered(columns):
        if value_split > 1:
            columns = jnp.sum(
                columns.reshape(slice_rows, tok // value_split, value_split, -1).astype(F32), axis=2
            ).astype(BF)
        return columns.reshape(-1, BLK)

    blocks = joined(
        [
            grad_gains.astype(BF).reshape(1, BLK),
            gathered(back[..., :qk_width]),
            gathered(back[..., qk_width : 2 * qk_width]),
            back[..., 2 * qk_width :].reshape(-1, BLK),
            grad_w_out.reshape(-1, BLK),
        ]
    )
    near = routes[0][2](selected(routes[0][1], blocks))

    normed_one, scale_one = normalize(input_rows)
    grad_input = grad_middle + norm_back(grad_hidden_one * gain_one, normed_one, scale_one)
    return result, grad_input.astype(BF), (near, far)


def layer_of_eight(tokens, cotangent, rounded, routes):
    me_tok = lax.axis_index("tok").astype(jnp.int32).reshape(1)
    seq_len = 8 * tokens.shape[1]
    half = seq_len // 2
    x_near, x_far = gather_of_eight(jnp.concatenate([tokens, cotangent]))

    ((place, rows),) = routes[0][0](rounded)
    gains, sent, w_out = call(
        unpack_mix,
        [((8, BLK), F32), ((8, 128, 256), BF), ((128, D), BF)],
        [((4, 128, 128), F32), ((16, 128, 128), F32)],
        operands=2,
        flops=2 * place.shape[0] * place.shape[1] * BLK,
        nbytes=2 << 20,
    )(place, rows)
    w_qkv = exchange(sent).reshape(D, 256)
    (place, rows), (down_place, down_rows) = routes[1][0](rounded)
    (sent,) = call(
        unpack_ff,
        [((8, 128, 768), BF)],
        [((2, 2816, 128), F32), ((24, 128, 128), F32)],
        operands=2,
        flops=2 * place.size * BLK,
        nbytes=4 << 20,
    )(place, rows)
    (w_down,) = call(
        unpack_down,
        [((384, D), BF)],
        [((8, 384, 128), F32)],
        operands=2,
        flops=2 * down_place.size * BLK,
        nbytes=2 << 20,
    )(down_place, down_rows)
    w_in = exchange(sent).reshape(D, 768)

    hidden_one, qkv, mixed, mean, total, keep, send = call(
        mix,
        [
            ((seq_len, D), BF),
            ((seq_len, 256), BF),
            ((seq_len, 128), BF),
            ((seq_len, 128), F32),
            ((seq_len, 128), F32),
            ((1, half, D), BF),
            ((1, half, D), BF),
        ],
        scalars=1,
        operands=6,
        flops=2 * seq_len * D * (256 + 128) + 4 * 2 * seq_len * seq_len * 256,
        nbytes=10 << 20,
    )(me_tok, x_near, x_far, gains[:, :D], w_qkv, w_out)
    out = scatter_of_eight(keep, send)[0]

    input_rows = tokens[0].astype(F32)
    middle = input_rows + out
    normed_two, scale_two = normalize(middle)
    gain_two = gains[0, D:]
    h_near, h_far = gather_of_eight((normed_two * gain_two).astype(BF)[None])

    hidden, grad_gate_up, keep, send, result_keep, result_send = call(
        feed_forward,
        [
            ((seq_len, 384), BF),
            ((seq_len, 768), BF),
            ((1, half, D), BF),
            ((1, half, D), BF),
            ((half, D), BF),
            ((half, D), BF),
        ],
        operands=6,
        flops=2 * seq_len * D * (768 * 2 + 384 * 2),
        nbytes=14 << 20,
    )(h_near, h_far, x_near, x_far, w_in, w_down)
    grad_hidden_two = scatter_of_eight(keep, send)[0]
    grad_gain_two = jnp.sum(grad_hidden_two * normed_two, axis=0)
    grad_middle = cotangent[0].astype(F32) + norm_back(
        grad_hidden_two * gain_two, normed_two, scale_two
    )
    m_near, m_far = gather_of_eight(grad_middle.astype(BF)[None])

    all_rows = jnp.concatenate([h_near[0], h_far[0]])
    grad_w_in = left_product(all_rows, grad_gate_up).astype(BF)
    all_rows = jnp.concatenate([x_near[1], x_far[1]])
    grad_w_down = left_product(hidden, all_rows).astype(BF)
    back = exchange(grad_w_in.reshape(8, 128, 768))
    (rows,) = call(
        pack_ff,
        [((routes[1][1][0].shape[0], BLK), BF)],
        [((2, 2816, 128), F32), ((24, 128, 128), F32)],
        operands=2,
        flops=2 * routes[1][1][0].size * BLK,
        nbytes=4 << 20,
    )(routes[1][1][0], back)
    (down_rows,) = call(
        pack_down,
        [((routes[1][1][1].shape[0], BLK), BF)],
        [((8, 384, 128), F32)],
        operands=2,
        flops=2 * routes[1][1][1].size * BLK,
        nbytes=2 << 20,
    )(routes[1][1][1], grad_w_down)
    far = routes[1][2]([rows, down_rows])

    grad_qkv, keep, send, gain_terms, grad_w_out = call(
        mix_back,
        [
            ((seq_len, 256), BF),
            ((2, half, D), BF),
            ((2, half, D), BF),
            ((8, D), F32),
            ((128, D), BF),
        ],
        [
            ((seq_len, 128), BF),
            ((seq_len, 128), F32),
            ((2, seq_len, 16), F32),
            ((2, seq_len, 64), F32),
            ((128, D), F32),
        ],
        scalars=1,
        operands=13,
        flops=2 * seq_len * D * (256 + 256) + 10 * 2 * seq_len * seq_len * 256,
        nbytes=20 << 20,
    )(
        me_tok, m_near, m_far, x_near, x_far, w_qkv, w_out, qkv, mixed, mean, total,
        result_keep, result_send,
    )
    grad_w_qkv = left_product(hidden_one, grad_qkv).astype(BF)
    back = exchange(grad_w_qkv.reshape(8, 128, 256))
    out_sum, grad_hidden_one = scatter_of_eight(keep, send)
    result = (middle + out_sum).astype(BF)
    grad_gains = jnp.concatenate([gain_terms[0], grad_gain_two])
    (rows,) = call(
        pack_mix,
        [((routes[0][1][0].shape[0], BLK), BF)],
        [((4, 128, 128), F32), ((16, 128, 128), F32)],
        operands=4,
        flops=2 * routes[0][1][0].size * BLK,
        nbytes=2 << 20,
    )(routes[0][1][0], jnp.pad(grad_gains[None], ((0, 7), (0, 0))), back, grad_w_out)
    near = routes[0][2]([rows])

    normed_one, scale_one = normalize(input_rows)
    grad_input = grad_middle + norm_back(
        grad_hidden_one * gains[0, :D], normed_one, scale_one
    )
    return result, grad_input.astype(BF), (near, far)


def solution(mesh):
    in_specs = (
        P("seq", "tok", None),
        P("seq", "tok", None),
        P(),
        P(("seq", "tok"), None),
        P(("seq", "tok"), None),
        P(("seq", "tok"), None),
    )
    out_specs = (
        P("seq", "tok", None),
        P("seq", "tok", None),
        P(("seq", "tok"), None),
        P(("seq", "tok"), None),
        P(("seq", "tok"), None),
        P(("seq", "tok"), None),
    )
    return jax.shard_map(step, mesh=mesh, in_specs=in_specs, out_specs=out_specs, check_vma=False)
```

```python
import math

import jax
import jax.numpy as jnp
from jax import lax
from jax.experimental import pallas as pl
from jax.experimental.pallas import tpu as pltpu
from jax.sharding import PartitionSpec as P


D = 1024
HEADS = 16
FD = 16
DV = 64
FF = 2752
STEP = 10
BLK = 2048

NORM_EPSILON = 1e-05
ADAM_EPSILON = 1e-08
BETA_ONE = 0.9
BETA_TWO = 0.95
DECAY_RATE = 0.1
BF = jnp.bfloat16
F32 = jnp.float32


MATRIX_BLOCKS = [
    D * HEADS * FD // BLK,
    D * HEADS * FD // BLK,
    D * HEADS * DV // BLK,
    HEADS * DV * D // BLK,
    D * FF // BLK,
    D * FF // BLK,
    FF * D // BLK,
]
MATRIX_STARTS = [1 + sum(MATRIX_BLOCKS[:k]) for k in range(len(MATRIX_BLOCKS))]
LIMITS = [1] + [MATRIX_STARTS[k] + MATRIX_BLOCKS[k] for k in range(len(MATRIX_BLOCKS))]
GROUPS = [(0, 1, 2, 3), (4, 5, 6)]


def product(left, right):
    return jnp.dot(left, right, preferred_element_type=F32)


def left_product(left, right):
    return lax.dot_general(left, right, (((0,), (0,)), ((), ())), preferred_element_type=F32)


def right_product(left, right):
    return lax.dot_general(left, right, (((1,), (1,)), ((), ())), preferred_element_type=F32)


def normalize(values):
    scale = lax.rsqrt(jnp.mean(values * values, axis=-1, keepdims=True) + NORM_EPSILON)
    return (values * scale, scale)


def norm_back(grad_hat, normed_rows, scale):
    return scale * (
        grad_hat - normed_rows * jnp.mean(grad_hat * normed_rows, axis=-1, keepdims=True)
    )


def swap(values, mask):
    return lax.ppermute(values, "tok", [(i, i ^ mask) for i in range(8)])


def exchange(values):
    return lax.all_to_all(values, "tok", 0, 0, tiled=True)


def gather_rows(rows):
    return lax.all_gather(rows, "tok", axis=0, tiled=True)


def scatter_sum(parts, tok):
    sent = parts.astype(BF).reshape(tok, -1, parts.shape[1])
    return jnp.sum(exchange(sent).astype(F32), axis=0)


def gather_of_eight(rows):
    count, height, width = rows.shape
    half = width // 2
    a, b = rows[:, :, :half], rows[:, :, half:]
    ax, by = swap(a, 2), swap(b, 4)
    a2, b2 = jnp.stack([a, ax], 1), jnp.stack([b, by], 1)
    ay, bx = swap(a2, 4), swap(b2, 2)
    first = jnp.concatenate([a2, ay], 1)
    second = jnp.stack([b, bx[:, 0], by, bx[:, 1]], 1)
    near = jnp.concatenate([first, second], -1).reshape(count, 4 * height, width)
    return near, swap(near, 1)


def scatter_of_eight(keep, send):
    many, height, width = keep.shape
    half = width // 2
    mine = keep.astype(F32) + swap(send, 1).astype(F32)
    mine = mine.reshape(many, 4, height // 4, width)
    a, b = mine[..., :half], mine[..., half:]
    got_a = swap(a[:, 2:].astype(BF), 4)
    got_b = swap(jnp.stack([b[:, 1], b[:, 3]], 1).astype(BF), 2)
    a = a[:, :2] + got_a.astype(F32)
    b = jnp.stack([b[:, 0], b[:, 2]], 1) + got_b.astype(F32)
    got_a = swap(a[:, 1].astype(BF), 2)
    got_b = swap(b[:, 1].astype(BF), 4)
    return jnp.concatenate([a[:, 0] + got_a.astype(F32), b[:, 0] + got_b.astype(F32)], -1)


def ff_share(tok):
    return round_up(FF / tok, 128)


def sharded(per_block, tok, group, fill):
    pieces = []
    if group == 0:
        first = jnp.broadcast_to(per_block[:1][None], (tok, 1))
        pieces.append(jnp.pad(first, ((0, 0), (0, 7)), constant_values=fill))
    for k in GROUPS[group]:
        piece = lax.slice_in_dim(per_block, MATRIX_STARTS[k], MATRIX_STARTS[k] + MATRIX_BLOCKS[k])
        if k == 6:
            missing = tok * ff_share(tok) * D // BLK - MATRIX_BLOCKS[k]
            piece = jnp.pad(piece, (0, missing), constant_values=fill)
        piece = piece.reshape(tok, -1)
        missing = -piece.shape[1] % 8
        pieces.append(jnp.pad(piece, ((0, 0), (0, missing)), constant_values=fill))
    return jnp.concatenate(pieces, axis=1)


def piece_of(shard, tok, group, k):
    offset = 0
    for other in (-1,) * (group == 0) + GROUPS[group]:
        if other == -1:
            count = 1
        elif other == 6:
            count = ff_share(tok) * D // BLK
        else:
            count = MATRIX_BLOCKS[other] // tok
        if other == k:
            return shard[offset : offset + count]
        offset += round_up(count, 8)


def joined(pieces):
    return jnp.concatenate([jnp.pad(p, ((0, -p.shape[0] % 8), (0, 0))) for p in pieces], axis=0)


def selected(places, blocks):
    found, at = [], 0
    for place in places:
        found.append(product(place, blocks[at : at + place.shape[1]]).astype(BF))
        at += place.shape[1]
    return found


def line(count, step):
    return [(i, i + step) for i in range(count) if 0 <= i + step < count]


def shift(values, step, seq):
    return lax.ppermute(values, "seq", line(seq, step))


def sum_line(pieces, seq):
    pieces = pieces.reshape(seq, -1, pieces.shape[1])
    up = down = None
    for k in range(1, seq):
        own_up, own_down = pieces[seq - k], pieces[k]
        up = own_up if up is None else (own_up.astype(F32) + up.astype(F32)).astype(BF)
        down = own_down if down is None else (own_down.astype(F32) + down.astype(F32)).astype(BF)
        up = shift(up, 1, seq)
        down = shift(down, -1, seq)
    return pieces[0].astype(F32) + up.astype(F32) + down.astype(F32)


def rotate(values, count):
    return lax.ppermute(values, "seq", [(i, (i + 1) % count) for i in range(count)])


def onehot(index, size):
    return (index[:, None] == jnp.arange(size, dtype=jnp.int32)[None, :]).astype(BF)


def before(size):
    rows = jnp.arange(size, dtype=jnp.int32)
    return (rows[:, None] < rows[None, :]).astype(BF)


def slot_ranks(owners, devices):
    count = owners.shape[0]
    chunks = -(-count // 128)
    padded = jnp.pad(owners, (0, chunks * 128 - count), constant_values=-1).reshape(chunks, 128)
    match = (
        padded[None] == jnp.arange(devices, dtype=jnp.int32)[:, None, None]
    ).astype(BF)
    within = jnp.einsum("ocl,lm->ocm", match, before(128), preferred_element_type=F32)
    totals = jnp.sum(match.astype(F32), axis=2)
    base = product(totals.astype(BF), before(chunks))
    ranks = jnp.sum(match.astype(F32) * (within + base[:, :, None]), axis=0)
    return ranks.reshape(-1)[:count].astype(jnp.int32)


def round_up(value, unit):
    return int(-(-value // unit) * unit)


class Route:
    def __init__(self, owners, slots, group, seq, tok, capacity):
        devices = seq * tok
        count = owners.shape[0]
        self.seq, self.tok, self.capacity, self.group = seq, tok, capacity, group
        owner = sharded(owners, tok, group, -1)
        slot = sharded(slots, tok, group, 0)
        size = owner.shape[1]
        self.size = size
        mean = capacity * size / count
        self.pair_cap = round_up(mean + 4.2 * math.sqrt(mean) + 1, 8)
        share = min(1.0, ((tok - 1) * count / devices + capacity) / count)
        cuts = [0, size] if group == 0 else [0, size - ff_share(tok) * D // BLK, size]
        self.cuts = list(zip(cuts[:-1], cuts[1:], strict=True))
        self.row_caps = []
        for start, end in self.cuts:
            mean = (end - start) * share
            cap = round_up(mean + 3.7 * math.sqrt(mean * (1 - share)), 8)
            self.row_caps.append(min(cap, end - start))
        match = (owner[None] == jnp.arange(devices, dtype=jnp.int32)[:, None, None]).astype(BF)
        earlier = jnp.einsum("otl,lm->otm", match, before(size), preferred_element_type=F32)
        pair_rank = jnp.sum(match.astype(F32) * earlier, axis=0).astype(jnp.int32)
        owner_seq = jnp.where(owner >= 0, owner // tok, -1)
        earlier_seq = jnp.sum(earlier.reshape(seq, tok, tok, size), axis=1)
        match_seq = owner_seq[None] == jnp.arange(seq, dtype=jnp.int32)[:, None, None]
        self.fits = jnp.max(pair_rank) < self.pair_cap
        row_ranks = []
        for (start, end), cap in zip(self.cuts, self.row_caps, strict=True):
            part = earlier_seq[:, :, start:end] - earlier_seq[:, :, start : start + 1]
            rank = jnp.sum(jnp.where(match_seq[:, :, start:end], part, 0.0), axis=0)
            rank = rank.astype(jnp.int32)
            self.fits = self.fits & (jnp.max(rank) < cap)
            row_ranks.append(jnp.where(rank < cap, rank, -1))
        row_rank = jnp.concatenate(row_ranks, axis=1)
        me_seq, me_tok = lax.axis_index("seq"), lax.axis_index("tok")
        me = me_seq * tok + me_tok
        shard = jnp.arange(tok, dtype=jnp.int32)[:, None]
        place = jnp.where(pair_rank < self.pair_cap, shard * self.pair_cap + pair_rank, -1)
        self.own_slot = jnp.where(owner == me, slot, -1)
        self.has_gains = (owners[0] == me) & (jnp.arange(capacity, dtype=jnp.int32) == 0)
        once = 1 if group == 0 else 0
        own_slot = self.own_slot[:, once:].reshape(-1)
        hit = own_slot[None, :] == jnp.arange(capacity, dtype=jnp.int32)[:, None]
        target = (
            jnp.sum(jnp.where(hit, place[:, once:].reshape(-1)[None, :] + 1, 0), axis=1) - 1
        )
        columns = jnp.arange(tok * self.pair_cap, dtype=jnp.int32)[None, :]
        send = target[:, None] == columns
        if once:
            send = send | (self.has_gains[:, None] & (columns % self.pair_cap == 0))
        self.send = send.astype(BF)
        my_owner = lax.dynamic_index_in_dim(owner, me_tok, 0, keepdims=False)
        my_seq = lax.dynamic_index_in_dim(owner_seq, me_tok, 0, keepdims=False)
        my_pair = lax.dynamic_index_in_dim(pair_rank, me_tok, 0, keepdims=False)
        my_row = lax.dynamic_index_in_dim(row_rank, me_tok, 0, keepdims=False)
        arrive = jnp.where(
            (my_pair < self.pair_cap) & (my_owner >= 0),
            (my_owner % tok) * self.pair_cap + my_pair,
            -1,
        )
        from_pairs = onehot(arrive, tok * self.pair_cap)
        offset = [sum(self.row_caps[:k]) for k in range(len(self.row_caps))]
        shift = jnp.concatenate(
            [
                jnp.full((end - start,), at, jnp.int32)
                for (start, end), at in zip(self.cuts, offset, strict=True)
            ]
        )
        to_rows = onehot(
            jnp.where((my_seq == me_seq) & (my_row >= 0), my_row + shift, -1), sum(self.row_caps)
        )
        self.compact = left_product(to_rows, from_pairs).astype(BF)
        self.places, self.places_back = [], []
        for (start, end), cap in zip(self.cuts, self.row_caps, strict=True):
            row, owner_of = my_row[start:end], my_owner[start:end]
            at = jnp.where((row >= 0) & (owner_of >= 0), my_seq[start:end] * cap + row, -1)
            self.places.append(onehot(at, seq * cap))
            if group == 0:
                away = (my_seq[start:end] - me_seq + seq) % seq
                at = jnp.where((row >= 0) & (owner_of >= 0), away * cap + row, -1)
            every = jnp.arange(seq * cap, dtype=jnp.int32)[:, None]
            self.places_back.append((every == at[None, :]).astype(BF))

    def fetch(self, rounded):
        packed = left_product(self.send, rounded).astype(BF)
        packed = exchange(packed)
        rows = product(self.compact, packed).astype(BF)
        fetched, at = [], 0
        for place, cap in zip(self.places, self.row_caps, strict=True):
            part = lax.all_gather(rows[at : at + cap], "seq", axis=0, tiled=True)
            fetched.append((place, part))
            at += cap
        return fetched

    def fetch_any(self, rounded):
        width = rounded.shape[1]
        own = self.own_slot.reshape(-1)
        mine = jnp.where(
            (own >= 0)[:, None], jnp.take(rounded, jnp.maximum(own, 0), axis=0), 0
        ).astype(BF)
        mine = lax.all_to_all(mine.reshape(self.tok, self.size, width), "tok", 0, 0, tiled=True)
        mine = jnp.sum(mine, axis=0)
        total = mine
        for _ in range(self.seq - 1):
            mine = rotate(mine, self.seq)
            total = total + mine
        return [(jnp.eye(end - start, dtype=BF), total[start:end]) for start, end in self.cuts]

    def plain(self):
        eyes = [jnp.eye(end - start, dtype=BF) for start, end in self.cuts]
        return (self.fetch_any, eyes, self.give_any)

    def give(self, rows):
        if self.group == 0:
            return sum_line(rows[0], self.seq).astype(BF)
        return jnp.concatenate(
            [lax.psum_scatter(part, "seq", scatter_dimension=0, tiled=True) for part in rows]
        )

    def give_any(self, rows):
        rows = jnp.concatenate(rows)
        width = rows.shape[1]
        total = rows.astype(F32)
        passing = rows
        for _ in range(self.seq - 1):
            passing = rotate(passing, self.seq)
            total = total + passing.astype(F32)
        every = jnp.broadcast_to(total.astype(BF)[None], (self.tok, self.size, width))
        every = lax.all_to_all(every, "tok", 0, 0, tiled=True)
        once = 1 if self.group == 0 else 0
        own = self.own_slot[:, once:].reshape(-1)
        hit = own[None, :] == jnp.arange(self.capacity, dtype=jnp.int32)[:, None]
        index = jnp.sum(
            jnp.where(hit, jnp.arange(1, own.shape[0] + 1, dtype=jnp.int32)[None, :], 0), axis=1
        )
        taken = jnp.take(
            every[:, once:].reshape(-1, width), jnp.maximum(index - 1, 0), axis=0
        ).astype(F32)
        taken = jnp.where((index > 0)[:, None], taken, 0.0)
        if once:
            gains = jnp.sum(every[:, 0].astype(F32), axis=0)
            taken = jnp.where(self.has_gains[:, None], gains[None, :], taken)
        return taken


def rates_for(kinds, seq_len):
    out_std = 1.0 / math.sqrt(max(1, D * 16 // seq_len))
    matrix_rate = 3.0 / math.sqrt(D)
    rate_list = [
        1.0,
        matrix_rate,
        matrix_rate,
        matrix_rate,
        3.0 * out_std,
        matrix_rate,
        matrix_rate,
        3.0 / math.sqrt(FF),
        0.0,
    ]
    decay_list = [0.0] + [DECAY_RATE] * 7 + [0.0]
    chosen = (kinds[:, None] == jnp.arange(9, dtype=jnp.int32)[None, :]).astype(F32)
    rate_values = jnp.sum(chosen * jnp.array(rate_list, F32)[None, :], axis=1)
    decay_values = jnp.sum(chosen * jnp.array(decay_list, F32)[None, :], axis=1)
    return (rate_values, decay_values)


def adam_update(grads, moment_one, moment_two, weights, rate_values, decay_values):
    first = BETA_ONE * moment_one + (1.0 - BETA_ONE) * grads
    second = BETA_TWO * moment_two + (1.0 - BETA_TWO) * grads * grads
    first_hat = first / (1.0 - BETA_ONE**STEP)
    second_hat = second / (1.0 - BETA_TWO**STEP)
    updated = weights - rate_values[:, None] * (
        first_hat / (jnp.sqrt(second_hat) + ADAM_EPSILON) + decay_values[:, None] * weights
    )
    return (first, second, updated)


def columns_out(rows, split):
    return rows.reshape(rows.shape[0], split, -1).transpose(1, 0, 2)


def step(tokens, cotangent, owners, master, first_moment, second_moment):
    seq = lax.axis_size("seq")
    tok = lax.axis_size("tok")
    capacity = master.shape[0]
    me = lax.axis_index("seq") * tok + lax.axis_index("tok")
    slots = slot_ranks(owners, seq * tok)
    routes = [Route(owners, slots, group, seq, tok, capacity) for group in range(2)]
    rounded = master.astype(BF)
    layer = layer_of_eight if tok == 8 else layer_of_any
    result, grad_input, sums = layer(
        tokens, cotangent, rounded, [(r.fetch, r.places_back, r.give) for r in routes]
    )
    rows = sum(sum(r.row_caps) for r in routes)
    wide = [r.compact.reshape(-1, tok, r.pair_cap) for r in routes]
    compact = jnp.concatenate(
        [
            jnp.pad(wide[0], ((0, 0), (0, 0), (0, routes[1].pair_cap))),
            jnp.pad(wide[1], ((0, 0), (0, 0), (routes[0].pair_cap, 0))),
        ]
    ).reshape(rows, -1)
    send = jnp.concatenate(
        [r.send.reshape(capacity, tok, r.pair_cap) for r in routes], axis=2
    ).reshape(capacity, -1)
    packed = left_product(compact, jnp.concatenate(sums)).astype(BF)
    packed = exchange(packed)
    mine = (owners == me)[None, :]
    numbers = jnp.arange(owners.shape[0], dtype=jnp.int32)[None, :]
    counts = jnp.sum(
        (mine & (numbers < jnp.array(LIMITS, jnp.int32)[:, None])).astype(jnp.int32), axis=1
    )
    kinds = jnp.sum(
        (jnp.arange(capacity, dtype=jnp.int32)[:, None] >= counts[None, :]).astype(jnp.int32),
        axis=1,
    )
    rates = rates_for(kinds, tokens.shape[1] * tok)
    held = (first_moment, second_moment, master)
    found = (result, grad_input) + owned_update(send, packed, held, rates)

    def any_owners(carried):
        result, grad_input, parts = layer(
            tokens, cotangent, rounded, [route.plain() for route in routes]
        )
        reduced = parts[0] + parts[1]
        updated = adam_update(reduced, *held, *rates)
        return (jnp.int32(1), result, grad_input, reduced) + updated

    missing = jnp.where(routes[0].fits & routes[1].fits, 1, 0).astype(jnp.int32)
    found = lax.while_loop(lambda carried: carried[0] == 0, any_owners, (missing,) + found)
    _, result, grad_input, reduced, first, second, updated = found
    return (result[None], grad_input[None], reduced, first, second, updated)


def call(kernel, outs, scratch=(), scalars=0, operands=0, flops=0, nbytes=0):
    return pl.pallas_call(
        kernel,
        out_shape=[jax.ShapeDtypeStruct(shape, kind) for shape, kind in outs],
        in_specs=[pl.BlockSpec(memory_space=pltpu.SMEM)] * scalars
        + [pl.BlockSpec(memory_space=pltpu.VMEM)] * (operands - scalars),
        scratch_shapes=[pltpu.VMEM(shape, kind) for shape, kind in scratch],
        compiler_params=pltpu.CompilerParams(vmem_limit_bytes=60 * 1024 * 1024),
        cost_estimate=pl.CostEstimate(flops=flops, bytes_accessed=nbytes, transcendentals=0),
    )


def dot(left, right):
    return jnp.dot(left, right, preferred_element_type=F32)


def low_lanes(shape):
    return lax.broadcasted_iota(jnp.int32, shape, 1) < 64


def unpack_ff(place_ref, rows_ref, sent_ref, flat, wide):
    for c in range(0, 16, 2):
        found = dot(place_ref[...], rows_ref[:, pl.ds(128 * c, 256)])
        for m in range(2):
            half = found[176 * m : 176 * m + 176]
            flat[m, pl.ds(c, 176, stride=16), :] = half[:, :128]
            flat[m, pl.ds(c + 1, 176, stride=16), :] = half[:, 128:]
    low = low_lanes((64, 128))
    zero = jnp.zeros((64, 128), F32)
    for m in range(2):
        for k in range(24):
            if k > 21:
                wide[k] = jnp.zeros((128, 128), F32)
                continue
            even = flat[m, pl.ds(k, 64, stride=43), :]
            first = flat[m, pl.ds(21 + k, 64, stride=43), :]
            second = flat[m, pl.ds(22 + k, 64, stride=43), :] if k < 21 else zero
            if k == 21:
                even = jnp.where(low, even, 0.0)
            odd = pltpu.roll(jnp.where(low, second, first), 64, 1)
            wide[k, pl.ds(0, 64, stride=2), :] = even
            wide[k, pl.ds(1, 64, stride=2), :] = odd
        for k in range(24):
            sent_ref[k // 3, :, pl.ds(384 * m + 128 * (k % 3), 128)] = wide[k].astype(BF)


def unpack_down(place_ref, rows_ref, down_ref, tall):
    for c in range(0, 16, 2):
        found = dot(place_ref[...], rows_ref[:, pl.ds(128 * c, 256)])
        tall[c % 8, pl.ds(c // 8, 192, stride=2), :] = found[:, :128]
        tall[c % 8 + 1, pl.ds(c // 8, 192, stride=2), :] = found[:, 128:]
    for k in range(8):
        down_ref[:, pl.ds(128 * k, 128)] = tall[k].astype(BF)


def pack_ff(place_ref, back_ref, rows_ref, flat, wide):
    low = low_lanes((64, 128))
    for m in range(2):
        flat[m, pl.ds(2752, 64), :] = jnp.zeros((64, 128), F32)
        for k in range(22):
            wide[k] = back_ref[k // 3, :, pl.ds(384 * m + 128 * (k % 3), 128)].astype(F32)

        def turned(k):
            return pltpu.roll(wide[k, pl.ds(1, 64, stride=2), :], 64, 1)

        for k in range(21):
            flat[m, pl.ds(k, 64, stride=43), :] = wide[k, pl.ds(0, 64, stride=2), :]
        after = turned(0)
        flat[m, pl.ds(21, 64, stride=43), :] = jnp.where(
            low, wide[21, pl.ds(0, 64, stride=2), :], after
        )
        for k in range(21):
            current, after = after, turned(k + 1)
            flat[m, pl.ds(22 + k, 64, stride=43), :] = jnp.where(low, current, after)
    for c in range(0, 16, 2):
        grads = jnp.concatenate(
            [
                jnp.concatenate([flat[m, pl.ds(c + h, 176, stride=16), :] for m in range(2)], axis=0)
                for h in range(2)
            ],
            axis=1,
        ).astype(BF)
        rows_ref[:, pl.ds(128 * c, 256)] = dot(place_ref[...], grads).astype(BF)


def pack_down(place_ref, down_ref, rows_ref, tall):
    for k in range(8):
        tall[k] = down_ref[:, pl.ds(128 * k, 128)].astype(F32)
    for c in range(0, 16, 2):
        grads = jnp.concatenate(
            [tall[c % 8 + h, pl.ds(c // 8, 192, stride=2), :] for h in range(2)], axis=1
        ).astype(BF)
        rows_ref[:, pl.ds(128 * c, 256)] = dot(place_ref[...], grads).astype(BF)


def unpack_mix(place_ref, rows_ref, gains_ref, sent_ref, out_ref, thin, tall):
    for c in range(16):
        lanes = pl.ds(128 * c, 128)
        found = dot(place_ref[...], rows_ref[:, lanes])
        gains_ref[:, lanes] = found[:8]
        thin[c % 2, pl.ds(c // 2, 16, stride=8), :] = found[8:24]
        thin[2 + c % 2, pl.ds(c // 2, 16, stride=8), :] = found[24:40]
        tall[c % 8, pl.ds(c // 8, 64, stride=2), :] = found[40:104]
        tall[8 + c % 8, pl.ds(c // 8, 64, stride=2), :] = found[104:]
    lane = lax.broadcasted_iota(jnp.int32, (128, 128), 1)
    for t in range(8):
        sent_ref[t, :, pl.ds(0, 128)] = tall[t].astype(BF)
        query, keys = thin[t // 4], thin[2 + t // 4]
        if t % 4 != 0:
            query = pltpu.roll(query, 128 - 32 * (t % 4), 1)
        if t % 4 != 1:
            keys = pltpu.roll(keys, (160 - 32 * (t % 4)) % 128, 1)
        both = jnp.where(lane < 32, query, jnp.where(lane < 64, keys, 0.0))
        sent_ref[t, :, pl.ds(128, 128)] = both.astype(BF)
        out_ref[:, pl.ds(128 * t, 128)] = tall[8 + t].astype(BF)


def pack_mix(place_ref, gains_ref, back_ref, out_ref, rows_ref, thin, tall):
    lane = lax.broadcasted_iota(jnp.int32, (128, 128), 1)
    for j in range(2):
        query = jnp.zeros((128, 128), F32)
        keys = jnp.zeros((128, 128), F32)
        for u in range(4):
            both = back_ref[4 * j + u, :, pl.ds(128, 128)].astype(F32)
            here = (lane >= 32 * u) & (lane < 32 * u + 32)
            moved = pltpu.roll(both, 32 * u, 1) if u else both
            query = jnp.where(here, moved, query)
            moved = pltpu.roll(both, (96 + 32 * u) % 128, 1) if u != 1 else both
            keys = jnp.where(here, moved, keys)
        thin[j] = query
        thin[2 + j] = keys
    for t in range(8):
        tall[t] = back_ref[t, :, pl.ds(0, 128)].astype(F32)
        tall[8 + t] = out_ref[:, pl.ds(128 * t, 128)].astype(F32)
    for c in range(16):
        lanes = pl.ds(128 * c, 128)
        grads = jnp.concatenate(
            [
                gains_ref[:, lanes],
                thin[c % 2, pl.ds(c // 2, 16, stride=8), :],
                thin[2 + c % 2, pl.ds(c // 2, 16, stride=8), :],
                tall[c % 8, pl.ds(c // 8, 64, stride=2), :],
                tall[8 + c % 8, pl.ds(c // 8, 64, stride=2), :],
            ],
            axis=0,
        ).astype(BF)
        rows_ref[:, lanes] = dot(place_ref[...], grads).astype(BF)


def select_update(send, rows, first, second, weights, rates, decays, out0, out1, out2, out3):
    grads = dot(send[...], rows[...])
    out0[...] = grads
    updated = adam_update(
        grads, first[...], second[...], weights[...], rates[...][:, 0], decays[...][:, 0]
    )
    out1[...], out2[...], out3[...] = updated


def owned_update(send, rows, held, rates):
    capacity, width = held[0].shape
    columns = 256

    def whole(array):
        return pl.BlockSpec(array.shape, lambda i: (0, 0))

    def part(array):
        return pl.BlockSpec((array.shape[0], columns), lambda i: (0, i))

    rates = [values[:, None] for values in rates]
    return tuple(
        pl.pallas_call(
            select_update,
            out_shape=[jax.ShapeDtypeStruct((capacity, width), F32)] * 4,
            grid=(width // columns,),
            in_specs=[whole(send)]
            + [part(array) for array in (rows, *held)]
            + [whole(rates[0]), whole(rates[1])],
            out_specs=[part(held[0])] * 4,
            cost_estimate=pl.CostEstimate(
                flops=2 * send.size * width, bytes_accessed=16 << 20, transcendentals=0
            ),
        )(send, rows, *held, *rates)
    )


ROWS = 256


def feed_forward(h0, h1, c0, c1, w_in, w_down, hidden_ref, grad_ref, keep, send, result_keep, result_send):
    for half, (h_ref, c_ref, out, result) in enumerate(
        ((h0, c0, keep, result_keep), (h1, c1, send, result_send))
    ):

        def block(i, carry, half=half, h_ref=h_ref, c_ref=c_ref, out=out, result=result):
            here = pl.ds(pl.multiple_of(i * ROWS, ROWS), ROWS)
            there = pl.ds(pl.multiple_of(i * ROWS + 512 * half, ROWS), ROWS)
            gate_up = dot(h_ref[0, here, :], w_in[...])
            gate, up = gate_up[:, :384], gate_up[:, 384:]
            sigmoid = jax.nn.sigmoid(gate)
            active = gate * sigmoid
            hidden = (active * up).astype(BF)
            hidden_ref[there, :] = hidden
            grad_hidden = right_product(c_ref[1, here, :], w_down[...])
            grad_gate = grad_hidden * up * sigmoid * (1.0 + gate * (1.0 - sigmoid))
            grads = jnp.concatenate([grad_gate, grad_hidden * active], axis=1).astype(BF)
            grad_ref[there, :] = grads
            out[0, here, :] = right_product(grads, w_in[...]).astype(BF)
            result[here, :] = dot(hidden, w_down[...]).astype(BF)
            return carry

        lax.fori_loop(0, 512 // ROWS, block, 0)


def token_at(index, me):
    group = index >> 7
    far = ((group & 3) << 1) | (group >> 2)
    return ((far ^ me) << 7) | (index & 127)


def pair_weights(query, keys, first, me):
    inner = right_product(query, keys) * (1.0 / math.sqrt(FD))
    row = lax.broadcasted_iota(jnp.int32, (inner.shape[0], 1), 0) + first
    column = lax.broadcasted_iota(jnp.int32, (1, inner.shape[1]), 1)
    causal = token_at(row, me) >= token_at(column, me)
    return inner, jnp.where(causal, 1.0 + inner + 0.5 * inner * inner, 0.0), causal


def mix(me_ref, x0, x1, gain, w_in, w_out, hidden_ref, qkv, mixed_ref, mean_ref, total_ref, keep, send):
    me = me_ref[0]
    for half, x_ref in enumerate((x0, x1)):

        def block(i, carry, half=half, x_ref=x_ref):
            here = pl.ds(pl.multiple_of(i * ROWS, ROWS), ROWS)
            there = pl.ds(pl.multiple_of(i * ROWS + 512 * half, ROWS), ROWS)
            x = x_ref[0, here, :].astype(F32)
            scale = lax.rsqrt(jnp.mean(x * x, axis=1, keepdims=True) + NORM_EPSILON)
            hidden = (x * scale * gain[0:1, :]).astype(BF)
            hidden_ref[there, :] = hidden
            qkv[there, :] = dot(hidden, w_in[...]).astype(BF)
            return carry

        lax.fori_loop(0, 512 // ROWS, block, 0)
    for half, out in enumerate((keep, send)):

        def block(i, carry, half=half, out=out):
            first = pl.multiple_of(i * ROWS + 512 * half, ROWS)
            there = pl.ds(first, ROWS)
            means, totals = [], []
            for u in range(2):
                query = qkv[there, pl.ds(128, 128)][:, 16 * u : 16 * u + 16]
                keys = qkv[:, pl.ds(128, 128)][:, 32 + 16 * u : 48 + 16 * u]
                values = qkv[:, pl.ds(0, 128)][:, 64 * u : 64 * u + 64]
                _, weight, _ = pair_weights(query, keys, first, me)
                total = jnp.sum(weight, axis=1, keepdims=True)
                means.append(dot(weight.astype(BF), values) / total)
                totals.append(jnp.broadcast_to(total, (ROWS, 64)))
            mean = jnp.concatenate(means, axis=1)
            mean_ref[there, :] = mean
            total_ref[there, :] = jnp.concatenate(totals, axis=1)
            mixed = mean.astype(BF)
            mixed_ref[there, :] = mixed
            here = pl.ds(pl.multiple_of(i * ROWS, ROWS), ROWS)
            out[0, here, :] = dot(mixed, w_out[...]).astype(BF)
            return carry

        lax.fori_loop(0, 512 // ROWS, block, 0)


def mix_back(
    me_ref, m0, m1, x0, x1, w_in, w_out, qkv, mixed_ref, mean_ref, total_ref, result_keep, result_send,
    grad_ref, keep, send, gain_ref, out_grad, numer, denom, back_keys, back_values, back_out,
):
    me = me_ref[0]
    keep[0] = result_keep[...]
    send[0] = result_send[...]
    back_out[...] = jnp.zeros_like(back_out)
    for half, m_ref in enumerate((m0, m1)):

        def block(i, carry, half=half, m_ref=m_ref):
            here = pl.ds(pl.multiple_of(i * ROWS, ROWS), ROWS)
            there = pl.ds(pl.multiple_of(i * ROWS + 512 * half, ROWS), ROWS)
            grad = right_product(m_ref[0, here, :], w_out[...]).astype(BF).astype(F32)
            back_out[...] += left_product(mixed_ref[there, :], m_ref[0, here, :])
            total = total_ref[there, :]
            numer[there, :] = (grad / total).astype(BF)
            lean = grad * mean_ref[there, :]
            sums = [jnp.sum(lean[:, 64 * u : 64 * u + 64], axis=1, keepdims=True) for u in range(2)]
            wide = jnp.concatenate([jnp.broadcast_to(s, (ROWS, 64)) for s in sums], axis=1)
            denom[there, :] = -wide / total
            return carry

        lax.fori_loop(0, 512 // ROWS, block, 0)
    out_grad[...] = back_out[...].astype(BF)
    back_keys[...] = jnp.zeros_like(back_keys)
    back_values[...] = jnp.zeros_like(back_values)

    def pairs(i, carry):
        first = pl.multiple_of(i * ROWS, ROWS)
        there = pl.ds(first, ROWS)
        query_grads = []
        for u in range(2):
            query = qkv[there, pl.ds(128, 128)][:, 16 * u : 16 * u + 16]
            keys = qkv[:, pl.ds(128, 128)][:, 32 + 16 * u : 48 + 16 * u]
            values = qkv[:, pl.ds(0, 128)][:, 64 * u : 64 * u + 64]
            inner, weight, causal = pair_weights(query, keys, first, me)
            down = numer[there, :][:, 64 * u : 64 * u + 64]
            grad_weight = right_product(down, values) + denom[there, :][:, 64 * u : 64 * u + 1]
            grad_inner = (
                jnp.where(causal, grad_weight * (1.0 + inner), 0.0) * (1.0 / math.sqrt(FD))
            ).astype(BF)
            query_grads.append(dot(grad_inner, keys))
            back_keys[u] += left_product(grad_inner, query)
            back_values[u] += left_product(weight.astype(BF), down)
        grad_ref[there, pl.ds(128, 128)] = jnp.concatenate(
            query_grads + [jnp.zeros((ROWS, 96), F32)], axis=1
        ).astype(BF)
        return carry

    lax.fori_loop(0, 1024 // ROWS, pairs, 0)
    gain_ref[...] = jnp.zeros_like(gain_ref)
    for half, (x_ref, out) in enumerate(((x0, keep), (x1, send))):

        def block(i, carry, half=half, x_ref=x_ref, out=out):
            here = pl.ds(pl.multiple_of(i * ROWS, ROWS), ROWS)
            there = pl.ds(pl.multiple_of(i * ROWS + 512 * half, ROWS), ROWS)
            query_grad = grad_ref[there, pl.ds(128, 128)][:, :32]
            keys_grad = [back_keys[u, there, :].astype(BF) for u in range(2)]
            values_grad = [back_values[u, there, :].astype(BF) for u in range(2)]
            grads = jnp.concatenate(
                values_grad + [query_grad] + keys_grad + [jnp.zeros((ROWS, 64), BF)], axis=1
            )
            grad_ref[there, :] = grads
            terms = right_product(grads, w_in[...])
            out[1, here, :] = terms.astype(BF)
            x = x_ref[0, here, :].astype(F32)
            scale = lax.rsqrt(jnp.mean(x * x, axis=1, keepdims=True) + NORM_EPSILON)
            gain_ref[0:1, :] += jnp.sum(terms * (x * scale), axis=0, keepdims=True)
            return carry

        lax.fori_loop(0, 512 // ROWS, block, 0)


def layer_of_any(tokens, cotangent, rounded, routes):
    tok = lax.axis_size("tok")
    row_count = tokens.shape[1]
    seq_len = row_count * tok
    value_split = max(1, tok // HEADS)
    units = max(1, HEADS // tok)
    unit_width = DV // value_split
    slice_rows = D // tok
    ff_slice = ff_share(tok)
    qk_width = units * FD
    v_width = units * unit_width

    x_all, c_all = gather_rows(tokens[0]), gather_rows(cotangent[0])

    shard = jnp.concatenate([product(*part).astype(BF) for part in routes[0][0](rounded)])
    gain_one = shard[0, :D].astype(F32)
    gain_two = shard[0, D:].astype(F32)

    def spread(columns):
        wide = columns.reshape(slice_rows, tok // value_split, 1, qk_width)
        return jnp.broadcast_to(
            wide, (slice_rows, tok // value_split, value_split, qk_width)
        ).reshape(slice_rows, tok, qk_width)

    sent = jnp.concatenate(
        [
            spread(piece_of(shard, tok, 0, 0).reshape(slice_rows, HEADS * FD)),
            spread(piece_of(shard, tok, 0, 1).reshape(slice_rows, HEADS * FD)),
            piece_of(shard, tok, 0, 2).reshape(slice_rows, tok, v_width),
        ],
        axis=-1,
    ).transpose(1, 0, 2)
    w_qkv = exchange(sent).reshape(D, -1)
    w_out = piece_of(shard, tok, 0, 3).reshape(v_width, D)

    def padded(blocks):
        return jnp.pad(blocks.reshape(slice_rows, FF), ((0, 0), (0, tok * ff_slice - FF)))

    shard = jnp.concatenate([product(*part).astype(BF) for part in routes[1][0](rounded)])
    sent = jnp.concatenate(
        [
            columns_out(padded(piece_of(shard, tok, 1, 4)), tok),
            columns_out(padded(piece_of(shard, tok, 1, 5)), tok),
        ],
        axis=-1,
    )
    w_gate_up = exchange(sent).reshape(D, -1)
    w_down = piece_of(shard, tok, 1, 6).reshape(ff_slice, D)

    normed_all, _ = normalize(x_all.astype(F32))
    hidden_one = (normed_all * gain_one).astype(BF)
    qkv = product(hidden_one, w_qkv).astype(BF)
    query = qkv[:, :qk_width].reshape(seq_len, units, FD).transpose(1, 0, 2)
    keys = qkv[:, qk_width : 2 * qk_width].reshape(seq_len, units, FD).transpose(1, 0, 2)
    values = qkv[:, 2 * qk_width :].reshape(seq_len, units, unit_width).transpose(1, 0, 2)
    index = jnp.arange(seq_len, dtype=jnp.int32)
    causal = (index[:, None] >= index[None, :])[None]
    inner = jnp.einsum("uif,ujf->uij", query, keys, preferred_element_type=F32) * (
        1.0 / math.sqrt(FD)
    )
    weight = jnp.where(causal, 1.0 + inner + 0.5 * inner * inner, 0.0)
    total = jnp.sum(weight, axis=2, keepdims=True)
    mixed_f = (
        jnp.einsum("uij,ujw->uiw", weight.astype(BF), values, preferred_element_type=F32) / total
    )
    mixed = mixed_f.astype(BF).transpose(1, 0, 2).reshape(seq_len, v_width)
    out = scatter_sum(product(mixed, w_out), tok)

    input_rows = tokens[0].astype(F32)
    middle = input_rows + out
    normed_two, scale_two = normalize(middle)
    hidden_two = gather_rows((normed_two * gain_two).astype(BF))

    gate_up = product(hidden_two, w_gate_up)
    gate, up_proj = gate_up[:, :ff_slice], gate_up[:, ff_slice:]
    sigmoid = jax.nn.sigmoid(gate)
    activated = gate * sigmoid
    hidden = (activated * up_proj).astype(BF)
    grad_hidden = right_product(c_all, w_down)
    grad_gate = (grad_hidden * up_proj * sigmoid * (1.0 + gate * (1.0 - sigmoid))).astype(BF)
    grad_up = (grad_hidden * activated).astype(BF)
    grad_gate_up = jnp.concatenate([grad_gate, grad_up], axis=1)
    grad_two_terms = right_product(grad_gate_up, w_gate_up)
    grad_hidden_two = scatter_sum(grad_two_terms, tok)
    result_terms = product(hidden, w_down)

    grad_gain_two = jnp.sum(grad_hidden_two * normed_two, axis=0)
    grad_middle = cotangent[0].astype(F32) + norm_back(
        grad_hidden_two * gain_two, normed_two, scale_two
    )
    grad_mixer = gather_rows(grad_middle.astype(BF))

    grad_w_down = left_product(hidden, c_all).astype(BF)
    grad_w_gate_up = left_product(hidden_two, grad_gate_up).astype(BF)
    back = exchange(grad_w_gate_up.reshape(tok, slice_rows, 2 * ff_slice))

    def flat(columns):
        rows = columns.transpose(1, 0, 2).reshape(slice_rows, tok * ff_slice)
        return rows[:, :FF].reshape(-1, BLK)

    back_gate, back_up = flat(back[..., :ff_slice]), flat(back[..., ff_slice:])
    blocks = joined([back_gate, back_up, grad_w_down.reshape(-1, BLK)])
    far = routes[1][2](selected(routes[1][1], blocks))

    grad_w_out = left_product(mixed, grad_mixer).astype(BF)
    grad_mixed = right_product(grad_mixer, w_out).astype(BF)
    grad_units = grad_mixed.reshape(seq_len, units, unit_width).transpose(1, 0, 2).astype(F32)
    grad_numer = (grad_units / total).astype(BF)
    grad_denom = -jnp.sum(grad_units * mixed_f, axis=-1, keepdims=True) / total
    grad_weight = (
        jnp.einsum("uiw,ujw->uij", grad_numer, values, preferred_element_type=F32) + grad_denom
    )
    grad_inner = (
        jnp.where(causal, grad_weight * (1.0 + inner), 0.0) * (1.0 / math.sqrt(FD))
    ).astype(BF)
    grad_query = jnp.einsum("uij,ujf->iuf", grad_inner, keys, preferred_element_type=F32)
    grad_keys = jnp.einsum("uij,uif->juf", grad_inner, query, preferred_element_type=F32)
    grad_values = jnp.einsum(
        "uij,uiw->juw", weight.astype(BF), grad_numer, preferred_element_type=F32
    )
    grad_qkv = jnp.concatenate(
        [
            grad_query.reshape(seq_len, -1),
            grad_keys.reshape(seq_len, -1),
            grad_values.reshape(seq_len, -1),
        ],
        axis=1,
    ).astype(BF)
    grad_w_qkv = left_product(hidden_one, grad_qkv).astype(BF)
    grad_one_terms = right_product(grad_qkv, w_qkv)
    grad_hidden_one = scatter_sum(grad_one_terms, tok)
    result = (middle + scatter_sum(result_terms, tok)).astype(BF)
    grad_gains = jnp.concatenate([jnp.sum(grad_one_terms * normed_all, axis=0), grad_gain_two])
    back = exchange(grad_w_qkv.reshape(tok, slice_rows, -1)).transpose(1, 0, 2)

    def gathered(columns):
        if value_split > 1:
            columns = jnp.sum(
                columns.reshape(slice_rows, tok // value_split, value_split, -1).astype(F32), axis=2
            ).astype(BF)
        return columns.reshape(-1, BLK)

    blocks = joined(
        [
            grad_gains.astype(BF).reshape(1, BLK),
            gathered(back[..., :qk_width]),
            gathered(back[..., qk_width : 2 * qk_width]),
            back[..., 2 * qk_width :].reshape(-1, BLK),
            grad_w_out.reshape(-1, BLK),
        ]
    )
    near = routes[0][2](selected(routes[0][1], blocks))

    normed_one, scale_one = normalize(input_rows)
    grad_input = grad_middle + norm_back(grad_hidden_one * gain_one, normed_one, scale_one)
    return result, grad_input.astype(BF), (near, far)


def layer_of_eight(tokens, cotangent, rounded, routes):
    me_tok = lax.axis_index("tok").astype(jnp.int32).reshape(1)
    seq_len = 8 * tokens.shape[1]
    half = seq_len // 2
    x_near, x_far = gather_of_eight(jnp.concatenate([tokens, cotangent]))

    ((place, rows),) = routes[0][0](rounded)
    gains, sent, w_out = call(
        unpack_mix,
        [((8, BLK), F32), ((8, 128, 256), BF), ((128, D), BF)],
        [((4, 128, 128), F32), ((16, 128, 128), F32)],
        operands=2,
        flops=2 * place.shape[0] * place.shape[1] * BLK,
        nbytes=2 << 20,
    )(place, rows)
    w_qkv = exchange(sent).reshape(D, 256)
    (place, rows), (down_place, down_rows) = routes[1][0](rounded)
    (sent,) = call(
        unpack_ff,
        [((8, 128, 768), BF)],
        [((2, 2816, 128), F32), ((24, 128, 128), F32)],
        operands=2,
        flops=2 * place.size * BLK,
        nbytes=4 << 20,
    )(place, rows)
    (w_down,) = call(
        unpack_down,
        [((384, D), BF)],
        [((8, 384, 128), F32)],
        operands=2,
        flops=2 * down_place.size * BLK,
        nbytes=2 << 20,
    )(down_place, down_rows)
    w_in = exchange(sent).reshape(D, 768)

    hidden_one, qkv, mixed, mean, total, keep, send = call(
        mix,
        [
            ((seq_len, D), BF),
            ((seq_len, 256), BF),
            ((seq_len, 128), BF),
            ((seq_len, 128), F32),
            ((seq_len, 128), F32),
            ((1, half, D), BF),
            ((1, half, D), BF),
        ],
        scalars=1,
        operands=6,
        flops=2 * seq_len * D * (256 + 128) + 4 * 2 * seq_len * seq_len * 256,
        nbytes=10 << 20,
    )(me_tok, x_near, x_far, gains[:, :D], w_qkv, w_out)
    out = scatter_of_eight(keep, send)[0]

    input_rows = tokens[0].astype(F32)
    middle = input_rows + out
    normed_two, scale_two = normalize(middle)
    gain_two = gains[0, D:]
    h_near, h_far = gather_of_eight((normed_two * gain_two).astype(BF)[None])

    hidden, grad_gate_up, keep, send, result_keep, result_send = call(
        feed_forward,
        [
            ((seq_len, 384), BF),
            ((seq_len, 768), BF),
            ((1, half, D), BF),
            ((1, half, D), BF),
            ((half, D), BF),
            ((half, D), BF),
        ],
        operands=6,
        flops=2 * seq_len * D * (768 * 2 + 384 * 2),
        nbytes=14 << 20,
    )(h_near, h_far, x_near, x_far, w_in, w_down)
    grad_hidden_two = scatter_of_eight(keep, send)[0]
    grad_gain_two = jnp.sum(grad_hidden_two * normed_two, axis=0)
    grad_middle = cotangent[0].astype(F32) + norm_back(
        grad_hidden_two * gain_two, normed_two, scale_two
    )
    m_near, m_far = gather_of_eight(grad_middle.astype(BF)[None])

    all_rows = jnp.concatenate([h_near[0], h_far[0]])
    grad_w_in = left_product(all_rows, grad_gate_up).astype(BF)
    all_rows = jnp.concatenate([x_near[1], x_far[1]])
    grad_w_down = left_product(hidden, all_rows).astype(BF)
    back = exchange(grad_w_in.reshape(8, 128, 768))
    (rows,) = call(
        pack_ff,
        [((routes[1][1][0].shape[0], BLK), BF)],
        [((2, 2816, 128), F32), ((24, 128, 128), F32)],
        operands=2,
        flops=2 * routes[1][1][0].size * BLK,
        nbytes=4 << 20,
    )(routes[1][1][0], back)
    (down_rows,) = call(
        pack_down,
        [((routes[1][1][1].shape[0], BLK), BF)],
        [((8, 384, 128), F32)],
        operands=2,
        flops=2 * routes[1][1][1].size * BLK,
        nbytes=2 << 20,
    )(routes[1][1][1], grad_w_down)
    far = routes[1][2]([rows, down_rows])

    grad_qkv, keep, send, gain_terms, grad_w_out = call(
        mix_back,
        [
            ((seq_len, 256), BF),
            ((2, half, D), BF),
            ((2, half, D), BF),
            ((8, D), F32),
            ((128, D), BF),
        ],
        [
            ((seq_len, 128), BF),
            ((seq_len, 128), F32),
            ((2, seq_len, 16), F32),
            ((2, seq_len, 64), F32),
            ((128, D), F32),
        ],
        scalars=1,
        operands=13,
        flops=2 * seq_len * D * (256 + 256) + 10 * 2 * seq_len * seq_len * 256,
        nbytes=20 << 20,
    )(
        me_tok, m_near, m_far, x_near, x_far, w_qkv, w_out, qkv, mixed, mean, total,
        result_keep, result_send,
    )
    grad_w_qkv = left_product(hidden_one, grad_qkv).astype(BF)
    back = exchange(grad_w_qkv.reshape(8, 128, 256))
    out_sum, grad_hidden_one = scatter_of_eight(keep, send)
    result = (middle + out_sum).astype(BF)
    grad_gains = jnp.concatenate([gain_terms[0], grad_gain_two])
    (rows,) = call(
        pack_mix,
        [((routes[0][1][0].shape[0], BLK), BF)],
        [((4, 128, 128), F32), ((16, 128, 128), F32)],
        operands=4,
        flops=2 * routes[0][1][0].size * BLK,
        nbytes=2 << 20,
    )(routes[0][1][0], jnp.pad(grad_gains[None], ((0, 7), (0, 0))), back, grad_w_out)
    near = routes[0][2]([rows])

    normed_one, scale_one = normalize(input_rows)
    grad_input = grad_middle + norm_back(
        grad_hidden_one * gains[0, :D], normed_one, scale_one
    )
    return result, grad_input.astype(BF), (near, far)


def solution(mesh):
    in_specs = (
        P("seq", "tok", None),
        P("seq", "tok", None),
        P(),
        P(("seq", "tok"), None),
        P(("seq", "tok"), None),
        P(("seq", "tok"), None),
    )
    out_specs = (
        P("seq", "tok", None),
        P("seq", "tok", None),
        P(("seq", "tok"), None),
        P(("seq", "tok"), None),
        P(("seq", "tok"), None),
        P(("seq", "tok"), None),
    )
    return jax.shard_map(step, mesh=mesh, in_specs=in_specs, out_specs=out_specs, check_vma=False)
```

```python
import math

import jax
import jax.numpy as jnp
from jax import lax
from jax.experimental import pallas as pl
from jax.experimental.pallas import tpu as pltpu
from jax.sharding import PartitionSpec as P


D = 1024
HEADS = 16
FD = 16
DV = 64
FF = 2752
STEP = 10
BLK = 2048

NORM_EPSILON = 1e-05
ADAM_EPSILON = 1e-08
BETA_ONE = 0.9
BETA_TWO = 0.95
DECAY_RATE = 0.1
BF = jnp.bfloat16
F32 = jnp.float32


MATRIX_BLOCKS = [
    D * HEADS * FD // BLK,
    D * HEADS * FD // BLK,
    D * HEADS * DV // BLK,
    HEADS * DV * D // BLK,
    D * FF // BLK,
    D * FF // BLK,
    FF * D // BLK,
]
MATRIX_STARTS = [1 + sum(MATRIX_BLOCKS[:k]) for k in range(len(MATRIX_BLOCKS))]
LIMITS = [1] + [MATRIX_STARTS[k] + MATRIX_BLOCKS[k] for k in range(len(MATRIX_BLOCKS))]
GROUPS = [(0, 1, 2, 3), (4, 5, 6)]


def product(left, right):
    return jnp.dot(left, right, preferred_element_type=F32)


def left_product(left, right):
    return lax.dot_general(left, right, (((0,), (0,)), ((), ())), preferred_element_type=F32)


def right_product(left, right):
    return lax.dot_general(left, right, (((1,), (1,)), ((), ())), preferred_element_type=F32)


def normalize(values):
    scale = lax.rsqrt(jnp.mean(values * values, axis=-1, keepdims=True) + NORM_EPSILON)
    return (values * scale, scale)


def norm_back(grad_hat, normed_rows, scale):
    return scale * (
        grad_hat - normed_rows * jnp.mean(grad_hat * normed_rows, axis=-1, keepdims=True)
    )


def swap(values, mask):
    return lax.ppermute(values, "tok", [(i, i ^ mask) for i in range(8)])


def exchange(values):
    return lax.all_to_all(values, "tok", 0, 0, tiled=True)


def gather_rows(rows):
    return lax.all_gather(rows, "tok", axis=0, tiled=True)


def scatter_sum(parts, tok):
    sent = parts.astype(BF).reshape(tok, -1, parts.shape[1])
    return jnp.sum(exchange(sent).astype(F32), axis=0)


def gather_of_eight(rows):
    count, height, width = rows.shape
    half = width // 2
    a, b = rows[:, :, :half], rows[:, :, half:]
    ax, by = swap(a, 2), swap(b, 4)
    a2, b2 = jnp.stack([a, ax], 1), jnp.stack([b, by], 1)
    ay, bx = swap(a2, 4), swap(b2, 2)
    first = jnp.concatenate([a2, ay], 1)
    second = jnp.stack([b, bx[:, 0], by, bx[:, 1]], 1)
    near = jnp.concatenate([first, second], -1).reshape(count, 4 * height, width)
    return near, swap(near, 1)


def scatter_of_eight(keep, send):
    many, height, width = keep.shape
    half = width // 2
    mine = keep.astype(F32) + swap(send, 1).astype(F32)
    mine = mine.reshape(many, 4, height // 4, width)
    a, b = mine[..., :half], mine[..., half:]
    got_a = swap(a[:, 2:].astype(BF), 4)
    got_b = swap(jnp.stack([b[:, 1], b[:, 3]], 1).astype(BF), 2)
    a = a[:, :2] + got_a.astype(F32)
    b = jnp.stack([b[:, 0], b[:, 2]], 1) + got_b.astype(F32)
    got_a = swap(a[:, 1].astype(BF), 2)
    got_b = swap(b[:, 1].astype(BF), 4)
    return jnp.concatenate([a[:, 0] + got_a.astype(F32), b[:, 0] + got_b.astype(F32)], -1)


def ff_share(tok):
    return round_up(FF / tok, 128)


def sharded(per_block, tok, group, fill):
    pieces = []
    if group == 0:
        first = jnp.broadcast_to(per_block[:1][None], (tok, 1))
        pieces.append(jnp.pad(first, ((0, 0), (0, 7)), constant_values=fill))
    for k in GROUPS[group]:
        piece = lax.slice_in_dim(per_block, MATRIX_STARTS[k], MATRIX_STARTS[k] + MATRIX_BLOCKS[k])
        if k == 6:
            missing = tok * ff_share(tok) * D // BLK - MATRIX_BLOCKS[k]
            piece = jnp.pad(piece, (0, missing), constant_values=fill)
        piece = piece.reshape(tok, -1)
        missing = -piece.shape[1] % 8
        pieces.append(jnp.pad(piece, ((0, 0), (0, missing)), constant_values=fill))
    return jnp.concatenate(pieces, axis=1)


def piece_of(shard, tok, group, k):
    offset = 0
    for other in (-1,) * (group == 0) + GROUPS[group]:
        if other == -1:
            count = 1
        elif other == 6:
            count = ff_share(tok) * D // BLK
        else:
            count = MATRIX_BLOCKS[other] // tok
        if other == k:
            return shard[offset : offset + count]
        offset += round_up(count, 8)


def joined(pieces):
    return jnp.concatenate([jnp.pad(p, ((0, -p.shape[0] % 8), (0, 0))) for p in pieces], axis=0)


def selected(places, blocks):
    found, at = [], 0
    for place in places:
        found.append(product(place, blocks[at : at + place.shape[1]]).astype(BF))
        at += place.shape[1]
    return found


def rotate(values, count):
    return lax.ppermute(values, "seq", [(i, (i + 1) % count) for i in range(count)])


def onehot(index, size):
    return (index[:, None] == jnp.arange(size, dtype=jnp.int32)[None, :]).astype(BF)


def before(size):
    rows = jnp.arange(size, dtype=jnp.int32)
    return (rows[:, None] < rows[None, :]).astype(BF)


def slot_ranks(owners, devices):
    count = owners.shape[0]
    chunks = -(-count // 128)
    padded = jnp.pad(owners, (0, chunks * 128 - count), constant_values=-1).reshape(chunks, 128)
    match = (
        padded[None] == jnp.arange(devices, dtype=jnp.int32)[:, None, None]
    ).astype(BF)
    within = jnp.einsum("ocl,lm->ocm", match, before(128), preferred_element_type=F32)
    totals = jnp.sum(match.astype(F32), axis=2)
    base = product(totals.astype(BF), before(chunks))
    ranks = jnp.sum(match.astype(F32) * (within + base[:, :, None]), axis=0)
    return ranks.reshape(-1)[:count].astype(jnp.int32)


def round_up(value, unit):
    return int(-(-value // unit) * unit)


class Route:
    def __init__(self, owners, slots, group, seq, tok, capacity):
        devices = seq * tok
        count = owners.shape[0]
        self.seq, self.tok, self.capacity, self.group = seq, tok, capacity, group
        owner = sharded(owners, tok, group, -1)
        slot = sharded(slots, tok, group, 0)
        size = owner.shape[1]
        self.size = size
        mean = capacity * size / count
        self.pair_cap = round_up(mean + 4.2 * math.sqrt(mean) + 1, 8)
        light = (count - capacity) / (devices - 1)
        share = min(1.0, ((tok - 1) * light + capacity) / count)
        cuts = [0, size] if group == 0 else [0, size - ff_share(tok) * D // BLK, size]
        self.cuts = list(zip(cuts[:-1], cuts[1:], strict=True))
        self.row_caps = []
        for start, end in self.cuts:
            used = end - start - (7 if group == 0 else 8 * (start == 0))
            mean = used * share
            cap = round_up(mean + 3.5 * math.sqrt(mean * (1 - share)), 8)
            self.row_caps.append(min(cap, end - start))
        match = (owner[None] == jnp.arange(devices, dtype=jnp.int32)[:, None, None]).astype(BF)
        earlier = jnp.einsum("otl,lm->otm", match, before(size), preferred_element_type=F32)
        pair_rank = jnp.sum(match.astype(F32) * earlier, axis=0).astype(jnp.int32)
        owner_seq = jnp.where(owner >= 0, owner // tok, -1)
        earlier_seq = jnp.sum(earlier.reshape(seq, tok, tok, size), axis=1)
        match_seq = owner_seq[None] == jnp.arange(seq, dtype=jnp.int32)[:, None, None]
        self.fits = jnp.max(pair_rank) < self.pair_cap
        row_ranks = []
        for (start, end), cap in zip(self.cuts, self.row_caps, strict=True):
            part = earlier_seq[:, :, start:end] - earlier_seq[:, :, start : start + 1]
            rank = jnp.sum(jnp.where(match_seq[:, :, start:end], part, 0.0), axis=0)
            rank = rank.astype(jnp.int32)
            self.fits = self.fits & (jnp.max(rank) < cap)
            row_ranks.append(jnp.where(rank < cap, rank, -1))
        row_rank = jnp.concatenate(row_ranks, axis=1)
        me_seq, me_tok = lax.axis_index("seq"), lax.axis_index("tok")
        me = me_seq * tok + me_tok
        shard = jnp.arange(tok, dtype=jnp.int32)[:, None]
        place = jnp.where(pair_rank < self.pair_cap, shard * self.pair_cap + pair_rank, -1)
        self.own_slot = jnp.where(owner == me, slot, -1)
        self.has_gains = (owners[0] == me) & (jnp.arange(capacity, dtype=jnp.int32) == 0)
        once = 1 if group == 0 else 0
        own_slot = self.own_slot[:, once:].reshape(-1)
        hit = own_slot[None, :] == jnp.arange(capacity, dtype=jnp.int32)[:, None]
        target = (
            jnp.sum(jnp.where(hit, place[:, once:].reshape(-1)[None, :] + 1, 0), axis=1) - 1
        )
        columns = jnp.arange(tok * self.pair_cap, dtype=jnp.int32)[None, :]
        send = target[:, None] == columns
        if once:
            send = send | (self.has_gains[:, None] & (columns % self.pair_cap == 0))
        self.send = send.astype(BF)
        my_owner = lax.dynamic_index_in_dim(owner, me_tok, 0, keepdims=False)
        my_seq = lax.dynamic_index_in_dim(owner_seq, me_tok, 0, keepdims=False)
        my_pair = lax.dynamic_index_in_dim(pair_rank, me_tok, 0, keepdims=False)
        my_row = lax.dynamic_index_in_dim(row_rank, me_tok, 0, keepdims=False)
        arrive = jnp.where(
            (my_pair < self.pair_cap) & (my_owner >= 0),
            (my_owner % tok) * self.pair_cap + my_pair,
            -1,
        )
        from_pairs = onehot(arrive, tok * self.pair_cap)
        offset = [sum(self.row_caps[:k]) for k in range(len(self.row_caps))]
        shift = jnp.concatenate(
            [
                jnp.full((end - start,), at, jnp.int32)
                for (start, end), at in zip(self.cuts, offset, strict=True)
            ]
        )
        to_rows = onehot(
            jnp.where((my_seq == me_seq) & (my_row >= 0), my_row + shift, -1), sum(self.row_caps)
        )
        self.compact = left_product(to_rows, from_pairs).astype(BF)
        self.places, self.places_back = [], []
        for (start, end), cap in zip(self.cuts, self.row_caps, strict=True):
            row, owner_of = my_row[start:end], my_owner[start:end]
            at = jnp.where((row >= 0) & (owner_of >= 0), my_seq[start:end] * cap + row, -1)
            self.places.append(onehot(at, seq * cap))
            every = jnp.arange(seq * cap, dtype=jnp.int32)[:, None]
            self.places_back.append((every == at[None, :]).astype(BF))

    def fetch(self, rounded):
        packed = left_product(self.send, rounded).astype(BF)
        packed = exchange(packed)
        rows = product(self.compact, packed).astype(BF)
        fetched, at = [], 0
        for place, cap in zip(self.places, self.row_caps, strict=True):
            part = lax.all_gather(rows[at : at + cap], "seq", axis=0, tiled=True)
            fetched.append((place, part))
            at += cap
        return fetched

    def fetch_any(self, rounded):
        width = rounded.shape[1]
        own = self.own_slot.reshape(-1)
        mine = jnp.where(
            (own >= 0)[:, None], jnp.take(rounded, jnp.maximum(own, 0), axis=0), 0
        ).astype(BF)
        mine = lax.all_to_all(mine.reshape(self.tok, self.size, width), "tok", 0, 0, tiled=True)
        mine = jnp.sum(mine, axis=0)
        total = mine
        for _ in range(self.seq - 1):
            mine = rotate(mine, self.seq)
            total = total + mine
        return [(jnp.eye(end - start, dtype=BF), total[start:end]) for start, end in self.cuts]

    def plain(self):
        eyes = [jnp.eye(end - start, dtype=BF) for start, end in self.cuts]
        return (self.fetch_any, eyes, self.give_any)

    def give(self, rows):
        rows = jnp.concatenate(
            [lax.psum_scatter(part, "seq", scatter_dimension=0, tiled=True) for part in rows]
        )
        packed = left_product(self.compact, rows).astype(BF)
        return exchange(packed)

    def give_any(self, rows):
        rows = jnp.concatenate(rows)
        width = rows.shape[1]
        total = rows.astype(F32)
        passing = rows
        for _ in range(self.seq - 1):
            passing = rotate(passing, self.seq)
            total = total + passing.astype(F32)
        every = jnp.broadcast_to(total.astype(BF)[None], (self.tok, self.size, width))
        every = lax.all_to_all(every, "tok", 0, 0, tiled=True)
        once = 1 if self.group == 0 else 0
        own = self.own_slot[:, once:].reshape(-1)
        hit = own[None, :] == jnp.arange(self.capacity, dtype=jnp.int32)[:, None]
        index = jnp.sum(
            jnp.where(hit, jnp.arange(1, own.shape[0] + 1, dtype=jnp.int32)[None, :], 0), axis=1
        )
        taken = jnp.take(
            every[:, once:].reshape(-1, width), jnp.maximum(index - 1, 0), axis=0
        ).astype(F32)
        taken = jnp.where((index > 0)[:, None], taken, 0.0)
        if once:
            gains = jnp.sum(every[:, 0].astype(F32), axis=0)
            taken = jnp.where(self.has_gains[:, None], gains[None, :], taken)
        return taken


def rates_for(kinds, seq_len):
    out_std = 1.0 / math.sqrt(max(1, D * 16 // seq_len))
    matrix_rate = 3.0 / math.sqrt(D)
    rate_list = [
        1.0,
        matrix_rate,
        matrix_rate,
        matrix_rate,
        3.0 * out_std,
        matrix_rate,
        matrix_rate,
        3.0 / math.sqrt(FF),
        0.0,
    ]
    decay_list = [0.0] + [DECAY_RATE] * 7 + [0.0]
    chosen = (kinds[:, None] == jnp.arange(9, dtype=jnp.int32)[None, :]).astype(F32)
    rate_values = jnp.sum(chosen * jnp.array(rate_list, F32)[None, :], axis=1)
    decay_values = jnp.sum(chosen * jnp.array(decay_list, F32)[None, :], axis=1)
    return (rate_values, decay_values)


def adam_update(grads, moment_one, moment_two, weights, rate_values, decay_values):
    first = BETA_ONE * moment_one + (1.0 - BETA_ONE) * grads
    second = BETA_TWO * moment_two + (1.0 - BETA_TWO) * grads * grads
    first_hat = first / (1.0 - BETA_ONE**STEP)
    second_hat = second / (1.0 - BETA_TWO**STEP)
    updated = weights - rate_values[:, None] * (
        first_hat / (jnp.sqrt(second_hat) + ADAM_EPSILON) + decay_values[:, None] * weights
    )
    return (first, second, updated)


def columns_out(rows, split):
    return rows.reshape(rows.shape[0], split, -1).transpose(1, 0, 2)


def step(tokens, cotangent, owners, master, first_moment, second_moment):
    seq = lax.axis_size("seq")
    tok = lax.axis_size("tok")
    capacity = master.shape[0]
    me = lax.axis_index("seq") * tok + lax.axis_index("tok")
    slots = slot_ranks(owners, seq * tok)
    routes = [Route(owners, slots, group, seq, tok, capacity) for group in range(2)]
    rounded = master.astype(BF)
    layer = layer_of_eight if tok == 8 else layer_of_any
    result, grad_input, packed = layer(
        tokens, cotangent, rounded, [(r.fetch, r.places_back, r.give) for r in routes]
    )
    mine = (owners == me)[None, :]
    numbers = jnp.arange(owners.shape[0], dtype=jnp.int32)[None, :]
    counts = jnp.sum(
        (mine & (numbers < jnp.array(LIMITS, jnp.int32)[:, None])).astype(jnp.int32), axis=1
    )
    kinds = jnp.sum(
        (jnp.arange(capacity, dtype=jnp.int32)[:, None] >= counts[None, :]).astype(jnp.int32),
        axis=1,
    )
    rates = rates_for(kinds, tokens.shape[1] * tok)
    held = (first_moment, second_moment, master)
    found = (result, grad_input) + owned_update(routes, packed, held, rates)

    def any_owners(carried):
        result, grad_input, parts = layer(
            tokens, cotangent, rounded, [route.plain() for route in routes]
        )
        reduced = parts[0] + parts[1]
        updated = adam_update(reduced, *held, *rates)
        return (jnp.int32(1), result, grad_input, reduced) + updated

    missing = jnp.where(routes[0].fits & routes[1].fits, 1, 0).astype(jnp.int32)
    found = lax.while_loop(lambda carried: carried[0] == 0, any_owners, (missing,) + found)
    _, result, grad_input, reduced, first, second, updated = found
    return (result[None], grad_input[None], reduced, first, second, updated)


def call(kernel, outs, scratch=(), scalars=0, operands=0, flops=0, nbytes=0):
    return pl.pallas_call(
        kernel,
        out_shape=[jax.ShapeDtypeStruct(shape, kind) for shape, kind in outs],
        in_specs=[pl.BlockSpec(memory_space=pltpu.SMEM)] * scalars
        + [pl.BlockSpec(memory_space=pltpu.VMEM)] * (operands - scalars),
        scratch_shapes=[pltpu.VMEM(shape, kind) for shape, kind in scratch],
        compiler_params=pltpu.CompilerParams(vmem_limit_bytes=60 * 1024 * 1024),
        cost_estimate=pl.CostEstimate(flops=flops, bytes_accessed=nbytes, transcendentals=0),
    )


def dot(left, right):
    return jnp.dot(left, right, preferred_element_type=F32)


def low_lanes(shape):
    return lax.broadcasted_iota(jnp.int32, shape, 1) < 64


def unpack_ff(place_ref, rows_ref, sent_ref, flat, wide):
    for c in range(0, 16, 2):
        found = dot(place_ref[...], rows_ref[:, pl.ds(128 * c, 256)])
        for m in range(2):
            half = found[176 * m : 176 * m + 176]
            flat[m, pl.ds(c, 176, stride=16), :] = half[:, :128]
            flat[m, pl.ds(c + 1, 176, stride=16), :] = half[:, 128:]
    low = low_lanes((64, 128))
    zero = jnp.zeros((64, 128), F32)
    for m in range(2):
        for k in range(24):
            if k > 21:
                wide[k] = jnp.zeros((128, 128), F32)
                continue
            even = flat[m, pl.ds(k, 64, stride=43), :]
            first = flat[m, pl.ds(21 + k, 64, stride=43), :]
            second = flat[m, pl.ds(22 + k, 64, stride=43), :] if k < 21 else zero
            if k == 21:
                even = jnp.where(low, even, 0.0)
            odd = pltpu.roll(jnp.where(low, second, first), 64, 1)
            wide[k, pl.ds(0, 64, stride=2), :] = even
            wide[k, pl.ds(1, 64, stride=2), :] = odd
        for k in range(24):
            sent_ref[k // 3, :, pl.ds(384 * m + 128 * (k % 3), 128)] = wide[k].astype(BF)


def unpack_down(place_ref, rows_ref, down_ref, tall):
    for c in range(0, 16, 2):
        found = dot(place_ref[...], rows_ref[:, pl.ds(128 * c, 256)])
        tall[c % 8, pl.ds(c // 8, 192, stride=2), :] = found[:, :128]
        tall[c % 8 + 1, pl.ds(c // 8, 192, stride=2), :] = found[:, 128:]
    for k in range(8):
        down_ref[:, pl.ds(128 * k, 128)] = tall[k].astype(BF)


def pack_ff(place_ref, back_ref, rows_ref, flat, wide):
    low = low_lanes((64, 128))
    for m in range(2):
        flat[m, pl.ds(2752, 64), :] = jnp.zeros((64, 128), F32)
        for k in range(22):
            wide[k] = back_ref[k // 3, :, pl.ds(384 * m + 128 * (k % 3), 128)].astype(F32)

        def turned(k):
            return pltpu.roll(wide[k, pl.ds(1, 64, stride=2), :], 64, 1)

        for k in range(21):
            flat[m, pl.ds(k, 64, stride=43), :] = wide[k, pl.ds(0, 64, stride=2), :]
        after = turned(0)
        flat[m, pl.ds(21, 64, stride=43), :] = jnp.where(
            low, wide[21, pl.ds(0, 64, stride=2), :], after
        )
        for k in range(21):
            current, after = after, turned(k + 1)
            flat[m, pl.ds(22 + k, 64, stride=43), :] = jnp.where(low, current, after)
    for c in range(0, 16, 2):
        grads = jnp.concatenate(
            [
                jnp.concatenate([flat[m, pl.ds(c + h, 176, stride=16), :] for m in range(2)], axis=0)
                for h in range(2)
            ],
            axis=1,
        ).astype(BF)
        rows_ref[:, pl.ds(128 * c, 256)] = dot(place_ref[...], grads).astype(BF)


def pack_down(place_ref, down_ref, rows_ref, tall):
    for k in range(8):
        tall[k] = down_ref[:, pl.ds(128 * k, 128)].astype(F32)
    for c in range(0, 16, 2):
        grads = jnp.concatenate(
            [tall[c % 8 + h, pl.ds(c // 8, 192, stride=2), :] for h in range(2)], axis=1
        ).astype(BF)
        rows_ref[:, pl.ds(128 * c, 256)] = dot(place_ref[...], grads).astype(BF)


def unpack_mix(place_ref, rows_ref, gains_ref, sent_ref, out_ref, thin, tall):
    for c in range(16):
        lanes = pl.ds(128 * c, 128)
        found = dot(place_ref[...], rows_ref[:, lanes])
        gains_ref[:, lanes] = found[:8]
        thin[c % 2, pl.ds(c // 2, 16, stride=8), :] = found[8:24]
        thin[2 + c % 2, pl.ds(c // 2, 16, stride=8), :] = found[24:40]
        tall[c % 8, pl.ds(c // 8, 64, stride=2), :] = found[40:104]
        tall[8 + c % 8, pl.ds(c // 8, 64, stride=2), :] = found[104:]
    lane = lax.broadcasted_iota(jnp.int32, (128, 128), 1)
    for t in range(8):
        sent_ref[t, :, pl.ds(0, 128)] = tall[t].astype(BF)
        query, keys = thin[t // 4], thin[2 + t // 4]
        if t % 4 != 0:
            query = pltpu.roll(query, 128 - 32 * (t % 4), 1)
        if t % 4 != 1:
            keys = pltpu.roll(keys, (160 - 32 * (t % 4)) % 128, 1)
        both = jnp.where(lane < 32, query, jnp.where(lane < 64, keys, 0.0))
        sent_ref[t, :, pl.ds(128, 128)] = both.astype(BF)
        out_ref[:, pl.ds(128 * t, 128)] = tall[8 + t].astype(BF)


def pack_mix(place_ref, gains_ref, back_ref, out_ref, rows_ref, thin, tall):
    lane = lax.broadcasted_iota(jnp.int32, (128, 128), 1)
    for j in range(2):
        query = jnp.zeros((128, 128), F32)
        keys = jnp.zeros((128, 128), F32)
        for u in range(4):
            both = back_ref[4 * j + u, :, pl.ds(128, 128)].astype(F32)
            here = (lane >= 32 * u) & (lane < 32 * u + 32)
            moved = pltpu.roll(both, 32 * u, 1) if u else both
            query = jnp.where(here, moved, query)
            moved = pltpu.roll(both, (96 + 32 * u) % 128, 1) if u != 1 else both
            keys = jnp.where(here, moved, keys)
        thin[j] = query
        thin[2 + j] = keys
    for t in range(8):
        tall[t] = back_ref[t, :, pl.ds(0, 128)].astype(F32)
        tall[8 + t] = out_ref[:, pl.ds(128 * t, 128)].astype(F32)
    for c in range(16):
        lanes = pl.ds(128 * c, 128)
        grads = jnp.concatenate(
            [
                gains_ref[:, lanes],
                thin[c % 2, pl.ds(c // 2, 16, stride=8), :],
                thin[2 + c % 2, pl.ds(c // 2, 16, stride=8), :],
                tall[c % 8, pl.ds(c // 8, 64, stride=2), :],
                tall[8 + c % 8, pl.ds(c // 8, 64, stride=2), :],
            ],
            axis=0,
        ).astype(BF)
        rows_ref[:, lanes] = dot(place_ref[...], grads).astype(BF)


def select_update(
    send0, send1, near, far, first, second, weights, rates, decays, out0, out1, out2, out3
):
    grads = dot(send0[...], near[...]) + dot(send1[...], far[...])
    out0[...] = grads
    updated = adam_update(
        grads, first[...], second[...], weights[...], rates[...][:, 0], decays[...][:, 0]
    )
    out1[...], out2[...], out3[...] = updated


def owned_update(routes, packed, held, rates):
    capacity, width = held[0].shape
    columns = 256

    def whole(array):
        return pl.BlockSpec(array.shape, lambda i: (0, 0))

    def part(array):
        return pl.BlockSpec((array.shape[0], columns), lambda i: (0, i))

    rates = [values[:, None] for values in rates]
    return tuple(
        pl.pallas_call(
            select_update,
            out_shape=[jax.ShapeDtypeStruct((capacity, width), F32)] * 4,
            grid=(width // columns,),
            in_specs=[whole(routes[0].send), whole(routes[1].send)]
            + [part(array) for array in (*packed, *held)]
            + [whole(rates[0]), whole(rates[1])],
            out_specs=[part(held[0])] * 4,
            cost_estimate=pl.CostEstimate(
                flops=2 * capacity * width * 576, bytes_accessed=16 << 20, transcendentals=0
            ),
        )(routes[0].send, routes[1].send, *packed, *held, *rates)
    )


ROWS = 256


def feed_forward(h0, h1, c0, c1, w_in, w_down, hidden_ref, grad_ref, keep, send, result_keep, result_send):
    for half, (h_ref, c_ref, out, result) in enumerate(
        ((h0, c0, keep, result_keep), (h1, c1, send, result_send))
    ):

        def block(i, carry, half=half, h_ref=h_ref, c_ref=c_ref, out=out, result=result):
            here = pl.ds(pl.multiple_of(i * ROWS, ROWS), ROWS)
            there = pl.ds(pl.multiple_of(i * ROWS + 512 * half, ROWS), ROWS)
            gate_up = dot(h_ref[0, here, :], w_in[...])
            gate, up = gate_up[:, :384], gate_up[:, 384:]
            sigmoid = jax.nn.sigmoid(gate)
            active = gate * sigmoid
            hidden = (active * up).astype(BF)
            hidden_ref[there, :] = hidden
            grad_hidden = right_product(c_ref[1, here, :], w_down[...])
            grad_gate = grad_hidden * up * sigmoid * (1.0 + gate * (1.0 - sigmoid))
            grads = jnp.concatenate([grad_gate, grad_hidden * active], axis=1).astype(BF)
            grad_ref[there, :] = grads
            out[0, here, :] = right_product(grads, w_in[...]).astype(BF)
            result[here, :] = dot(hidden, w_down[...]).astype(BF)
            return carry

        lax.fori_loop(0, 512 // ROWS, block, 0)


def token_at(index, me):
    group = index >> 7
    far = ((group & 3) << 1) | (group >> 2)
    return ((far ^ me) << 7) | (index & 127)


def pair_weights(query, keys, first, me):
    inner = right_product(query, keys) * (1.0 / math.sqrt(FD))
    row = lax.broadcasted_iota(jnp.int32, (inner.shape[0], 1), 0) + first
    column = lax.broadcasted_iota(jnp.int32, (1, inner.shape[1]), 1)
    causal = token_at(row, me) >= token_at(column, me)
    return inner, jnp.where(causal, 1.0 + inner + 0.5 * inner * inner, 0.0), causal


def mix(me_ref, x0, x1, gain, w_in, w_out, hidden_ref, qkv, mixed_ref, mean_ref, total_ref, keep, send):
    me = me_ref[0]
    for half, x_ref in enumerate((x0, x1)):

        def block(i, carry, half=half, x_ref=x_ref):
            here = pl.ds(pl.multiple_of(i * ROWS, ROWS), ROWS)
            there = pl.ds(pl.multiple_of(i * ROWS + 512 * half, ROWS), ROWS)
            x = x_ref[0, here, :].astype(F32)
            scale = lax.rsqrt(jnp.mean(x * x, axis=1, keepdims=True) + NORM_EPSILON)
            hidden = (x * scale * gain[0:1, :]).astype(BF)
            hidden_ref[there, :] = hidden
            qkv[there, :] = dot(hidden, w_in[...]).astype(BF)
            return carry

        lax.fori_loop(0, 512 // ROWS, block, 0)
    for half, out in enumerate((keep, send)):

        def block(i, carry, half=half, out=out):
            first = pl.multiple_of(i * ROWS + 512 * half, ROWS)
            there = pl.ds(first, ROWS)
            means, totals = [], []
            for u in range(2):
                query = qkv[there, pl.ds(128, 128)][:, 16 * u : 16 * u + 16]
                keys = qkv[:, pl.ds(128, 128)][:, 32 + 16 * u : 48 + 16 * u]
                values = qkv[:, pl.ds(0, 128)][:, 64 * u : 64 * u + 64]
                _, weight, _ = pair_weights(query, keys, first, me)
                total = jnp.sum(weight, axis=1, keepdims=True)
                means.append(dot(weight.astype(BF), values) / total)
                totals.append(jnp.broadcast_to(total, (ROWS, 64)))
            mean = jnp.concatenate(means, axis=1)
            mean_ref[there, :] = mean
            total_ref[there, :] = jnp.concatenate(totals, axis=1)
            mixed = mean.astype(BF)
            mixed_ref[there, :] = mixed
            here = pl.ds(pl.multiple_of(i * ROWS, ROWS), ROWS)
            out[0, here, :] = dot(mixed, w_out[...]).astype(BF)
            return carry

        lax.fori_loop(0, 512 // ROWS, block, 0)


def mix_back(
    me_ref, m0, m1, w_out, qkv, mixed_ref, mean_ref, total_ref,
    grad_ref, out_grad, numer, denom, back_keys, back_values, back_out,
):
    me = me_ref[0]
    back_out[...] = jnp.zeros_like(back_out)
    for half, m_ref in enumerate((m0, m1)):

        def block(i, carry, half=half, m_ref=m_ref):
            here = pl.ds(pl.multiple_of(i * ROWS, ROWS), ROWS)
            there = pl.ds(pl.multiple_of(i * ROWS + 512 * half, ROWS), ROWS)
            grad = right_product(m_ref[0, here, :], w_out[...]).astype(BF).astype(F32)
            back_out[...] += left_product(mixed_ref[there, :], m_ref[0, here, :])
            total = total_ref[there, :]
            numer[there, :] = (grad / total).astype(BF)
            lean = grad * mean_ref[there, :]
            sums = [jnp.sum(lean[:, 64 * u : 64 * u + 64], axis=1, keepdims=True) for u in range(2)]
            wide = jnp.concatenate([jnp.broadcast_to(s, (ROWS, 64)) for s in sums], axis=1)
            denom[there, :] = -wide / total
            return carry

        lax.fori_loop(0, 512 // ROWS, block, 0)
    out_grad[...] = back_out[...].astype(BF)
    back_keys[...] = jnp.zeros_like(back_keys)
    back_values[...] = jnp.zeros_like(back_values)

    def pairs(i, carry):
        first = pl.multiple_of(i * ROWS, ROWS)
        there = pl.ds(first, ROWS)
        query_grads = []
        for u in range(2):
            query = qkv[there, pl.ds(128, 128)][:, 16 * u : 16 * u + 16]
            keys = qkv[:, pl.ds(128, 128)][:, 32 + 16 * u : 48 + 16 * u]
            values = qkv[:, pl.ds(0, 128)][:, 64 * u : 64 * u + 64]
            inner, weight, causal = pair_weights(query, keys, first, me)
            down = numer[there, :][:, 64 * u : 64 * u + 64]
            grad_weight = right_product(down, values) + denom[there, :][:, 64 * u : 64 * u + 1]
            grad_inner = (
                jnp.where(causal, grad_weight * (1.0 + inner), 0.0) * (1.0 / math.sqrt(FD))
            ).astype(BF)
            query_grads.append(dot(grad_inner, keys))
            back_keys[u] += left_product(grad_inner, query)
            back_values[u] += left_product(weight.astype(BF), down)
        grad_ref[there, pl.ds(128, 128)] = jnp.concatenate(
            query_grads + [jnp.zeros((ROWS, 96), F32)], axis=1
        ).astype(BF)
        return carry

    lax.fori_loop(0, 1024 // ROWS, pairs, 0)

    def join(i, carry):
        there = pl.ds(pl.multiple_of(i * ROWS, ROWS), ROWS)
        query_grad = grad_ref[there, pl.ds(128, 128)][:, :32]
        keys_grad = [back_keys[u, there, :].astype(BF) for u in range(2)]
        values_grad = [back_values[u, there, :].astype(BF) for u in range(2)]
        grad_ref[there, :] = jnp.concatenate(
            values_grad + [query_grad] + keys_grad + [jnp.zeros((ROWS, 64), BF)], axis=1
        )
        return carry

    lax.fori_loop(0, 1024 // ROWS, join, 0)


def input_back(x0, x1, w_in, grad_ref, result_keep, result_send, keep, send, gain_ref):
    keep[0] = result_keep[...]
    send[0] = result_send[...]
    gain_ref[...] = jnp.zeros_like(gain_ref)
    for half, (x_ref, out) in enumerate(((x0, keep), (x1, send))):

        def block(i, carry, half=half, x_ref=x_ref, out=out):
            here = pl.ds(pl.multiple_of(i * ROWS, ROWS), ROWS)
            there = pl.ds(pl.multiple_of(i * ROWS + 512 * half, ROWS), ROWS)
            terms = right_product(grad_ref[there, :], w_in[...])
            out[1, here, :] = terms.astype(BF)
            x = x_ref[0, here, :].astype(F32)
            scale = lax.rsqrt(jnp.mean(x * x, axis=1, keepdims=True) + NORM_EPSILON)
            gain_ref[0:1, :] += jnp.sum(terms * (x * scale), axis=0, keepdims=True)
            return carry

        lax.fori_loop(0, 512 // ROWS, block, 0)


def layer_of_any(tokens, cotangent, rounded, routes):
    tok = lax.axis_size("tok")
    row_count = tokens.shape[1]
    seq_len = row_count * tok
    value_split = max(1, tok // HEADS)
    units = max(1, HEADS // tok)
    unit_width = DV // value_split
    slice_rows = D // tok
    ff_slice = ff_share(tok)
    qk_width = units * FD
    v_width = units * unit_width

    x_all, c_all = gather_rows(tokens[0]), gather_rows(cotangent[0])

    shard = jnp.concatenate([product(*part).astype(BF) for part in routes[0][0](rounded)])
    gain_one = shard[0, :D].astype(F32)
    gain_two = shard[0, D:].astype(F32)

    def spread(columns):
        wide = columns.reshape(slice_rows, tok // value_split, 1, qk_width)
        return jnp.broadcast_to(
            wide, (slice_rows, tok // value_split, value_split, qk_width)
        ).reshape(slice_rows, tok, qk_width)

    sent = jnp.concatenate(
        [
            spread(piece_of(shard, tok, 0, 0).reshape(slice_rows, HEADS * FD)),
            spread(piece_of(shard, tok, 0, 1).reshape(slice_rows, HEADS * FD)),
            piece_of(shard, tok, 0, 2).reshape(slice_rows, tok, v_width),
        ],
        axis=-1,
    ).transpose(1, 0, 2)
    w_qkv = exchange(sent).reshape(D, -1)
    w_out = piece_of(shard, tok, 0, 3).reshape(v_width, D)

    def padded(blocks):
        return jnp.pad(blocks.reshape(slice_rows, FF), ((0, 0), (0, tok * ff_slice - FF)))

    shard = jnp.concatenate([product(*part).astype(BF) for part in routes[1][0](rounded)])
    sent = jnp.concatenate(
        [
            columns_out(padded(piece_of(shard, tok, 1, 4)), tok),
            columns_out(padded(piece_of(shard, tok, 1, 5)), tok),
        ],
        axis=-1,
    )
    w_gate_up = exchange(sent).reshape(D, -1)
    w_down = piece_of(shard, tok, 1, 6).reshape(ff_slice, D)

    normed_all, _ = normalize(x_all.astype(F32))
    hidden_one = (normed_all * gain_one).astype(BF)
    qkv = product(hidden_one, w_qkv).astype(BF)
    query = qkv[:, :qk_width].reshape(seq_len, units, FD).transpose(1, 0, 2)
    keys = qkv[:, qk_width : 2 * qk_width].reshape(seq_len, units, FD).transpose(1, 0, 2)
    values = qkv[:, 2 * qk_width :].reshape(seq_len, units, unit_width).transpose(1, 0, 2)
    index = jnp.arange(seq_len, dtype=jnp.int32)
    causal = (index[:, None] >= index[None, :])[None]
    inner = jnp.einsum("uif,ujf->uij", query, keys, preferred_element_type=F32) * (
        1.0 / math.sqrt(FD)
    )
    weight = jnp.where(causal, 1.0 + inner + 0.5 * inner * inner, 0.0)
    total = jnp.sum(weight, axis=2, keepdims=True)
    mixed_f = (
        jnp.einsum("uij,ujw->uiw", weight.astype(BF), values, preferred_element_type=F32) / total
    )
    mixed = mixed_f.astype(BF).transpose(1, 0, 2).reshape(seq_len, v_width)
    out = scatter_sum(product(mixed, w_out), tok)

    input_rows = tokens[0].astype(F32)
    middle = input_rows + out
    normed_two, scale_two = normalize(middle)
    hidden_two = gather_rows((normed_two * gain_two).astype(BF))

    gate_up = product(hidden_two, w_gate_up)
    gate, up_proj = gate_up[:, :ff_slice], gate_up[:, ff_slice:]
    sigmoid = jax.nn.sigmoid(gate)
    activated = gate * sigmoid
    hidden = (activated * up_proj).astype(BF)
    grad_hidden = right_product(c_all, w_down)
    grad_gate = (grad_hidden * up_proj * sigmoid * (1.0 + gate * (1.0 - sigmoid))).astype(BF)
    grad_up = (grad_hidden * activated).astype(BF)
    grad_gate_up = jnp.concatenate([grad_gate, grad_up], axis=1)
    grad_two_terms = right_product(grad_gate_up, w_gate_up)
    grad_hidden_two = scatter_sum(grad_two_terms, tok)
    result_terms = product(hidden, w_down)

    grad_gain_two = jnp.sum(grad_hidden_two * normed_two, axis=0)
    grad_middle = cotangent[0].astype(F32) + norm_back(
        grad_hidden_two * gain_two, normed_two, scale_two
    )
    grad_mixer = gather_rows(grad_middle.astype(BF))

    grad_w_down = left_product(hidden, c_all).astype(BF)
    grad_w_gate_up = left_product(hidden_two, grad_gate_up).astype(BF)
    back = exchange(grad_w_gate_up.reshape(tok, slice_rows, 2 * ff_slice))

    def flat(columns):
        rows = columns.transpose(1, 0, 2).reshape(slice_rows, tok * ff_slice)
        return rows[:, :FF].reshape(-1, BLK)

    back_gate, back_up = flat(back[..., :ff_slice]), flat(back[..., ff_slice:])
    blocks = joined([back_gate, back_up, grad_w_down.reshape(-1, BLK)])
    far = routes[1][2](selected(routes[1][1], blocks))

    grad_w_out = left_product(mixed, grad_mixer).astype(BF)
    grad_mixed = right_product(grad_mixer, w_out).astype(BF)
    grad_units = grad_mixed.reshape(seq_len, units, unit_width).transpose(1, 0, 2).astype(F32)
    grad_numer = (grad_units / total).astype(BF)
    grad_denom = -jnp.sum(grad_units * mixed_f, axis=-1, keepdims=True) / total
    grad_weight = (
        jnp.einsum("uiw,ujw->uij", grad_numer, values, preferred_element_type=F32) + grad_denom
    )
    grad_inner = (
        jnp.where(causal, grad_weight * (1.0 + inner), 0.0) * (1.0 / math.sqrt(FD))
    ).astype(BF)
    grad_query = jnp.einsum("uij,ujf->iuf", grad_inner, keys, preferred_element_type=F32)
    grad_keys = jnp.einsum("uij,uif->juf", grad_inner, query, preferred_element_type=F32)
    grad_values = jnp.einsum(
        "uij,uiw->juw", weight.astype(BF), grad_numer, preferred_element_type=F32
    )
    grad_qkv = jnp.concatenate(
        [
            grad_query.reshape(seq_len, -1),
            grad_keys.reshape(seq_len, -1),
            grad_values.reshape(seq_len, -1),
        ],
        axis=1,
    ).astype(BF)
    grad_w_qkv = left_product(hidden_one, grad_qkv).astype(BF)
    grad_one_terms = right_product(grad_qkv, w_qkv)
    grad_hidden_one = scatter_sum(grad_one_terms, tok)
    result = (middle + scatter_sum(result_terms, tok)).astype(BF)
    grad_gains = jnp.concatenate([jnp.sum(grad_one_terms * normed_all, axis=0), grad_gain_two])
    back = exchange(grad_w_qkv.reshape(tok, slice_rows, -1)).transpose(1, 0, 2)

    def gathered(columns):
        if value_split > 1:
            columns = jnp.sum(
                columns.reshape(slice_rows, tok // value_split, value_split, -1).astype(F32), axis=2
            ).astype(BF)
        return columns.reshape(-1, BLK)

    blocks = joined(
        [
            grad_gains.astype(BF).reshape(1, BLK),
            gathered(back[..., :qk_width]),
            gathered(back[..., qk_width : 2 * qk_width]),
            back[..., 2 * qk_width :].reshape(-1, BLK),
            grad_w_out.reshape(-1, BLK),
        ]
    )
    near = routes[0][2](selected(routes[0][1], blocks))

    normed_one, scale_one = normalize(input_rows)
    grad_input = grad_middle + norm_back(grad_hidden_one * gain_one, normed_one, scale_one)
    return result, grad_input.astype(BF), (near, far)


def layer_of_eight(tokens, cotangent, rounded, routes):
    me_tok = lax.axis_index("tok").astype(jnp.int32).reshape(1)
    seq_len = 8 * tokens.shape[1]
    half = seq_len // 2
    x_near, x_far = gather_of_eight(jnp.concatenate([tokens, cotangent]))

    ((place, rows),) = routes[0][0](rounded)
    gains, sent, w_out = call(
        unpack_mix,
        [((8, BLK), F32), ((8, 128, 256), BF), ((128, D), BF)],
        [((4, 128, 128), F32), ((16, 128, 128), F32)],
        operands=2,
        flops=2 * place.shape[0] * place.shape[1] * BLK,
        nbytes=2 << 20,
    )(place, rows)
    w_qkv = exchange(sent).reshape(D, 256)
    (place, rows), (down_place, down_rows) = routes[1][0](rounded)
    (sent,) = call(
        unpack_ff,
        [((8, 128, 768), BF)],
        [((2, 2816, 128), F32), ((24, 128, 128), F32)],
        operands=2,
        flops=2 * place.size * BLK,
        nbytes=4 << 20,
    )(place, rows)
    (w_down,) = call(
        unpack_down,
        [((384, D), BF)],
        [((8, 384, 128), F32)],
        operands=2,
        flops=2 * down_place.size * BLK,
        nbytes=2 << 20,
    )(down_place, down_rows)
    w_in = exchange(sent).reshape(D, 768)

    hidden_one, qkv, mixed, mean, total, keep, send = call(
        mix,
        [
            ((seq_len, D), BF),
            ((seq_len, 256), BF),
            ((seq_len, 128), BF),
            ((seq_len, 128), F32),
            ((seq_len, 128), F32),
            ((1, half, D), BF),
            ((1, half, D), BF),
        ],
        scalars=1,
        operands=6,
        flops=2 * seq_len * D * (256 + 128) + 4 * 2 * seq_len * seq_len * 256,
        nbytes=10 << 20,
    )(me_tok, x_near, x_far, gains[:, :D], w_qkv, w_out)
    out = scatter_of_eight(keep, send)[0]

    input_rows = tokens[0].astype(F32)
    middle = input_rows + out
    normed_two, scale_two = normalize(middle)
    gain_two = gains[0, D:]
    h_near, h_far = gather_of_eight((normed_two * gain_two).astype(BF)[None])

    hidden, grad_gate_up, keep, send, result_keep, result_send = call(
        feed_forward,
        [
            ((seq_len, 384), BF),
            ((seq_len, 768), BF),
            ((1, half, D), BF),
            ((1, half, D), BF),
            ((half, D), BF),
            ((half, D), BF),
        ],
        operands=6,
        flops=2 * seq_len * D * (768 * 2 + 384 * 2),
        nbytes=14 << 20,
    )(h_near, h_far, x_near, x_far, w_in, w_down)
    grad_hidden_two = scatter_of_eight(keep, send)[0]
    grad_gain_two = jnp.sum(grad_hidden_two * normed_two, axis=0)
    grad_middle = cotangent[0].astype(F32) + norm_back(
        grad_hidden_two * gain_two, normed_two, scale_two
    )
    m_near, m_far = gather_of_eight(grad_middle.astype(BF)[None])

    all_rows = jnp.concatenate([h_near[0], h_far[0]])
    grad_w_in = left_product(all_rows, grad_gate_up).astype(BF)
    all_rows = jnp.concatenate([x_near[1], x_far[1]])
    grad_w_down = left_product(hidden, all_rows).astype(BF)
    back = exchange(grad_w_in.reshape(8, 128, 768))
    (rows,) = call(
        pack_ff,
        [((routes[1][1][0].shape[0], BLK), BF)],
        [((2, 2816, 128), F32), ((24, 128, 128), F32)],
        operands=2,
        flops=2 * routes[1][1][0].size * BLK,
        nbytes=4 << 20,
    )(routes[1][1][0], back)
    (down_rows,) = call(
        pack_down,
        [((routes[1][1][1].shape[0], BLK), BF)],
        [((8, 384, 128), F32)],
        operands=2,
        flops=2 * routes[1][1][1].size * BLK,
        nbytes=2 << 20,
    )(routes[1][1][1], grad_w_down)
    far = routes[1][2]([rows, down_rows])

    grad_qkv, grad_w_out = call(
        mix_back,
        [((seq_len, 256), BF), ((128, D), BF)],
        [
            ((seq_len, 128), BF),
            ((seq_len, 128), F32),
            ((2, seq_len, 16), F32),
            ((2, seq_len, 64), F32),
            ((128, D), F32),
        ],
        scalars=1,
        operands=8,
        flops=2 * seq_len * D * 256 + 10 * 2 * seq_len * seq_len * 256,
        nbytes=8 << 20,
    )(me_tok, m_near, m_far, w_out, qkv, mixed, mean, total)
    grad_w_qkv = left_product(hidden_one, grad_qkv).astype(BF)
    keep, send, gain_terms = call(
        input_back,
        [((2, half, D), BF), ((2, half, D), BF), ((8, D), F32)],
        operands=6,
        flops=2 * seq_len * D * 256,
        nbytes=14 << 20,
    )(x_near, x_far, w_qkv, grad_qkv, result_keep, result_send)
    back = exchange(grad_w_qkv.reshape(8, 128, 256))
    out_sum, grad_hidden_one = scatter_of_eight(keep, send)
    result = (middle + out_sum).astype(BF)
    grad_gains = jnp.concatenate([gain_terms[0], grad_gain_two])
    (rows,) = call(
        pack_mix,
        [((routes[0][1][0].shape[0], BLK), BF)],
        [((4, 128, 128), F32), ((16, 128, 128), F32)],
        operands=4,
        flops=2 * routes[0][1][0].size * BLK,
        nbytes=2 << 20,
    )(routes[0][1][0], jnp.pad(grad_gains[None], ((0, 7), (0, 0))), back, grad_w_out)
    near = routes[0][2]([rows])

    normed_one, scale_one = normalize(input_rows)
    grad_input = grad_middle + norm_back(
        grad_hidden_one * gains[0, :D], normed_one, scale_one
    )
    return result, grad_input.astype(BF), (near, far)


def solution(mesh):
    in_specs = (
        P("seq", "tok", None),
        P("seq", "tok", None),
        P(),
        P(("seq", "tok"), None),
        P(("seq", "tok"), None),
        P(("seq", "tok"), None),
    )
    out_specs = (
        P("seq", "tok", None),
        P("seq", "tok", None),
        P(("seq", "tok"), None),
        P(("seq", "tok"), None),
        P(("seq", "tok"), None),
        P(("seq", "tok"), None),
    )
    return jax.shard_map(step, mesh=mesh, in_specs=in_specs, out_specs=out_specs, check_vma=False)
```
